256 devices in a mesh: row: 32 (over y_hi, z, core), col: 8 (over y_lo, x).
Axes of the slice: x: 4, y: 4 (y_hi: 2, y_lo: 2; y = y_hi * 2 + y_lo), z: 8, core: 2. Of those that a mesh axis runs over, the one named last changes fastest.
Arguments:
- history: bfloat16 [2111, 131072], P(None, ('row', 'col')), may hold values from -6 to 6
- lag_class: int32 [131072], P(('row', 'col')), may hold values from 0 to 3
- lag_table: float32 [4, 64], replicated, may hold values from -0.9 to 0.9
- row_bases: bfloat16 [131072, 64], P(('row', 'col')), may hold values from -0.25 to 0.25
- coupling: bfloat16 [256, 32, 8, 64, 64], P('row', None, 'col'), may hold values from -0.09375 to 0.09375
- block_ranks: int32 [256, 32, 8], P('row', None, 'col'), may hold values from 16 to 64
- col_bases: bfloat16 [131072, 64], P(('row', 'col')), may hold values from -0.75 to 0.75
- near_blocks: bfloat16 [256, 3, 512, 512], P(('row', 'col')), may hold values from -0.25 to 0.25
- near_flags: int32 [256, 2], P(('row', 'col')), may hold values 0 or 1
Outputs:
- adjoint: float32 [2048, 131072], P(None, ('row', 'col'))
The draws below stay inside these ranges and needn't reach their ends.
All inputs are finite; a program needn't handle non-finite values. No bound on the sum of `near_flags` on one device may be relied on, other than what follows from the above.
Results may differ from the reference program's by a relative error of at most 0.015.
Values may be sent and summed in bfloat16 or wider, within the bound.
A program may use at most 128 MiB of HBM per device.

```python
import jax
import jax.numpy as jnp
from jax import lax

STEPS = 2048
CLUSTER = 512
RANK = 64
LAGS = 64
CLASSES = 4
CLUSTERS = 256
ELEMENTS = 131072
HIST = 2111
N_ROW = 32
N_COL = 8


def touch_ends(array, rng, smallest, largest):
    extent = array.shape
    place = [jax.random.randint(jax.random.fold_in(rng, axis), (), 0, extent[axis]) for axis in range(len(extent))]
    array = array.at[tuple(place)].set(smallest)
    longest = extent.index(max(extent))
    place[longest] = (place[longest] + 1) % extent[longest]
    return array.at[tuple(place)].set(largest)


def with_spikes(array, own_key, source, target, blocks, factor):
    def block_of(position):
        return (jnp.arange(array.shape[position]) // (array.shape[position] // blocks)).reshape((-1,) + (1,) * (array.ndim - 1 - position))

    near = jax.random.permutation(own_key, blocks)[block_of(target)]
    other_side = (block_of(target) + blocks // 2) % blocks
    return jnp.where((block_of(source) == near) | (block_of(source) == other_side), factor * array, array)


def block_levels(stream_key, shape, shards, low, top_value):
    def one(axis_at, shards_of):
        steps = jax.random.uniform(jax.random.fold_in(jax.random.fold_in(stream_key, 6), axis_at), (shards_of,), jnp.float32, low / len(shards), top_value / len(shards))
        return jnp.repeat(jnp.exp(steps), shape[axis_at] // shards_of).reshape((-1,) + (1,) * (len(shape) - axis_at - 1))

    factor_of = one(*shards[0])
    for cut in shards[1:]:
        factor_of = factor_of * one(*cut)
    return factor_of


def gaussian(rng, shape, deviation, most, cuts=(), kind=jnp.bfloat16):
    result = deviation * jax.random.normal(rng, shape, jnp.float32)
    if cuts:
        result = result * block_levels(rng, shape, cuts, -0.22, 0.18)
    return jnp.clip(result, -most, most).astype(kind)


def bell_draw_with(rng, extent, spread, most, split, heavy, kind=jnp.bfloat16):
    drawn = spread * jax.random.normal(rng, extent, jnp.float32)
    if split:
        drawn = drawn * block_levels(rng, extent, split, -0.22, 0.18)
    return jnp.clip(with_spikes(drawn, jax.random.fold_in(rng, 3), *heavy), -most, most).astype(kind)


def setup_inputs(seed: int = 0) -> dict:
    seeds = jax.random.split(jax.random.key(seed), 10)
    history = gaussian(seeds[0], (HIST, ELEMENTS), 1.0, 6.0, ((1, 256),))
    lag_class = touch_ends(jax.random.randint(seeds[1], (ELEMENTS,), 0, CLASSES), jax.random.fold_in(seeds[1], 1), 0, CLASSES - 1).astype(jnp.int32)
    lag_table = gaussian(seeds[2], (CLASSES, LAGS), 0.15, 0.9, (), jnp.float32)
    row_bases = gaussian(seeds[3], (ELEMENTS, RANK), CLUSTER ** -0.5, 0.25, ((0, 256),))
    coupling = bell_draw_with(seeds[4], (CLUSTERS, N_ROW, N_COL, RANK, RANK), (CLUSTERS * RANK) ** -0.5, 0.09375, ((0, 32), (2, 8)), (0, 1, 32, 2.75))
    block_ranks = touch_ends(jax.random.randint(seeds[5], (CLUSTERS, N_ROW, N_COL), RANK // 4, RANK + 1), jax.random.fold_in(seeds[5], 1), RANK // 4, RANK).astype(jnp.int32)
    col_bases = gaussian(seeds[6], (ELEMENTS, RANK), RANK ** -0.5, 0.75, ((0, 256),))
    near_blocks = gaussian(seeds[7], (CLUSTERS, 3, CLUSTER, CLUSTER), CLUSTER ** -0.5, 0.25, ((0, 256),))
    near_flags = touch_ends((jax.random.randint(seeds[8], (CLUSTERS, 2), 0, 2) < 1).astype(jnp.int32), jax.random.fold_in(seeds[8], 1), 0, 1)
    return {"history": history, "lag_class": lag_class, "lag_table": lag_table, "row_bases": row_bases, "coupling": coupling, "block_ranks": block_ranks, "col_bases": col_bases, "near_blocks": near_blocks, "near_flags": near_flags}


def contract_cluster(lag_table, pieces):
    cluster_hist, cluster_class, cluster_rows, cluster_near, cluster_flags = pieces
    lag_weights = jnp.transpose(lag_table[cluster_class])

    def add_lag(lag_step, summed):
        window = lax.dynamic_slice_in_dim(cluster_hist, lag_step, STEPS, 0).astype(jnp.float32)
        return summed + window * lax.dynamic_slice_in_dim(lag_weights, lag_step, 1, 0)

    contracted = lax.fori_loop(jnp.int32(0), jnp.int32(LAGS), add_lag, jnp.zeros((STEPS, CLUSTER), jnp.float32)).astype(jnp.bfloat16)
    projected = jnp.dot(contracted, cluster_rows, preferred_element_type=jnp.float32).astype(jnp.bfloat16)
    near_terms = jnp.einsum("te,dej->dtj", contracted.astype(jnp.float32), cluster_near.astype(jnp.float32))
    flag_float = cluster_flags.astype(jnp.float32)
    lower_terms = (near_terms[0] * flag_float[0]).astype(jnp.bfloat16)
    upper_terms = (near_terms[2] * flag_float[1]).astype(jnp.bfloat16)
    return projected, near_terms[1], lower_terms, upper_terms


def reference(history, lag_class, lag_table, row_bases, coupling, block_ranks, col_bases, near_blocks, near_flags):
    hist_blocks = jnp.transpose(history.reshape(HIST, CLUSTERS, CLUSTER), (1, 0, 2))
    pieces = (hist_blocks, lag_class.reshape(CLUSTERS, CLUSTER), row_bases.reshape(CLUSTERS, CLUSTER, RANK), near_blocks, near_flags)
    projected, centre, lower_terms, upper_terms = lax.map(lambda items: contract_cluster(lag_table, items), pieces)

    proj_blocks = projected.reshape(N_ROW, N_COL, STEPS, RANK)
    coup_blocks = coupling.reshape(N_ROW, N_COL, N_ROW, N_COL, RANK, RANK)
    rank_blocks = block_ranks.reshape(N_ROW, N_COL, N_ROW, N_COL)
    flag_blocks = near_flags.reshape(N_ROW, N_COL, 2)
    levels = jnp.arange(RANK, dtype=jnp.int32)
    source_local = jnp.arange(N_COL, dtype=jnp.int32)[:, None, None]
    target_row = jnp.arange(N_ROW, dtype=jnp.int32)[None, :, None]
    target_col = jnp.arange(N_COL, dtype=jnp.int32)[None, None, :]

    def add_block(summed, items):
        block_proj, block_coup, block_rank, block_flag, block_row = items
        offset = jnp.remainder((target_row - block_row) * N_COL + target_col - source_local, CLUSTERS)
        left_near = (block_flag[:, 0] == 1)[:, None, None]
        right_near = (block_flag[:, 1] == 1)[:, None, None]
        near_pair = (offset == 0) | ((offset == CLUSTERS - 1) & left_near) | ((offset == 1) & right_near)
        live_rank = levels < block_rank[..., None]
        live_pairs = jnp.logical_not(near_pair)[..., None, None] & live_rank[..., :, None] & live_rank[..., None, :]
        masked = jnp.where(live_pairs, block_coup.astype(jnp.float32), jnp.float32(0.0))
        partial_value = jnp.einsum("ita,iqcab->tqcb", block_proj.astype(jnp.float32), masked)
        rounded = lax.optimization_barrier(partial_value.astype(jnp.bfloat16))
        return summed + rounded.astype(jnp.float32), None

    start_sum = jnp.zeros((STEPS, N_ROW, N_COL, RANK), jnp.float32)
    row_ids = jnp.arange(N_ROW, dtype=jnp.int32)
    summed, _ = lax.scan(add_block, start_sum, (proj_blocks, coup_blocks, rank_blocks, flag_blocks, row_ids))
    coeffs = summed.astype(jnp.bfloat16).reshape(STEPS, CLUSTERS, RANK)
    far_part = jnp.einsum("tjb,jeb->jte", coeffs.astype(jnp.float32), col_bases.reshape(CLUSTERS, CLUSTER, RANK).astype(jnp.float32))
    from_left = jnp.roll(upper_terms, 1, axis=0)
    from_right = jnp.roll(lower_terms, -1, axis=0)
    total = far_part + centre + from_left.astype(jnp.float32) + from_right.astype(jnp.float32)
    return jnp.transpose(total, (1, 0, 2)).reshape(STEPS, ELEMENTS)
```

```python
import jax
import jax.numpy as jnp
from jax import lax
from jax.sharding import PartitionSpec as P

BLOCK = 256


def shifted(value, axis, pairs):
    return lax.ppermute(value, axis, pairs)


def lag_matrices(lag_table, lags):
    rows = jnp.arange(BLOCK, dtype=jnp.int32)[:, None]
    cols = jnp.arange(BLOCK + lags, dtype=jnp.int32)[None, :]
    gap = cols - rows
    live = (gap >= 0) & (gap < lags)
    picked = jnp.take(lag_table, jnp.clip(gap, 0, lags - 1), axis=1)
    full = jnp.where(live[None], picked, 0.0)
    high = full.astype(jnp.bfloat16)
    low = (full - high.astype(jnp.float32)).astype(jnp.bfloat16)
    return high, low


def lag_contract(history, lag_class, lag_table, steps):
    class_total, lags = lag_table.shape
    blocks = steps // BLOCK
    padded_rows = (blocks + 1) * BLOCK
    chosen = (lag_class[None, :] == jnp.arange(class_total, dtype=jnp.int32)[:, None]).astype(
        jnp.bfloat16
    )
    padded = jnp.pad(history, ((0, padded_rows - history.shape[0]), (0, 0)))
    split = chosen[:, None, :] * padded[None, :, :]
    split = split.reshape(class_total, blocks + 1, BLOCK, history.shape[1])
    head = split[:, :blocks]
    tail = split[:, 1:, :lags]
    high, low = lag_matrices(lag_table, lags)
    total = jnp.zeros((blocks, BLOCK, history.shape[1]), jnp.float32)
    for part in (high, low):
        total = total + jnp.einsum(
            "kts,kbse->bte", part[:, :, :BLOCK], head, preferred_element_type=jnp.float32
        )
        total = total + jnp.einsum(
            "kts,kbse->bte", part[:, :, BLOCK:], tail, preferred_element_type=jnp.float32
        )
    return total.reshape(steps, history.shape[1]).astype(jnp.bfloat16)


def row_reduce(partial, row_count):
    r = lax.axis_index("row")
    core = r % 2
    zpos = (r // 2) % 8
    yh = r // 16
    steps, width = partial.shape[1], partial.shape[2]
    grid = partial.reshape(2, 8, 2, steps, width)
    keep = lax.dynamic_index_in_dim(grid, core, axis=2, keepdims=False)
    give = lax.dynamic_index_in_dim(grid, 1 - core, axis=2, keepdims=False)
    core_pairs = [(s, s ^ 1) for s in range(row_count)]
    got = shifted(give, "row", core_pairs)
    summed = keep.astype(jnp.float32) + got.astype(jnp.float32)
    sent = summed.astype(jnp.bfloat16)

    half = steps // 2
    up_pairs = [(s, (s // 16) * 16 + (((s // 2) % 8 + 1) % 8) * 2 + s % 2) for s in range(row_count)]
    down_pairs = [(s, (s // 16) * 16 + (((s // 2) % 8 + 7) % 8) * 2 + s % 2) for s in range(row_count)]

    def chunk(values, index, lo):
        block = lax.dynamic_index_in_dim(values, index % 8, axis=1, keepdims=False)
        return block[:, lo : lo + half]

    up = shifted(chunk(sent, zpos + 7, 0), "row", up_pairs)
    down = shifted(chunk(sent, zpos + 1, half), "row", down_pairs)
    for step in range(1, 7):
        up_acc = up.astype(jnp.float32) + chunk(summed, zpos + 7 * (step + 1), 0)
        down_acc = down.astype(jnp.float32) + chunk(summed, zpos + step + 1, half)
        up = shifted(up_acc.astype(jnp.bfloat16), "row", up_pairs)
        down = shifted(down_acc.astype(jnp.bfloat16), "row", down_pairs)
    up_acc = up.astype(jnp.float32) + chunk(summed, zpos, 0)
    down_acc = down.astype(jnp.float32) + chunk(summed, zpos, half)
    mine = jnp.concatenate([up_acc, down_acc], axis=1)
    keep_y = lax.dynamic_index_in_dim(mine, yh, axis=0, keepdims=False)
    give_y = lax.dynamic_index_in_dim(mine, 1 - yh, axis=0, keepdims=False)
    y_pairs = [(s, s ^ 16) for s in range(row_count)]
    got_y = shifted(give_y.astype(jnp.bfloat16), "row", y_pairs)
    return keep_y + got_y.astype(jnp.float32)


def local(
    history,
    lag_class,
    lag_table,
    row_bases,
    coupling,
    block_ranks,
    col_bases,
    near_blocks,
    near_flags,
):
    row_count = lax.axis_size("row")
    col_count = lax.axis_size("col")
    cluster_total = row_count * col_count
    row_index = lax.axis_index("row")
    col_index = lax.axis_index("col")
    rank_cap = row_bases.shape[1]
    steps = history.shape[0] - lag_table.shape[1] + 1
    contracted = lag_contract(history, lag_class, lag_table, steps)
    projected = jnp.dot(contracted, row_bases, preferred_element_type=jnp.float32).astype(
        jnp.bfloat16
    )
    flag_block = jnp.zeros((16, rank_cap), jnp.bfloat16).at[0, 0:2].set(
        near_flags[0].astype(jnp.bfloat16)
    )
    extended = jnp.concatenate([projected, flag_block], axis=0)
    gathered = lax.all_gather(extended, "col", axis=0, tiled=False)
    source_proj = gathered[:, :steps]
    flag_rows = gathered[:, steps, 0:2]

    near_terms = jnp.einsum(
        "te,dej->dtj", contracted, near_blocks[0], preferred_element_type=jnp.float32
    )
    flag_float = near_flags[0].astype(jnp.float32)
    lower_terms = (near_terms[0] * flag_float[0]).astype(jnp.bfloat16)
    upper_terms = (near_terms[2] * flag_float[1]).astype(jnp.bfloat16)
    flat_next = [(s, (s + 1) % cluster_total) for s in range(cluster_total)]
    flat_prev = [(s, (s - 1) % cluster_total) for s in range(cluster_total)]
    from_left = shifted(upper_terms, ("row", "col"), flat_next)
    from_right = shifted(lower_terms, ("row", "col"), flat_prev)

    source_local = jnp.arange(col_count, dtype=jnp.int32)[:, None]
    target_row = jnp.arange(row_count, dtype=jnp.int32)[None, :]
    offset = jnp.remainder(
        (target_row - row_index) * col_count + col_index - source_local, cluster_total
    )
    left_near = flag_rows[:, 0:1] > 0.5
    right_near = flag_rows[:, 1:2] > 0.5
    near_pair = (
        (offset == 0) | (offset == cluster_total - 1) & left_near | (offset == 1) & right_near
    )
    levels = jnp.arange(rank_cap, dtype=jnp.int32)
    live_rank = levels[None, None, :] < block_ranks[:, :, 0][:, :, None]
    live_pairs = (
        jnp.logical_not(near_pair)[:, :, None, None]
        & live_rank[:, :, :, None]
        & live_rank[:, :, None, :]
    )
    masked = jnp.where(live_pairs, coupling[:, :, 0], jnp.zeros((), jnp.bfloat16))
    partial = jnp.einsum(
        "sta,sqab->qtb", source_proj, masked, preferred_element_type=jnp.float32
    ).astype(jnp.bfloat16)
    coeffs = row_reduce(partial, row_count).astype(jnp.bfloat16)
    far_part = jnp.einsum("tb,eb->te", coeffs, col_bases, preferred_element_type=jnp.float32)
    return far_part + near_terms[1] + from_left.astype(jnp.float32) + from_right.astype(jnp.float32)


def solution(mesh):
    return jax.shard_map(
        local,
        mesh=mesh,
        in_specs=(
            P(None, ("row", "col")),
            P(("row", "col")),
            P(),
            P(("row", "col"), None),
            P("row", None, "col", None, None),
            P("row", None, "col"),
            P(("row", "col"), None),
            P(("row", "col"), None, None, None),
            P(("row", "col"), None),
        ),
        out_specs=P(None, ("row", "col")),
        check_vma=False,
    )
```

```python
import jax
import jax.numpy as jnp
from jax import lax
from jax.sharding import PartitionSpec as P

BLOCK = 256


def shifted(value, axis, pairs):
    return lax.ppermute(value, axis, pairs)


def lag_matrices(lag_table, lags):
    class_total = lag_table.shape[0]
    period = 2 * BLOCK + lags
    row = jnp.pad(lag_table, ((0, 0), (0, period - lags)))
    tiled = jnp.tile(row, (1, BLOCK))[:, : BLOCK * (period - 1)]
    full = tiled.reshape(class_total, BLOCK, period - 1)[:, :, : BLOCK + lags]
    high = full.astype(jnp.bfloat16)
    low = (full - high.astype(jnp.float32)).astype(jnp.bfloat16)
    return high, low


def lag_contract(history, lag_class, lag_table, steps):
    class_total, lags = lag_table.shape
    blocks = steps // BLOCK
    padded_rows = (blocks + 1) * BLOCK
    chosen = (lag_class[None, :] == jnp.arange(class_total, dtype=jnp.int32)[:, None]).astype(
        jnp.bfloat16
    )
    padded = jnp.pad(history, ((0, padded_rows - history.shape[0]), (0, 0)))
    split = chosen[:, None, :] * padded[None, :, :]
    split = split.reshape(class_total, blocks + 1, BLOCK, history.shape[1])
    head = split[:, :blocks]
    tail = split[:, 1:, :lags]
    high, low = lag_matrices(lag_table, lags)
    total = jnp.zeros((blocks, BLOCK, history.shape[1]), jnp.float32)
    for part in (high, low):
        total = total + jnp.einsum(
            "kts,kbse->bte", part[:, :, :BLOCK], head, preferred_element_type=jnp.float32
        )
        total = total + jnp.einsum(
            "kts,kbse->bte", part[:, :, BLOCK:], tail, preferred_element_type=jnp.float32
        )
    return total.reshape(steps, history.shape[1]).astype(jnp.bfloat16)


def row_reduce(partial, row_count):
    r = lax.axis_index("row")
    core = r % 2
    zpos = (r // 2) % 8
    yh = r // 16
    steps, width = partial.shape[1], partial.shape[2]
    grid = partial.reshape(2, 8, 2, steps, width)
    keep = lax.dynamic_index_in_dim(grid, core, axis=2, keepdims=False)
    give = lax.dynamic_index_in_dim(grid, 1 - core, axis=2, keepdims=False)
    core_pairs = [(s, s ^ 1) for s in range(row_count)]
    got = shifted(give, "row", core_pairs)
    summed = keep.astype(jnp.float32) + got.astype(jnp.float32)
    sent = summed.astype(jnp.bfloat16)

    half = steps // 2
    up_pairs = [(s, (s // 16) * 16 + (((s // 2) % 8 + 1) % 8) * 2 + s % 2) for s in range(row_count)]
    down_pairs = [(s, (s // 16) * 16 + (((s // 2) % 8 + 7) % 8) * 2 + s % 2) for s in range(row_count)]

    def chunk(values, index, lo):
        block = lax.dynamic_index_in_dim(values, index % 8, axis=1, keepdims=False)
        return block[:, lo : lo + half]

    up = shifted(chunk(sent, zpos + 7, 0), "row", up_pairs)
    down = shifted(chunk(sent, zpos + 1, half), "row", down_pairs)
    for step in range(1, 7):
        up_acc = up.astype(jnp.float32) + chunk(summed, zpos + 7 * (step + 1), 0)
        down_acc = down.astype(jnp.float32) + chunk(summed, zpos + step + 1, half)
        up = shifted(up_acc.astype(jnp.bfloat16), "row", up_pairs)
        down = shifted(down_acc.astype(jnp.bfloat16), "row", down_pairs)
    up_acc = up.astype(jnp.float32) + chunk(summed, zpos, 0)
    down_acc = down.astype(jnp.float32) + chunk(summed, zpos, half)
    mine = jnp.concatenate([up_acc, down_acc], axis=1)
    keep_y = lax.dynamic_index_in_dim(mine, yh, axis=0, keepdims=False)
    give_y = lax.dynamic_index_in_dim(mine, 1 - yh, axis=0, keepdims=False)
    y_pairs = [(s, s ^ 16) for s in range(row_count)]
    got_y = shifted(give_y.astype(jnp.bfloat16), "row", y_pairs)
    return keep_y + got_y.astype(jnp.float32)


def local(
    history,
    lag_class,
    lag_table,
    row_bases,
    coupling,
    block_ranks,
    col_bases,
    near_blocks,
    near_flags,
):
    row_count = lax.axis_size("row")
    col_count = lax.axis_size("col")
    cluster_total = row_count * col_count
    row_index = lax.axis_index("row")
    col_index = lax.axis_index("col")
    rank_cap = row_bases.shape[1]
    steps = history.shape[0] - lag_table.shape[1] + 1
    contracted = lag_contract(history, lag_class, lag_table, steps)
    projected = jnp.dot(contracted, row_bases, preferred_element_type=jnp.float32).astype(
        jnp.bfloat16
    )
    flag_block = jnp.zeros((16, rank_cap), jnp.bfloat16).at[0, 0:2].set(
        near_flags[0].astype(jnp.bfloat16)
    )
    extended = jnp.concatenate([projected, flag_block], axis=0)
    gathered = lax.all_gather(extended, "col", axis=0, tiled=False)
    source_proj = gathered[:, :steps]
    flag_rows = gathered[:, steps, 0:2]

    near_terms = jnp.einsum(
        "te,dej->dtj", contracted, near_blocks[0], preferred_element_type=jnp.float32
    )
    flag_float = near_flags[0].astype(jnp.float32)
    lower_terms = (near_terms[0] * flag_float[0]).astype(jnp.bfloat16)
    upper_terms = (near_terms[2] * flag_float[1]).astype(jnp.bfloat16)
    flat_next = [(s, (s + 1) % cluster_total) for s in range(cluster_total)]
    flat_prev = [(s, (s - 1) % cluster_total) for s in range(cluster_total)]
    from_left = shifted(upper_terms, ("row", "col"), flat_next)
    from_right = shifted(lower_terms, ("row", "col"), flat_prev)

    source_local = jnp.arange(col_count, dtype=jnp.int32)[:, None]
    target_row = jnp.arange(row_count, dtype=jnp.int32)[None, :]
    offset = jnp.remainder(
        (target_row - row_index) * col_count + col_index - source_local, cluster_total
    )
    left_near = flag_rows[:, 0:1] > 0.5
    right_near = flag_rows[:, 1:2] > 0.5
    near_pair = (
        (offset == 0) | (offset == cluster_total - 1) & left_near | (offset == 1) & right_near
    )
    levels = jnp.arange(rank_cap, dtype=jnp.int32)
    live_rank = levels[None, None, :] < block_ranks[:, :, 0][:, :, None]
    live_pairs = (
        jnp.logical_not(near_pair)[:, :, None, None]
        & live_rank[:, :, :, None]
        & live_rank[:, :, None, :]
    )
    masked = jnp.where(live_pairs, coupling[:, :, 0], jnp.zeros((), jnp.bfloat16))
    partial = jnp.einsum(
        "sta,sqab->qtb", source_proj, masked, preferred_element_type=jnp.float32
    ).astype(jnp.bfloat16)
    coeffs = lax.psum_scatter(partial, "row", scatter_dimension=0, tiled=True)[0]
    far_part = jnp.einsum("tb,eb->te", coeffs, col_bases, preferred_element_type=jnp.float32)
    return far_part + near_terms[1] + from_left.astype(jnp.float32) + from_right.astype(jnp.float32)


def solution(mesh):
    return jax.shard_map(
        local,
        mesh=mesh,
        in_specs=(
            P(None, ("row", "col")),
            P(("row", "col")),
            P(),
            P(("row", "col"), None),
            P("row", None, "col", None, None),
            P("row", None, "col"),
            P(("row", "col"), None),
            P(("row", "col"), None, None, None),
            P(("row", "col"), None),
        ),
        out_specs=P(None, ("row", "col")),
        check_vma=False,
    )
```

```python
import functools

import jax
import jax.numpy as jnp
from jax import lax
from jax.experimental import pallas as pl
from jax.experimental.pallas import tpu as pltpu
from jax.sharding import PartitionSpec as P


def lag_contract(history, lag_class, lag_table):
    class_total = lag_table.shape[0]
    chosen = (lag_class[None, :] == jnp.arange(class_total, dtype=jnp.int32)[:, None]).astype(
        jnp.float32
    )
    lag_weights = jnp.dot(jnp.transpose(lag_table), chosen, precision=lax.Precision.HIGHEST)
    kernel = lag_weights[:, None, :]
    signal = history.astype(jnp.float32)[None, :, :]
    summed = lax.conv_general_dilated(
        signal,
        kernel,
        (1,),
        "VALID",
        dimension_numbers=("NWC", "WIO", "NWC"),
        feature_group_count=history.shape[1],
        precision=lax.Precision.HIGHEST,
    )
    return summed[0].astype(jnp.bfloat16)


def ring_kernel(z_count, data_ref, out_ref, recv, send, send_sem, recv_sem):
    row = lax.axis_index("row")
    col = lax.axis_index("col")
    core = row % 2
    zpos = (row // 2) % z_count
    base = row - zpos * 2
    up_dev = base + ((zpos + 1) % z_count) * 2
    down_dev = base + ((zpos + z_count - 1) % z_count) * 2
    half = data_ref.shape[2] // 2
    mesh_kind = pl.DeviceIdType.MESH

    barrier = pltpu.get_barrier_semaphore()
    for neighbour in (up_dev, down_dev):
        pl.semaphore_signal(barrier, inc=1, device_id=(neighbour, col), device_id_type=mesh_kind)
    pl.semaphore_wait(barrier, 2)

    rings = (
        (0, up_dev, lambda s: (zpos + (z_count - 1) * (s + 1)) % z_count, 0),
        (1, down_dev, lambda s: (zpos + s + 1) % z_count, half),
    )
    last = z_count - 1
    copies = {}
    for step in range(last):
        for way, target, index, low in rings:
            if step == 0:
                source = data_ref.at[index(step), :, pl.ds(low, half), :]
            else:
                copies[(way, step - 1)].wait_recv()
                own = data_ref[index(step), :, pl.ds(low, half), :].astype(jnp.float32)
                send[way, step] = (recv[way, step - 1].astype(jnp.float32) + own).astype(jnp.bfloat16)
                source = send.at[way, step]
            copy = pltpu.make_async_remote_copy(
                src_ref=source,
                dst_ref=recv.at[way, step],
                send_sem=send_sem.at[way, step],
                recv_sem=recv_sem.at[way, step],
                device_id=(target, col),
                device_id_type=mesh_kind,
            )
            copy.start()
            copies[(way, step)] = copy
    for way, target, index, low in rings:
        copies[(way, last - 1)].wait_recv()
        own = data_ref[zpos, :, pl.ds(low, half), :].astype(jnp.float32)
        out_ref[:, pl.ds(low, half), :] = recv[way, last - 1].astype(jnp.float32) + own
    for copy in copies.values():
        copy.wait_send()


def z_ring(data, z_count):
    _, pairs, rows, lanes = data.shape
    half = rows // 2
    return pl.pallas_call(
        functools.partial(ring_kernel, z_count),
        out_shape=jax.ShapeDtypeStruct((pairs, rows, lanes), jnp.float32),
        in_specs=[pl.BlockSpec(memory_space=pltpu.VMEM)],
        out_specs=pl.BlockSpec(memory_space=pltpu.VMEM),
        scratch_shapes=[
            pltpu.VMEM((2, z_count - 1, pairs, half, lanes), jnp.bfloat16),
            pltpu.VMEM((2, z_count - 1, pairs, half, lanes), jnp.bfloat16),
            pltpu.SemaphoreType.DMA((2, z_count - 1)),
            pltpu.SemaphoreType.DMA((2, z_count - 1)),
        ],
        compiler_params=pltpu.CompilerParams(collective_id=0, has_side_effects=True),
    )(data)


def row_reduce(partial, row_count):
    r = lax.axis_index("row")
    core = r % 2
    z_count = row_count // 4
    yh = r // (2 * z_count)
    steps, width = partial.shape[3], partial.shape[4]
    lanes = 128
    rows = steps * width // lanes
    keep = lax.dynamic_index_in_dim(partial, core, axis=0, keepdims=False)
    give = lax.dynamic_index_in_dim(partial, 1 - core, axis=0, keepdims=False)
    core_pairs = [(s, s ^ 1) for s in range(row_count)]
    got = lax.ppermute(give, "row", core_pairs)
    summed = (keep.astype(jnp.float32) + got.astype(jnp.float32)).astype(jnp.bfloat16)
    summed = summed.reshape(z_count, 2, rows, lanes)
    mine = z_ring(summed, z_count)
    keep_y = lax.dynamic_index_in_dim(mine, yh, axis=0, keepdims=False)
    give_y = lax.dynamic_index_in_dim(mine, 1 - yh, axis=0, keepdims=False)
    y_pairs = [(s, s ^ (2 * z_count)) for s in range(row_count)]
    got_y = lax.ppermute(give_y.astype(jnp.bfloat16), "row", y_pairs)
    return (keep_y + got_y.astype(jnp.float32)).reshape(steps, width)


def local(
    history,
    lag_class,
    lag_table,
    row_bases,
    coupling,
    block_ranks,
    col_bases,
    near_blocks,
    near_flags,
):
    row_count = lax.axis_size("row")
    col_count = lax.axis_size("col")
    cluster_total = row_count * col_count
    row_index = lax.axis_index("row")
    col_index = lax.axis_index("col")
    rank_cap = row_bases.shape[1]
    steps = history.shape[0] - lag_table.shape[1] + 1
    contracted = lag_contract(history, lag_class, lag_table)
    projected = jnp.dot(contracted, row_bases, preferred_element_type=jnp.float32).astype(
        jnp.bfloat16
    )
    flag_block = jnp.zeros((16, rank_cap), jnp.bfloat16).at[0, 0:2].set(
        near_flags[0].astype(jnp.bfloat16)
    )
    extended = jnp.concatenate([projected, flag_block], axis=0)
    gathered = lax.all_gather(extended, "col", axis=0, tiled=False)
    source_proj = gathered[:, :steps]
    flag_rows = gathered[:, steps, 0:2]

    near_terms = jnp.einsum(
        "te,dej->dtj", contracted, near_blocks[0], preferred_element_type=jnp.float32
    )
    flag_float = near_flags[0].astype(jnp.float32)
    lower_terms = (near_terms[0] * flag_float[0]).astype(jnp.bfloat16)
    upper_terms = (near_terms[2] * flag_float[1]).astype(jnp.bfloat16)
    flat_next = [(s, (s + 1) % cluster_total) for s in range(cluster_total)]
    flat_prev = [(s, (s - 1) % cluster_total) for s in range(cluster_total)]
    from_left = lax.ppermute(upper_terms, ("row", "col"), flat_next)
    from_right = lax.ppermute(lower_terms, ("row", "col"), flat_prev)

    source_local = jnp.arange(col_count, dtype=jnp.int32)[:, None]
    target_row = jnp.arange(row_count, dtype=jnp.int32)[None, :]
    offset = jnp.remainder(
        (target_row - row_index) * col_count + col_index - source_local, cluster_total
    )
    left_near = flag_rows[:, 0:1] > 0.5
    right_near = flag_rows[:, 1:2] > 0.5
    near_pair = (
        (offset == 0) | (offset == cluster_total - 1) & left_near | (offset == 1) & right_near
    )
    levels = jnp.arange(rank_cap, dtype=jnp.int32)
    live_rank = levels[None, None, :] < block_ranks[:, :, 0][:, :, None]
    live_pairs = (
        jnp.logical_not(near_pair)[:, :, None, None]
        & live_rank[:, :, :, None]
        & live_rank[:, :, None, :]
    )
    masked = jnp.where(live_pairs, coupling[:, :, 0], jnp.zeros((), jnp.bfloat16))
    z_count = row_count // 4
    masked = masked.reshape(col_count, 2, z_count, 2, rank_cap, rank_cap)
    partial = jnp.einsum(
        "sta,syzcab->czytb", source_proj, masked, preferred_element_type=jnp.float32
    ).astype(jnp.bfloat16)
    coeffs = row_reduce(partial, row_count).astype(jnp.bfloat16)
    far_part = jnp.einsum("tb,eb->te", coeffs, col_bases, preferred_element_type=jnp.float32)
    return far_part + near_terms[1] + from_left.astype(jnp.float32) + from_right.astype(jnp.float32)


def solution(mesh):
    return jax.shard_map(
        local,
        mesh=mesh,
        in_specs=(
            P(None, ("row", "col")),
            P(("row", "col")),
            P(),
            P(("row", "col"), None),
            P("row", None, "col", None, None),
            P("row", None, "col"),
            P(("row", "col"), None),
            P(("row", "col"), None, None, None),
            P(("row", "col"), None),
        ),
        out_specs=P(None, ("row", "col")),
        check_vma=False,
    )
```

```python
import functools

import jax
import jax.numpy as jnp
from jax import lax
from jax.experimental import pallas as pl
from jax.experimental.pallas import tpu as pltpu
from jax.sharding import PartitionSpec as P


def lag_contract(history, lag_class, lag_table):
    class_total = lag_table.shape[0]
    chosen = (lag_class[None, :] == jnp.arange(class_total, dtype=jnp.int32)[:, None]).astype(
        jnp.float32
    )
    lag_weights = jnp.dot(jnp.transpose(lag_table), chosen, precision=lax.Precision.HIGHEST)
    kernel = lag_weights[:, None, :]
    signal = history.astype(jnp.float32)[None, :, :]
    summed = lax.conv_general_dilated(
        signal,
        kernel,
        (1,),
        "VALID",
        dimension_numbers=("NWC", "WIO", "NWC"),
        feature_group_count=history.shape[1],
        precision=lax.Precision.HIGHEST,
    )
    return summed[0].astype(jnp.bfloat16)


def ring_kernel(z_count, data_ref, out_ref, recv, send, send_sem, recv_sem):
    row = lax.axis_index("row")
    col = lax.axis_index("col")
    core = row % 2
    zpos = (row // 2) % z_count
    base = row - zpos * 2
    up_dev = base + ((zpos + 1) % z_count) * 2
    down_dev = base + ((zpos + z_count - 1) % z_count) * 2
    half = data_ref.shape[3] // 2
    mesh_kind = pl.DeviceIdType.MESH

    barrier = pltpu.get_barrier_semaphore()
    for neighbour in (up_dev, down_dev):
        pl.semaphore_signal(barrier, inc=1, device_id=(neighbour, col), device_id_type=mesh_kind)
    pl.semaphore_wait(barrier, 2)

    rings = (
        (0, up_dev, lambda s: (zpos + (z_count - 1) * (s + 1)) % z_count, 0),
        (1, down_dev, lambda s: (zpos + s + 1) % z_count, half),
    )
    last = z_count - 1
    copies = {}
    for step in range(last):
        for way, target, index, low in rings:
            if step == 0:
                source = data_ref.at[index(step), :, :, pl.ds(low, half)]
            else:
                copies[(way, step - 1)].wait_recv()
                own = data_ref[index(step), :, :, pl.ds(low, half)].astype(jnp.float32)
                send[way, step] = (recv[way, step - 1].astype(jnp.float32) + own).astype(jnp.bfloat16)
                source = send.at[way, step]
            copy = pltpu.make_async_remote_copy(
                src_ref=source,
                dst_ref=recv.at[way, step],
                send_sem=send_sem.at[way, step],
                recv_sem=recv_sem.at[way, step],
                device_id=(target, col),
                device_id_type=mesh_kind,
            )
            copy.start()
            copies[(way, step)] = copy
    for way, target, index, low in rings:
        copies[(way, last - 1)].wait_recv()
        own = data_ref[zpos, :, :, pl.ds(low, half)].astype(jnp.float32)
        out_ref[:, :, pl.ds(low, half)] = recv[way, last - 1].astype(jnp.float32) + own
    for copy in copies.values():
        copy.wait_send()


def z_ring(data, z_count):
    _, pairs, width, steps = data.shape
    half = steps // 2
    return pl.pallas_call(
        functools.partial(ring_kernel, z_count),
        out_shape=jax.ShapeDtypeStruct((pairs, width, steps), jnp.float32),
        in_specs=[pl.BlockSpec(memory_space=pltpu.VMEM)],
        out_specs=pl.BlockSpec(memory_space=pltpu.VMEM),
        scratch_shapes=[
            pltpu.VMEM((2, z_count - 1, pairs, width, half), jnp.bfloat16),
            pltpu.VMEM((2, z_count - 1, pairs, width, half), jnp.bfloat16),
            pltpu.SemaphoreType.DMA((2, z_count - 1)),
            pltpu.SemaphoreType.DMA((2, z_count - 1)),
        ],
        compiler_params=pltpu.CompilerParams(collective_id=0, has_side_effects=True),
    )(data)


def row_reduce(keep, give, row_count):
    r = lax.axis_index("row")
    z_count = row_count // 4
    yh = r // (2 * z_count)
    core_pairs = [(s, s ^ 1) for s in range(row_count)]
    got = lax.ppermute(give, "row", core_pairs)
    summed = (keep.astype(jnp.float32) + got.astype(jnp.float32)).astype(jnp.bfloat16)
    mine = z_ring(summed, z_count)
    keep_y = lax.dynamic_index_in_dim(mine, yh, axis=0, keepdims=False)
    give_y = lax.dynamic_index_in_dim(mine, 1 - yh, axis=0, keepdims=False)
    y_pairs = [(s, s ^ (2 * z_count)) for s in range(row_count)]
    got_y = lax.ppermute(give_y.astype(jnp.bfloat16), "row", y_pairs)
    return keep_y + got_y.astype(jnp.float32)


def local(
    history,
    lag_class,
    lag_table,
    row_bases,
    coupling,
    block_ranks,
    col_bases,
    near_blocks,
    near_flags,
):
    row_count = lax.axis_size("row")
    col_count = lax.axis_size("col")
    cluster_total = row_count * col_count
    row_index = lax.axis_index("row")
    col_index = lax.axis_index("col")
    rank_cap = row_bases.shape[1]
    steps = history.shape[0] - lag_table.shape[1] + 1
    contracted = lag_contract(history, lag_class, lag_table)
    projected = jnp.dot(contracted, row_bases, preferred_element_type=jnp.float32).astype(
        jnp.bfloat16
    )
    flag_block = jnp.zeros((16, rank_cap), jnp.bfloat16).at[0, 0:2].set(
        near_flags[0].astype(jnp.bfloat16)
    )
    extended = jnp.concatenate([projected, flag_block], axis=0)
    gathered = lax.all_gather(extended, "col", axis=0, tiled=False)
    source_proj = gathered[:, :steps]
    flag_rows = gathered[:, steps, 0:2]

    near_terms = jnp.einsum(
        "te,dej->dtj", contracted, near_blocks[0], preferred_element_type=jnp.float32
    )
    flag_float = near_flags[0].astype(jnp.float32)
    lower_terms = (near_terms[0] * flag_float[0]).astype(jnp.bfloat16)
    upper_terms = (near_terms[2] * flag_float[1]).astype(jnp.bfloat16)
    flat_next = [(s, (s + 1) % cluster_total) for s in range(cluster_total)]
    flat_prev = [(s, (s - 1) % cluster_total) for s in range(cluster_total)]
    from_left = lax.ppermute(upper_terms, ("row", "col"), flat_next)
    from_right = lax.ppermute(lower_terms, ("row", "col"), flat_prev)

    source_local = jnp.arange(col_count, dtype=jnp.int32)[:, None]
    target_row = jnp.arange(row_count, dtype=jnp.int32)[None, :]
    offset = jnp.remainder(
        (target_row - row_index) * col_count + col_index - source_local, cluster_total
    )
    left_near = flag_rows[:, 0:1] > 0.5
    right_near = flag_rows[:, 1:2] > 0.5
    near_pair = (
        (offset == 0) | (offset == cluster_total - 1) & left_near | (offset == 1) & right_near
    )
    levels = jnp.arange(rank_cap, dtype=jnp.int32)
    live_rank = levels[None, None, :] < block_ranks[:, :, 0][:, :, None]
    live_pairs = (
        jnp.logical_not(near_pair)[:, :, None, None]
        & live_rank[:, :, :, None]
        & live_rank[:, :, None, :]
    )
    masked = jnp.where(live_pairs, coupling[:, :, 0], jnp.zeros((), jnp.bfloat16))
    z_count = row_count // 4
    masked = masked.reshape(col_count, 2, z_count, 2, rank_cap, rank_cap)
    core = row_index % 2
    halves = []
    for pick in (core, 1 - core):
        chosen = lax.dynamic_index_in_dim(masked, pick, axis=3, keepdims=False)
        halves.append(
            jnp.einsum(
                "sta,syzab->zybt", source_proj, chosen, preferred_element_type=jnp.float32
            ).astype(jnp.bfloat16)
        )
    coeffs = row_reduce(halves[0], halves[1], row_count).astype(jnp.bfloat16)
    far_part = jnp.einsum("bt,eb->te", coeffs, col_bases, preferred_element_type=jnp.float32)
    return far_part + near_terms[1] + from_left.astype(jnp.float32) + from_right.astype(jnp.float32)


def solution(mesh):
    return jax.shard_map(
        local,
        mesh=mesh,
        in_specs=(
            P(None, ("row", "col")),
            P(("row", "col")),
            P(),
            P(("row", "col"), None),
            P("row", None, "col", None, None),
            P("row", None, "col"),
            P(("row", "col"), None),
            P(("row", "col"), None, None, None),
            P(("row", "col"), None),
        ),
        out_specs=P(None, ("row", "col")),
        check_vma=False,
    )
```

```python
import functools

import jax
import jax.numpy as jnp
from jax import lax
from jax.experimental import pallas as pl
from jax.experimental.pallas import tpu as pltpu
from jax.sharding import PartitionSpec as P


def local_kernel(
    hist_ref, table_ref, class_ref, rows_ref, near_ref, flag_ref,
    proj_ref, centre_ref, lower_ref, upper_ref, high_ref, low_ref,
):
    block, width = high_ref.shape[1], high_ref.shape[2]
    step = pl.program_id(0)

    @pl.when(step == 0)
    def _():
        table = table_ref[...]
        for kind in range(high_ref.shape[0]):
            row = jnp.broadcast_to(table[kind : kind + 1, :], (block, width))
            full = pltpu.roll(row, 0, 1, stride=1, stride_axis=0)
            high = full.astype(jnp.bfloat16)
            high_ref[kind] = high
            low_ref[kind] = (full - high.astype(jnp.float32)).astype(jnp.bfloat16)

    start = pl.multiple_of(step * block, block)
    window = hist_ref[pl.ds(start, width), :]
    kinds = class_ref[...]
    total = jnp.zeros((block, window.shape[1]), jnp.float32)
    for kind in range(high_ref.shape[0]):
        part = jnp.dot(high_ref[kind], window, preferred_element_type=jnp.float32)
        part = part + jnp.dot(low_ref[kind], window, preferred_element_type=jnp.float32)
        total = jnp.where(kinds == kind, part, total)
    contracted = total.astype(jnp.bfloat16)
    proj_ref[...] = jnp.dot(contracted, rows_ref[...], preferred_element_type=jnp.float32).astype(
        jnp.bfloat16
    )
    flags = flag_ref[...]
    centre_ref[...] = jnp.dot(contracted, near_ref[1], preferred_element_type=jnp.float32)
    lower = jnp.dot(contracted, near_ref[0], preferred_element_type=jnp.float32)
    lower_ref[...] = (lower * flags[0:1, :]).astype(jnp.bfloat16)
    upper = jnp.dot(contracted, near_ref[2], preferred_element_type=jnp.float32)
    upper_ref[...] = (upper * flags[1:2, :]).astype(jnp.bfloat16)


def local_terms(history, lag_class, lag_table, row_bases, near_blocks, near_flags, steps):
    class_total, lags = lag_table.shape
    size = history.shape[1]
    rank = row_bases.shape[1]
    block = 256
    width = block + 128
    blocks = steps // block
    padded = jnp.pad(history, ((0, (blocks - 1) * block + width - history.shape[0]), (0, 0)))
    table = jnp.pad(lag_table, ((0, 0), (0, width - lags)))
    kinds = lag_class.reshape(1, size)
    flags = jnp.broadcast_to(near_flags[0].astype(jnp.float32)[:, None], (2, size))
    whole = lambda shape: pl.BlockSpec(shape, lambda b: (0,) * len(shape))
    rows_of = lambda cols: pl.BlockSpec((block, cols), lambda b: (b, 0))
    return pl.pallas_call(
        local_kernel,
        grid=(blocks,),
        out_shape=(
            jax.ShapeDtypeStruct((steps, rank), jnp.bfloat16),
            jax.ShapeDtypeStruct((steps, size), jnp.float32),
            jax.ShapeDtypeStruct((steps, size), jnp.bfloat16),
            jax.ShapeDtypeStruct((steps, size), jnp.bfloat16),
        ),
        in_specs=[
            whole(padded.shape),
            whole(table.shape),
            whole(kinds.shape),
            whole(row_bases.shape),
            whole(near_blocks.shape[1:]),
            whole(flags.shape),
        ],
        out_specs=(rows_of(rank), rows_of(size), rows_of(size), rows_of(size)),
        scratch_shapes=[
            pltpu.VMEM((class_total, block, width), jnp.bfloat16),
            pltpu.VMEM((class_total, block, width), jnp.bfloat16),
        ],
        compiler_params=pltpu.CompilerParams(dimension_semantics=("arbitrary",)),
    )(padded, table, kinds, row_bases, near_blocks[0], flags)


def ring_kernel(z_count, data_ref, out_ref, recv, send, send_sem, recv_sem):
    row = lax.axis_index("row")
    col = lax.axis_index("col")
    core = row % 2
    zpos = (row // 2) % z_count
    base = row - zpos * 2
    up_dev = base + ((zpos + 1) % z_count) * 2
    down_dev = base + ((zpos + z_count - 1) % z_count) * 2
    half = data_ref.shape[3] // 2
    mesh_kind = pl.DeviceIdType.MESH

    barrier = pltpu.get_barrier_semaphore()
    for neighbour in (up_dev, down_dev):
        pl.semaphore_signal(barrier, inc=1, device_id=(neighbour, col), device_id_type=mesh_kind)
    pl.semaphore_wait(barrier, 2)

    rings = (
        (0, up_dev, lambda s: (zpos + (z_count - 1) * (s + 1)) % z_count, 0),
        (1, down_dev, lambda s: (zpos + s + 1) % z_count, half),
    )
    last = z_count - 1
    copies = {}
    for step in range(last):
        for way, target, index, low in rings:
            if step == 0:
                source = data_ref.at[index(step), :, :, pl.ds(low, half)]
            else:
                copies[(way, step - 1)].wait_recv()
                own = data_ref[index(step), :, :, pl.ds(low, half)].astype(jnp.float32)
                send[way, step] = (recv[way, step - 1].astype(jnp.float32) + own).astype(jnp.bfloat16)
                source = send.at[way, step]
            copy = pltpu.make_async_remote_copy(
                src_ref=source,
                dst_ref=recv.at[way, step],
                send_sem=send_sem.at[way, step],
                recv_sem=recv_sem.at[way, step],
                device_id=(target, col),
                device_id_type=mesh_kind,
            )
            copy.start()
            copies[(way, step)] = copy
    for way, target, index, low in rings:
        copies[(way, last - 1)].wait_recv()
        own = data_ref[zpos, :, :, pl.ds(low, half)].astype(jnp.float32)
        out_ref[:, :, pl.ds(low, half)] = recv[way, last - 1].astype(jnp.float32) + own
    for copy in copies.values():
        copy.wait_send()


def z_ring(data, z_count):
    _, pairs, width, steps = data.shape
    half = steps // 2
    return pl.pallas_call(
        functools.partial(ring_kernel, z_count),
        out_shape=jax.ShapeDtypeStruct((pairs, width, steps), jnp.float32),
        in_specs=[pl.BlockSpec(memory_space=pltpu.VMEM)],
        out_specs=pl.BlockSpec(memory_space=pltpu.VMEM),
        scratch_shapes=[
            pltpu.VMEM((2, z_count - 1, pairs, width, half), jnp.bfloat16),
            pltpu.VMEM((2, z_count - 1, pairs, width, half), jnp.bfloat16),
            pltpu.SemaphoreType.DMA((2, z_count - 1)),
            pltpu.SemaphoreType.DMA((2, z_count - 1)),
        ],
        compiler_params=pltpu.CompilerParams(collective_id=0, has_side_effects=True),
    )(data)


def row_reduce(keep, give, row_count):
    r = lax.axis_index("row")
    z_count = row_count // 4
    yh = r // (2 * z_count)
    core_pairs = [(s, s ^ 1) for s in range(row_count)]
    got = lax.ppermute(give, "row", core_pairs)
    summed = (keep.astype(jnp.float32) + got.astype(jnp.float32)).astype(jnp.bfloat16)
    mine = z_ring(summed, z_count)
    keep_y = lax.dynamic_index_in_dim(mine, yh, axis=0, keepdims=False)
    give_y = lax.dynamic_index_in_dim(mine, 1 - yh, axis=0, keepdims=False)
    y_pairs = [(s, s ^ (2 * z_count)) for s in range(row_count)]
    got_y = lax.ppermute(give_y.astype(jnp.bfloat16), "row", y_pairs)
    return keep_y + got_y.astype(jnp.float32)


def local(
    history,
    lag_class,
    lag_table,
    row_bases,
    coupling,
    block_ranks,
    col_bases,
    near_blocks,
    near_flags,
):
    row_count = lax.axis_size("row")
    col_count = lax.axis_size("col")
    cluster_total = row_count * col_count
    row_index = lax.axis_index("row")
    col_index = lax.axis_index("col")
    rank_cap = row_bases.shape[1]
    steps = history.shape[0] - lag_table.shape[1] + 1
    projected, centre, lower_terms, upper_terms = local_terms(
        history, lag_class, lag_table, row_bases, near_blocks, near_flags, steps
    )
    flag_block = jnp.zeros((16, rank_cap), jnp.bfloat16).at[0, 0:2].set(
        near_flags[0].astype(jnp.bfloat16)
    )
    extended = jnp.concatenate([projected, flag_block], axis=0)
    gathered = lax.all_gather(extended, "col", axis=0, tiled=False)
    source_proj = gathered[:, :steps]
    flag_rows = gathered[:, steps, 0:2]

    flat_next = [(s, (s + 1) % cluster_total) for s in range(cluster_total)]
    flat_prev = [(s, (s - 1) % cluster_total) for s in range(cluster_total)]
    from_left = lax.ppermute(upper_terms, ("row", "col"), flat_next)
    from_right = lax.ppermute(lower_terms, ("row", "col"), flat_prev)

    source_local = jnp.arange(col_count, dtype=jnp.int32)[:, None]
    target_row = jnp.arange(row_count, dtype=jnp.int32)[None, :]
    offset = jnp.remainder(
        (target_row - row_index) * col_count + col_index - source_local, cluster_total
    )
    left_near = flag_rows[:, 0:1] > 0.5
    right_near = flag_rows[:, 1:2] > 0.5
    near_pair = (
        (offset == 0) | (offset == cluster_total - 1) & left_near | (offset == 1) & right_near
    )
    levels = jnp.arange(rank_cap, dtype=jnp.int32)
    live_rank = levels[None, None, :] < block_ranks[:, :, 0][:, :, None]
    live_pairs = (
        jnp.logical_not(near_pair)[:, :, None, None]
        & live_rank[:, :, :, None]
        & live_rank[:, :, None, :]
    )
    masked = jnp.where(live_pairs, coupling[:, :, 0], jnp.zeros((), jnp.bfloat16))
    z_count = row_count // 4
    masked = masked.reshape(col_count, 2, z_count, 2, rank_cap, rank_cap)
    core = row_index % 2
    halves = []
    for pick in (core, 1 - core):
        chosen = lax.dynamic_index_in_dim(masked, pick, axis=3, keepdims=False)
        halves.append(
            jnp.einsum(
                "sta,syzab->zybt", source_proj, chosen, preferred_element_type=jnp.float32
            ).astype(jnp.bfloat16)
        )
    coeffs = row_reduce(halves[0], halves[1], row_count).astype(jnp.bfloat16)
    far_part = jnp.einsum("bt,eb->te", coeffs, col_bases, preferred_element_type=jnp.float32)
    return far_part + centre + from_left.astype(jnp.float32) + from_right.astype(jnp.float32)


def solution(mesh):
    return jax.shard_map(
        local,
        mesh=mesh,
        in_specs=(
            P(None, ("row", "col")),
            P(("row", "col")),
            P(),
            P(("row", "col"), None),
            P("row", None, "col", None, None),
            P("row", None, "col"),
            P(("row", "col"), None),
            P(("row", "col"), None, None, None),
            P(("row", "col"), None),
        ),
        out_specs=P(None, ("row", "col")),
        check_vma=False,
    )
```

```python
import functools

import jax
import jax.numpy as jnp
from jax import lax
from jax.experimental import pallas as pl
from jax.experimental.pallas import tpu as pltpu
from jax.sharding import PartitionSpec as P


def local_kernel(
    hist_ref, table_ref, class_ref, rows_ref, near_ref, flag_ref,
    proj_ref, centre_ref, lower_ref, upper_ref, high_ref, low_ref,
):
    block, width = high_ref.shape[1], high_ref.shape[2]
    step = pl.program_id(0)

    @pl.when(step == 0)
    def _():
        table = table_ref[...]
        for kind in range(high_ref.shape[0]):
            row = jnp.broadcast_to(table[kind : kind + 1, :], (block, width))
            full = pltpu.roll(row, 0, 1, stride=1, stride_axis=0)
            high = full.astype(jnp.bfloat16)
            high_ref[kind] = high
            low_ref[kind] = (full - high.astype(jnp.float32)).astype(jnp.bfloat16)

    start = pl.multiple_of(step * block, block)
    window = hist_ref[pl.ds(start, width), :]
    kinds = class_ref[...]
    total = jnp.zeros((block, window.shape[1]), jnp.float32)
    for kind in range(high_ref.shape[0]):
        part = jnp.dot(high_ref[kind], window, preferred_element_type=jnp.float32)
        part = part + jnp.dot(low_ref[kind], window, preferred_element_type=jnp.float32)
        total = jnp.where(kinds == kind, part, total)
    contracted = total.astype(jnp.bfloat16)
    proj_ref[...] = jnp.dot(contracted, rows_ref[...], preferred_element_type=jnp.float32).astype(
        jnp.bfloat16
    )
    flags = flag_ref[...]
    centre_ref[...] = jnp.dot(contracted, near_ref[1], preferred_element_type=jnp.float32)
    lower = jnp.dot(contracted, near_ref[0], preferred_element_type=jnp.float32)
    lower_ref[...] = (lower * flags[0:1, :]).astype(jnp.bfloat16)
    upper = jnp.dot(contracted, near_ref[2], preferred_element_type=jnp.float32)
    upper_ref[...] = (upper * flags[1:2, :]).astype(jnp.bfloat16)


def local_terms(history, lag_class, lag_table, row_bases, near_blocks, near_flags, steps):
    class_total, lags = lag_table.shape
    size = history.shape[1]
    rank = row_bases.shape[1]
    block = 256
    width = block + 128
    blocks = steps // block
    padded = jnp.pad(history, ((0, (blocks - 1) * block + width - history.shape[0]), (0, 0)))
    table = jnp.pad(lag_table, ((0, 0), (0, width - lags)))
    kinds = lag_class.reshape(1, size)
    flags = jnp.broadcast_to(near_flags[0].astype(jnp.float32)[:, None], (2, size))
    whole = lambda shape: pl.BlockSpec(shape, lambda b: (0,) * len(shape))
    rows_of = lambda cols: pl.BlockSpec((block, cols), lambda b: (b, 0))
    return pl.pallas_call(
        local_kernel,
        grid=(blocks,),
        out_shape=(
            jax.ShapeDtypeStruct((steps, rank), jnp.bfloat16),
            jax.ShapeDtypeStruct((steps, size), jnp.float32),
            jax.ShapeDtypeStruct((steps, size), jnp.bfloat16),
            jax.ShapeDtypeStruct((steps, size), jnp.bfloat16),
        ),
        in_specs=[
            whole(padded.shape),
            whole(table.shape),
            whole(kinds.shape),
            whole(row_bases.shape),
            whole(near_blocks.shape[1:]),
            whole(flags.shape),
        ],
        out_specs=(rows_of(rank), rows_of(size), rows_of(size), rows_of(size)),
        scratch_shapes=[
            pltpu.VMEM((class_total, block, width), jnp.bfloat16),
            pltpu.VMEM((class_total, block, width), jnp.bfloat16),
        ],
        compiler_params=pltpu.CompilerParams(dimension_semantics=("arbitrary",)),
    )(padded, table, kinds, row_bases, near_blocks[0], flags)


def ring_kernel(z_count, data_ref, out_ref, recv, send, send_sem, recv_sem):
    row = lax.axis_index("row")
    col = lax.axis_index("col")
    core = row % 2
    zpos = (row // 2) % z_count
    base = row - zpos * 2
    up_dev = base + ((zpos + 1) % z_count) * 2
    down_dev = base + ((zpos + z_count - 1) % z_count) * 2
    half = data_ref.shape[3] // 2
    mesh_kind = pl.DeviceIdType.MESH

    barrier = pltpu.get_barrier_semaphore()
    for neighbour in (up_dev, down_dev):
        pl.semaphore_signal(barrier, inc=1, device_id=(neighbour, col), device_id_type=mesh_kind)
    pl.semaphore_wait(barrier, 2)

    rings = (
        (0, up_dev, lambda s: (zpos + (z_count - 1) * (s + 1)) % z_count, 0),
        (1, down_dev, lambda s: (zpos + s + 1) % z_count, half),
    )
    last = z_count - 1
    copies = {}
    for step in range(last):
        for way, target, index, low in rings:
            if step == 0:
                source = data_ref.at[index(step), :, :, pl.ds(low, half)]
            else:
                copies[(way, step - 1)].wait_recv()
                own = data_ref[index(step), :, :, pl.ds(low, half)].astype(jnp.float32)
                send[way, step] = (recv[way, step - 1].astype(jnp.float32) + own).astype(jnp.bfloat16)
                source = send.at[way, step]
            copy = pltpu.make_async_remote_copy(
                src_ref=source,
                dst_ref=recv.at[way, step],
                send_sem=send_sem.at[way, step],
                recv_sem=recv_sem.at[way, step],
                device_id=(target, col),
                device_id_type=mesh_kind,
            )
            copy.start()
            copies[(way, step)] = copy
    for way, target, index, low in rings:
        copies[(way, last - 1)].wait_recv()
        own = data_ref[zpos, :, :, pl.ds(low, half)].astype(jnp.float32)
        out_ref[:, :, pl.ds(low, half)] = recv[way, last - 1].astype(jnp.float32) + own
    for copy in copies.values():
        copy.wait_send()


def z_ring(data, z_count):
    _, pairs, width, steps = data.shape
    half = steps // 2
    return pl.pallas_call(
        functools.partial(ring_kernel, z_count),
        out_shape=jax.ShapeDtypeStruct((pairs, width, steps), jnp.float32),
        in_specs=[pl.BlockSpec(memory_space=pltpu.VMEM)],
        out_specs=pl.BlockSpec(memory_space=pltpu.VMEM),
        scratch_shapes=[
            pltpu.VMEM((2, z_count - 1, pairs, width, half), jnp.bfloat16),
            pltpu.VMEM((2, z_count - 1, pairs, width, half), jnp.bfloat16),
            pltpu.SemaphoreType.DMA((2, z_count - 1)),
            pltpu.SemaphoreType.DMA((2, z_count - 1)),
        ],
        compiler_params=pltpu.CompilerParams(collective_id=0, has_side_effects=True),
    )(data)


def row_reduce(keep, give, row_count):
    r = lax.axis_index("row")
    z_count = row_count // 4
    yh = r // (2 * z_count)
    core_pairs = [(s, s ^ 1) for s in range(row_count)]
    got = lax.ppermute(give, "row", core_pairs)
    summed = (keep.astype(jnp.float32) + got.astype(jnp.float32)).astype(jnp.bfloat16)
    mine = z_ring(summed, z_count)
    keep_y = lax.dynamic_index_in_dim(mine, yh, axis=0, keepdims=False)
    give_y = lax.dynamic_index_in_dim(mine, 1 - yh, axis=0, keepdims=False)
    y_pairs = [(s, s ^ (2 * z_count)) for s in range(row_count)]
    got_y = lax.ppermute(give_y.astype(jnp.bfloat16), "row", y_pairs)
    return keep_y + got_y.astype(jnp.float32)


def local(
    history,
    lag_class,
    lag_table,
    row_bases,
    coupling,
    block_ranks,
    col_bases,
    near_blocks,
    near_flags,
):
    row_count = lax.axis_size("row")
    col_count = lax.axis_size("col")
    cluster_total = row_count * col_count
    row_index = lax.axis_index("row")
    col_index = lax.axis_index("col")
    rank_cap = row_bases.shape[1]
    steps = history.shape[0] - lag_table.shape[1] + 1
    projected, centre, lower_terms, upper_terms = local_terms(
        history, lag_class, lag_table, row_bases, near_blocks, near_flags, steps
    )
    flag_block = jnp.zeros((16, rank_cap), jnp.bfloat16).at[0, 0:2].set(
        near_flags[0].astype(jnp.bfloat16)
    )
    extended = jnp.concatenate([projected, flag_block], axis=0)
    gathered = lax.all_gather(extended, "col", axis=0, tiled=False)
    source_proj = gathered[:, :steps]
    flag_rows = gathered[:, steps, 0:2]

    flat_next = [(s, (s + 1) % cluster_total) for s in range(cluster_total)]
    flat_prev = [(s, (s - 1) % cluster_total) for s in range(cluster_total)]
    from_left = lax.ppermute(upper_terms, ("row", "col"), flat_next)
    from_right = lax.ppermute(lower_terms, ("row", "col"), flat_prev)

    source_local = jnp.arange(col_count, dtype=jnp.int32)[:, None]
    target_row = jnp.arange(row_count, dtype=jnp.int32)[None, :]
    offset = jnp.remainder(
        (target_row - row_index) * col_count + col_index - source_local, cluster_total
    )
    levels = jnp.arange(rank_cap, dtype=jnp.int32)
    live_rank = levels[None, None, :] < block_ranks[:, :, 0][:, :, None]
    live_pairs = (
        (offset != 0)[:, :, None, None] & live_rank[:, :, :, None] & live_rank[:, :, None, :]
    )
    masked = jnp.where(live_pairs, coupling[:, :, 0], jnp.zeros((), jnp.bfloat16))
    source_proj, flag_rows, from_left, from_right = lax.optimization_barrier(
        (source_proj, flag_rows, from_left, from_right)
    )
    for way, lane in ((1, 1), (-1, 0)):
        source = jnp.remainder(col_index - way, col_count)
        target = jnp.remainder(row_index + (way - col_index + source) // col_count, row_count)
        corner = (source, target, 0, 0)
        piece = lax.dynamic_slice(masked, corner, (1, 1, rank_cap, rank_cap))
        far = lax.dynamic_index_in_dim(flag_rows, source, axis=0, keepdims=False)[lane] < 0.5
        piece = jnp.where(far, piece, jnp.zeros((), jnp.bfloat16))
        masked = lax.dynamic_update_slice(masked, piece, corner)
    z_count = row_count // 4
    masked = masked.reshape(col_count, 2, z_count, 2, rank_cap, rank_cap)
    core = row_index % 2
    halves = []
    for pick in (core, 1 - core):
        chosen = lax.dynamic_index_in_dim(masked, pick, axis=3, keepdims=False)
        halves.append(
            jnp.einsum(
                "sta,syzab->zybt", source_proj, chosen, preferred_element_type=jnp.float32
            ).astype(jnp.bfloat16)
        )
    coeffs = row_reduce(halves[0], halves[1], row_count).astype(jnp.bfloat16)
    far_part = jnp.einsum("bt,eb->te", coeffs, col_bases, preferred_element_type=jnp.float32)
    return far_part + centre + from_left.astype(jnp.float32) + from_right.astype(jnp.float32)


def solution(mesh):
    return jax.shard_map(
        local,
        mesh=mesh,
        in_specs=(
            P(None, ("row", "col")),
            P(("row", "col")),
            P(),
            P(("row", "col"), None),
            P("row", None, "col", None, None),
            P("row", None, "col"),
            P(("row", "col"), None),
            P(("row", "col"), None, None, None),
            P(("row", "col"), None),
        ),
        out_specs=P(None, ("row", "col")),
        check_vma=False,
    )
```

```python
import functools

import jax
import jax.numpy as jnp
from jax import lax
from jax.experimental import pallas as pl
from jax.experimental.pallas import tpu as pltpu
from jax.sharding import PartitionSpec as P


def local_kernel(
    hist_ref, table_ref, class_ref, rows_ref, near_ref, flag_ref,
    proj_ref, centre_ref, lower_ref, upper_ref, high_ref, low_ref,
):
    block, width = high_ref.shape[1], high_ref.shape[2]
    step = pl.program_id(0)

    @pl.when(step == 0)
    def _():
        table = table_ref[...]
        for kind in range(high_ref.shape[0]):
            row = jnp.broadcast_to(table[kind : kind + 1, :], (block, width))
            full = pltpu.roll(row, 0, 1, stride=1, stride_axis=0)
            high = full.astype(jnp.bfloat16)
            high_ref[kind] = high
            low_ref[kind] = (full - high.astype(jnp.float32)).astype(jnp.bfloat16)

    start = pl.multiple_of(step * block, block)
    window = hist_ref[pl.ds(start, width), :]
    kinds = class_ref[...]
    total = jnp.zeros((block, window.shape[1]), jnp.float32)
    for kind in range(high_ref.shape[0]):
        part = jnp.dot(high_ref[kind], window, preferred_element_type=jnp.float32)
        part = part + jnp.dot(low_ref[kind], window, preferred_element_type=jnp.float32)
        total = jnp.where(kinds == kind, part, total)
    contracted = total.astype(jnp.bfloat16)
    proj_ref[...] = jnp.dot(contracted, rows_ref[...], preferred_element_type=jnp.float32).astype(
        jnp.bfloat16
    )
    flags = flag_ref[...]
    centre_ref[...] = jnp.dot(contracted, near_ref[1], preferred_element_type=jnp.float32)
    lower = jnp.dot(contracted, near_ref[0], preferred_element_type=jnp.float32)
    lower_ref[...] = (lower * flags[0:1, :]).astype(jnp.bfloat16)
    upper = jnp.dot(contracted, near_ref[2], preferred_element_type=jnp.float32)
    upper_ref[...] = (upper * flags[1:2, :]).astype(jnp.bfloat16)


def local_terms(history, lag_class, lag_table, row_bases, near_blocks, near_flags, steps):
    class_total, lags = lag_table.shape
    size = history.shape[1]
    rank = row_bases.shape[1]
    block = 256
    width = block + 128
    blocks = steps // block
    padded = jnp.pad(history, ((0, (blocks - 1) * block + width - history.shape[0]), (0, 0)))
    table = jnp.pad(lag_table, ((0, 0), (0, width - lags)))
    kinds = lag_class.reshape(1, size)
    flags = jnp.broadcast_to(near_flags[0].astype(jnp.float32)[:, None], (2, size))
    whole = lambda shape: pl.BlockSpec(shape, lambda b: (0,) * len(shape))
    rows_of = lambda cols: pl.BlockSpec((block, cols), lambda b: (b, 0))
    return pl.pallas_call(
        local_kernel,
        grid=(blocks,),
        out_shape=(
            jax.ShapeDtypeStruct((steps, rank), jnp.bfloat16),
            jax.ShapeDtypeStruct((steps, size), jnp.float32),
            jax.ShapeDtypeStruct((steps, size), jnp.bfloat16),
            jax.ShapeDtypeStruct((steps, size), jnp.bfloat16),
        ),
        in_specs=[
            whole(padded.shape),
            whole(table.shape),
            whole(kinds.shape),
            whole(row_bases.shape),
            whole(near_blocks.shape[1:]),
            whole(flags.shape),
        ],
        out_specs=(rows_of(rank), rows_of(size), rows_of(size), rows_of(size)),
        scratch_shapes=[
            pltpu.VMEM((class_total, block, width), jnp.bfloat16),
            pltpu.VMEM((class_total, block, width), jnp.bfloat16),
        ],
        compiler_params=pltpu.CompilerParams(dimension_semantics=("arbitrary",)),
    )(padded, table, kinds, row_bases, near_blocks[0], flags)


def ring_kernel(z_count, data_ref, out_ref, recv, send, send_sem, recv_sem):
    row = lax.axis_index("row")
    col = lax.axis_index("col")
    core = row % 2
    zpos = (row // 2) % z_count
    base = row - zpos * 2
    up_dev = base + ((zpos + 1) % z_count) * 2
    down_dev = base + ((zpos + z_count - 1) % z_count) * 2
    half = data_ref.shape[3] // 2
    mesh_kind = pl.DeviceIdType.MESH

    barrier = pltpu.get_barrier_semaphore()
    for neighbour in (up_dev, down_dev):
        pl.semaphore_signal(barrier, inc=1, device_id=(neighbour, col), device_id_type=mesh_kind)
    pl.semaphore_wait(barrier, 2)

    rings = (
        (0, up_dev, lambda s: (zpos + (z_count - 1) * (s + 1)) % z_count, 0),
        (1, down_dev, lambda s: (zpos + s + 1) % z_count, half),
    )
    last = z_count - 1
    copies = {}
    for step in range(last):
        for way, target, index, low in rings:
            if step == 0:
                source = data_ref.at[index(step), :, :, pl.ds(low, half)]
            else:
                copies[(way, step - 1)].wait_recv()
                own = data_ref[index(step), :, :, pl.ds(low, half)].astype(jnp.float32)
                send[way, step] = (recv[way, step - 1].astype(jnp.float32) + own).astype(jnp.bfloat16)
                source = send.at[way, step]
            copy = pltpu.make_async_remote_copy(
                src_ref=source,
                dst_ref=recv.at[way, step],
                send_sem=send_sem.at[way, step],
                recv_sem=recv_sem.at[way, step],
                device_id=(target, col),
                device_id_type=mesh_kind,
            )
            copy.start()
            copies[(way, step)] = copy
    for way, target, index, low in rings:
        copies[(way, last - 1)].wait_recv()
        own = data_ref[zpos, :, :, pl.ds(low, half)].astype(jnp.float32)
        out_ref[:, :, pl.ds(low, half)] = recv[way, last - 1].astype(jnp.float32) + own
    for copy in copies.values():
        copy.wait_send()


def z_ring(data, z_count):
    _, pairs, width, steps = data.shape
    half = steps // 2
    return pl.pallas_call(
        functools.partial(ring_kernel, z_count),
        out_shape=jax.ShapeDtypeStruct((pairs, width, steps), jnp.float32),
        in_specs=[pl.BlockSpec(memory_space=pltpu.VMEM)],
        out_specs=pl.BlockSpec(memory_space=pltpu.VMEM),
        scratch_shapes=[
            pltpu.VMEM((2, z_count - 1, pairs, width, half), jnp.bfloat16),
            pltpu.VMEM((2, z_count - 1, pairs, width, half), jnp.bfloat16),
            pltpu.SemaphoreType.DMA((2, z_count - 1)),
            pltpu.SemaphoreType.DMA((2, z_count - 1)),
        ],
        compiler_params=pltpu.CompilerParams(collective_id=0, has_side_effects=True),
    )(data)


def row_reduce(keep, give, row_count):
    r = lax.axis_index("row")
    z_count = row_count // 4
    yh = r // (2 * z_count)
    core_pairs = [(s, s ^ 1) for s in range(row_count)]
    got = lax.ppermute(give, "row", core_pairs)
    summed = (keep.astype(jnp.float32) + got.astype(jnp.float32)).astype(jnp.bfloat16)
    mine = z_ring(summed, z_count)
    keep_y = lax.dynamic_index_in_dim(mine, yh, axis=0, keepdims=False)
    give_y = lax.dynamic_index_in_dim(mine, 1 - yh, axis=0, keepdims=False)
    y_pairs = [(s, s ^ (2 * z_count)) for s in range(row_count)]
    got_y = lax.ppermute(give_y.astype(jnp.bfloat16), "row", y_pairs)
    return keep_y + got_y.astype(jnp.float32)


def local(
    history,
    lag_class,
    lag_table,
    row_bases,
    coupling,
    block_ranks,
    col_bases,
    near_blocks,
    near_flags,
):
    row_count = lax.axis_size("row")
    col_count = lax.axis_size("col")
    cluster_total = row_count * col_count
    row_index = lax.axis_index("row")
    col_index = lax.axis_index("col")
    rank_cap = row_bases.shape[1]
    steps = history.shape[0] - lag_table.shape[1] + 1
    projected, centre, lower_terms, upper_terms = local_terms(
        history, lag_class, lag_table, row_bases, near_blocks, near_flags, steps
    )
    flag_block = jnp.zeros((16, rank_cap), jnp.bfloat16).at[0, 0:2].set(
        near_flags[0].astype(jnp.bfloat16)
    )
    extended = jnp.concatenate([projected, flag_block], axis=0)
    gathered = lax.all_gather(extended, "col", axis=0, tiled=False)
    source_proj = gathered[:, :steps]
    flag_rows = gathered[:, steps, 0:2]

    flat_next = [(s, (s + 1) % cluster_total) for s in range(cluster_total)]
    flat_prev = [(s, (s - 1) % cluster_total) for s in range(cluster_total)]
    from_left = lax.ppermute(upper_terms, ("row", "col"), flat_next)
    from_right = lax.ppermute(lower_terms, ("row", "col"), flat_prev)

    source_local = jnp.arange(col_count, dtype=jnp.int32)[:, None]
    target_row = jnp.arange(row_count, dtype=jnp.int32)[None, :]
    offset = jnp.remainder(
        (target_row - row_index) * col_count + col_index - source_local, cluster_total
    )
    levels = jnp.arange(rank_cap, dtype=jnp.int32)
    live_rank = levels[None, None, :] < block_ranks[:, :, 0][:, :, None]
    live_pairs = (
        (offset != 0)[:, :, None, None] & live_rank[:, :, :, None] & live_rank[:, :, None, :]
    )
    masked = jnp.where(live_pairs, coupling[:, :, 0], jnp.zeros((), jnp.bfloat16))
    for way, lane in ((1, 1), (-1, 0)):
        source = jnp.remainder(col_index - way, col_count)
        target = jnp.remainder(row_index + (way - col_index + source) // col_count, row_count)
        corner = (source, target, 0, 0)
        piece = lax.dynamic_slice(masked, corner, (1, 1, rank_cap, rank_cap))
        far = lax.dynamic_index_in_dim(flag_rows, source, axis=0, keepdims=False)[lane] < 0.5
        piece = jnp.where(far, piece, jnp.zeros((), jnp.bfloat16))
        masked = lax.dynamic_update_slice(masked, piece, corner)
    z_count = row_count // 4
    masked = masked.reshape(col_count, 2, z_count, 2, rank_cap, rank_cap)
    core = row_index % 2
    halves = []
    for pick in (core, 1 - core):
        chosen = lax.dynamic_index_in_dim(masked, pick, axis=3, keepdims=False)
        halves.append(
            jnp.einsum(
                "sta,syzab->zybt", source_proj, chosen, preferred_element_type=jnp.float32
            ).astype(jnp.bfloat16)
        )
    coeffs = row_reduce(halves[0], halves[1], row_count).astype(jnp.bfloat16)
    far_part = jnp.einsum("bt,eb->te", coeffs, col_bases, preferred_element_type=jnp.float32)
    return far_part + centre + from_left.astype(jnp.float32) + from_right.astype(jnp.float32)


def solution(mesh):
    return jax.shard_map(
        local,
        mesh=mesh,
        in_specs=(
            P(None, ("row", "col")),
            P(("row", "col")),
            P(),
            P(("row", "col"), None),
            P("row", None, "col", None, None),
            P("row", None, "col"),
            P(("row", "col"), None),
            P(("row", "col"), None, None, None),
            P(("row", "col"), None),
        ),
        out_specs=P(None, ("row", "col")),
        check_vma=False,
    )
```

```python
import functools

import jax
import jax.numpy as jnp
from jax import lax
from jax.experimental import pallas as pl
from jax.experimental.pallas import tpu as pltpu
from jax.sharding import PartitionSpec as P


def local_kernel(
    hist_ref, table_ref, class_ref, rows_ref, near_ref, flag_ref,
    proj_ref, centre_ref, lower_ref, upper_ref, high_ref, low_ref,
):
    block, width = high_ref.shape[1], high_ref.shape[2]
    step = pl.program_id(0)

    @pl.when(step == 0)
    def _():
        table = table_ref[...]
        for kind in range(high_ref.shape[0]):
            row = jnp.broadcast_to(table[kind : kind + 1, :], (block, width))
            full = pltpu.roll(row, 0, 1, stride=1, stride_axis=0)
            high = full.astype(jnp.bfloat16)
            high_ref[kind] = high
            low_ref[kind] = (full - high.astype(jnp.float32)).astype(jnp.bfloat16)

    start = pl.multiple_of(step * block, block)
    window = hist_ref[pl.ds(start, width), :]
    kinds = class_ref[...]
    total = jnp.zeros((block, window.shape[1]), jnp.float32)
    for kind in range(high_ref.shape[0]):
        part = jnp.dot(high_ref[kind], window, preferred_element_type=jnp.float32)
        part = part + jnp.dot(low_ref[kind], window, preferred_element_type=jnp.float32)
        total = jnp.where(kinds == kind, part, total)
    contracted = total.astype(jnp.bfloat16)
    proj_ref[...] = jnp.dot(contracted, rows_ref[...], preferred_element_type=jnp.float32).astype(
        jnp.bfloat16
    )
    flags = flag_ref[...]
    centre_ref[...] = jnp.dot(contracted, near_ref[1], preferred_element_type=jnp.float32)
    lower = jnp.dot(contracted, near_ref[0], preferred_element_type=jnp.float32)
    lower_ref[...] = (lower * flags[0:1, :]).astype(jnp.bfloat16)
    upper = jnp.dot(contracted, near_ref[2], preferred_element_type=jnp.float32)
    upper_ref[...] = (upper * flags[1:2, :]).astype(jnp.bfloat16)


def local_terms(history, lag_class, lag_table, row_bases, near_blocks, near_flags, steps):
    class_total, lags = lag_table.shape
    size = history.shape[1]
    rank = row_bases.shape[1]
    block = 256
    width = block + 128
    blocks = steps // block
    padded = jnp.pad(history, ((0, (blocks - 1) * block + width - history.shape[0]), (0, 0)))
    table = jnp.pad(lag_table, ((0, 0), (0, width - lags)))
    kinds = lag_class.reshape(1, size)
    flags = jnp.broadcast_to(near_flags[0].astype(jnp.float32)[:, None], (2, size))
    whole = lambda shape: pl.BlockSpec(shape, lambda b: (0,) * len(shape))
    rows_of = lambda cols: pl.BlockSpec((block, cols), lambda b: (b, 0))
    return pl.pallas_call(
        local_kernel,
        grid=(blocks,),
        out_shape=(
            jax.ShapeDtypeStruct((steps, rank), jnp.bfloat16),
            jax.ShapeDtypeStruct((steps, size), jnp.float32),
            jax.ShapeDtypeStruct((steps, size), jnp.bfloat16),
            jax.ShapeDtypeStruct((steps, size), jnp.bfloat16),
        ),
        in_specs=[
            whole(padded.shape),
            whole(table.shape),
            whole(kinds.shape),
            whole(row_bases.shape),
            whole(near_blocks.shape[1:]),
            whole(flags.shape),
        ],
        out_specs=(rows_of(rank), rows_of(size), rows_of(size), rows_of(size)),
        scratch_shapes=[
            pltpu.VMEM((class_total, block, width), jnp.bfloat16),
            pltpu.VMEM((class_total, block, width), jnp.bfloat16),
        ],
        compiler_params=pltpu.CompilerParams(dimension_semantics=("arbitrary",)),
    )(padded, table, kinds, row_bases, near_blocks[0], flags)


def ring_kernel(
    z_count, keep_ref, give_ref, out_ref, mate, recv, send, mate_send, mate_recv, send_sem, recv_sem
):
    row = lax.axis_index("row")
    col = lax.axis_index("col")
    zpos = (row // 2) % z_count
    base = row - zpos * 2
    up_dev = base + ((zpos + 1) % z_count) * 2
    down_dev = base + ((zpos + z_count - 1) % z_count) * 2
    mate_dev = row + 1 - 2 * (row % 2)
    half = keep_ref.shape[3] // 2
    mesh_kind = pl.DeviceIdType.MESH

    barrier = pltpu.get_barrier_semaphore()
    for neighbour in (up_dev, down_dev, mate_dev):
        pl.semaphore_signal(barrier, inc=1, device_id=(neighbour, col), device_id_type=mesh_kind)
    pl.semaphore_wait(barrier, 3)

    order = []
    for distance in range(1, z_count // 2 + 1):
        for shift in (-distance, distance):
            if shift % z_count not in order:
                order.append(shift % z_count)
    order.append(0)
    mate_copies = {}
    for slot, shift in enumerate(order):
        index = (zpos + shift) % z_count
        copy = pltpu.make_async_remote_copy(
            src_ref=give_ref.at[index],
            dst_ref=mate.at[index],
            send_sem=mate_send.at[slot],
            recv_sem=mate_recv.at[slot],
            device_id=(mate_dev, col),
            device_id_type=mesh_kind,
        )
        copy.start()
        mate_copies[shift] = copy
    arrived = set()

    def own(shift, low):
        if shift not in arrived:
            mate_copies[shift].wait_recv()
            arrived.add(shift)
        index = (zpos + shift) % z_count
        mine = keep_ref[index, :, :, pl.ds(low, half)].astype(jnp.float32)
        return mine + mate[index, :, :, pl.ds(low, half)].astype(jnp.float32)

    rings = ((0, up_dev, -1, 0), (1, down_dev, 1, half))
    last = z_count - 1
    copies = {}
    for step in range(last):
        for way, target, sign, low in rings:
            shift = (sign * (step + 1)) % z_count
            total = own(shift, low)
            if step > 0:
                copies[(way, step - 1)].wait_recv()
                total = total + recv[way, step - 1].astype(jnp.float32)
            send[way, step] = total.astype(jnp.bfloat16)
            copy = pltpu.make_async_remote_copy(
                src_ref=send.at[way, step],
                dst_ref=recv.at[way, step],
                send_sem=send_sem.at[way, step],
                recv_sem=recv_sem.at[way, step],
                device_id=(target, col),
                device_id_type=mesh_kind,
            )
            copy.start()
            copies[(way, step)] = copy
    for way, target, sign, low in rings:
        copies[(way, last - 1)].wait_recv()
        out_ref[:, :, pl.ds(low, half)] = recv[way, last - 1].astype(jnp.float32) + own(0, low)
    for copy in copies.values():
        copy.wait_send()
    for copy in mate_copies.values():
        copy.wait_send()


def z_ring(keep, give, z_count):
    _, pairs, width, steps = keep.shape
    half = steps // 2
    return pl.pallas_call(
        functools.partial(ring_kernel, z_count),
        out_shape=jax.ShapeDtypeStruct((pairs, width, steps), jnp.float32),
        in_specs=[pl.BlockSpec(memory_space=pltpu.VMEM)] * 2,
        out_specs=pl.BlockSpec(memory_space=pltpu.VMEM),
        scratch_shapes=[
            pltpu.VMEM(keep.shape, jnp.bfloat16),
            pltpu.VMEM((2, z_count - 1, pairs, width, half), jnp.bfloat16),
            pltpu.VMEM((2, z_count - 1, pairs, width, half), jnp.bfloat16),
            pltpu.SemaphoreType.DMA((z_count,)),
            pltpu.SemaphoreType.DMA((z_count,)),
            pltpu.SemaphoreType.DMA((2, z_count - 1)),
            pltpu.SemaphoreType.DMA((2, z_count - 1)),
        ],
        compiler_params=pltpu.CompilerParams(collective_id=0, has_side_effects=True),
    )(keep, give)


def row_reduce(keep, give, row_count):
    r = lax.axis_index("row")
    z_count = row_count // 4
    yh = r // (2 * z_count)
    mine = z_ring(keep, give, z_count)
    keep_y = lax.dynamic_index_in_dim(mine, yh, axis=0, keepdims=False)
    give_y = lax.dynamic_index_in_dim(mine, 1 - yh, axis=0, keepdims=False)
    y_pairs = [(s, s ^ (2 * z_count)) for s in range(row_count)]
    got_y = lax.ppermute(give_y.astype(jnp.bfloat16), "row", y_pairs)
    return keep_y + got_y.astype(jnp.float32)


def local(
    history,
    lag_class,
    lag_table,
    row_bases,
    coupling,
    block_ranks,
    col_bases,
    near_blocks,
    near_flags,
):
    row_count = lax.axis_size("row")
    col_count = lax.axis_size("col")
    cluster_total = row_count * col_count
    row_index = lax.axis_index("row")
    col_index = lax.axis_index("col")
    rank_cap = row_bases.shape[1]
    steps = history.shape[0] - lag_table.shape[1] + 1
    projected, centre, lower_terms, upper_terms = local_terms(
        history, lag_class, lag_table, row_bases, near_blocks, near_flags, steps
    )
    flag_block = jnp.zeros((16, rank_cap), jnp.bfloat16).at[0, 0:2].set(
        near_flags[0].astype(jnp.bfloat16)
    )
    extended = jnp.concatenate([projected, flag_block], axis=0)
    gathered = lax.all_gather(extended, "col", axis=0, tiled=False)
    source_proj = gathered[:, :steps]
    flag_rows = gathered[:, steps, 0:2]

    flat_next = [(s, (s + 1) % cluster_total) for s in range(cluster_total)]
    flat_prev = [(s, (s - 1) % cluster_total) for s in range(cluster_total)]
    from_left = lax.ppermute(upper_terms, ("row", "col"), flat_next)
    from_right = lax.ppermute(lower_terms, ("row", "col"), flat_prev)

    source_local = jnp.arange(col_count, dtype=jnp.int32)[:, None]
    target_row = jnp.arange(row_count, dtype=jnp.int32)[None, :]
    offset = jnp.remainder(
        (target_row - row_index) * col_count + col_index - source_local, cluster_total
    )
    levels = jnp.arange(rank_cap, dtype=jnp.int32)
    live_rank = levels[None, None, :] < block_ranks[:, :, 0][:, :, None]
    live_pairs = (
        (offset != 0)[:, :, None, None] & live_rank[:, :, :, None] & live_rank[:, :, None, :]
    )
    masked = jnp.where(live_pairs, coupling[:, :, 0], jnp.zeros((), jnp.bfloat16))
    for way, lane in ((1, 1), (-1, 0)):
        source = jnp.remainder(col_index - way, col_count)
        target = jnp.remainder(row_index + (way - col_index + source) // col_count, row_count)
        corner = (source, target, 0, 0)
        piece = lax.dynamic_slice(masked, corner, (1, 1, rank_cap, rank_cap))
        far = lax.dynamic_index_in_dim(flag_rows, source, axis=0, keepdims=False)[lane] < 0.5
        piece = jnp.where(far, piece, jnp.zeros((), jnp.bfloat16))
        masked = lax.dynamic_update_slice(masked, piece, corner)
    z_count = row_count // 4
    masked = masked.reshape(col_count, 2, z_count, 2, rank_cap, rank_cap)
    core = row_index % 2
    halves = []
    for pick in (core, 1 - core):
        chosen = lax.dynamic_index_in_dim(masked, pick, axis=3, keepdims=False)
        halves.append(
            jnp.einsum(
                "sta,syzab->zybt", source_proj, chosen, preferred_element_type=jnp.float32
            ).astype(jnp.bfloat16)
        )
    coeffs = row_reduce(halves[0], halves[1], row_count).astype(jnp.bfloat16)
    far_part = jnp.einsum("bt,eb->te", coeffs, col_bases, preferred_element_type=jnp.float32)
    return far_part + centre + from_left.astype(jnp.float32) + from_right.astype(jnp.float32)


def solution(mesh):
    return jax.shard_map(
        local,
        mesh=mesh,
        in_specs=(
            P(None, ("row", "col")),
            P(("row", "col")),
            P(),
            P(("row", "col"), None),
            P("row", None, "col", None, None),
            P("row", None, "col"),
            P(("row", "col"), None),
            P(("row", "col"), None, None, None),
            P(("row", "col"), None),
        ),
        out_specs=P(None, ("row", "col")),
        check_vma=False,
    )
```

```python
import functools

import jax
import jax.numpy as jnp
from jax import lax
from jax.experimental import pallas as pl
from jax.experimental.pallas import tpu as pltpu
from jax.sharding import PartitionSpec as P


def local_kernel(
    hist_ref, table_ref, class_ref, rows_ref, near_ref, flag_ref,
    proj_ref, centre_ref, lower_ref, upper_ref, high_ref, low_ref,
):
    block, width = high_ref.shape[1], high_ref.shape[2]
    step = pl.program_id(0)

    @pl.when(step == 0)
    def _():
        table = table_ref[...]
        for kind in range(high_ref.shape[0]):
            row = jnp.broadcast_to(table[kind : kind + 1, :], (block, width))
            full = pltpu.roll(row, 0, 1, stride=1, stride_axis=0)
            high = full.astype(jnp.bfloat16)
            high_ref[kind] = high
            low_ref[kind] = (full - high.astype(jnp.float32)).astype(jnp.bfloat16)

    start = pl.multiple_of(step * block, block)
    window = hist_ref[pl.ds(start, width), :]
    kinds = class_ref[...]
    total = jnp.zeros((block, window.shape[1]), jnp.float32)
    for kind in range(high_ref.shape[0]):
        part = jnp.dot(high_ref[kind], window, preferred_element_type=jnp.float32)
        part = part + jnp.dot(low_ref[kind], window, preferred_element_type=jnp.float32)
        total = jnp.where(kinds == kind, part, total)
    contracted = total.astype(jnp.bfloat16)
    proj_ref[...] = jnp.dot(contracted, rows_ref[...], preferred_element_type=jnp.float32).astype(
        jnp.bfloat16
    )
    flags = flag_ref[...]
    centre_ref[...] = jnp.dot(contracted, near_ref[1], preferred_element_type=jnp.float32)
    lower = jnp.dot(contracted, near_ref[0], preferred_element_type=jnp.float32)
    lower_ref[...] = (lower * flags[0:1, :]).astype(jnp.bfloat16)
    upper = jnp.dot(contracted, near_ref[2], preferred_element_type=jnp.float32)
    upper_ref[...] = (upper * flags[1:2, :]).astype(jnp.bfloat16)


def local_terms(history, lag_class, lag_table, row_bases, near_blocks, near_flags, steps):
    class_total, lags = lag_table.shape
    size = history.shape[1]
    rank = row_bases.shape[1]
    block = 256
    width = block + 128
    blocks = steps // block
    padded = jnp.pad(history, ((0, (blocks - 1) * block + width - history.shape[0]), (0, 0)))
    table = jnp.pad(lag_table, ((0, 0), (0, width - lags)))
    kinds = lag_class.reshape(1, size)
    flags = jnp.broadcast_to(near_flags[0].astype(jnp.float32)[:, None], (2, size))
    whole = lambda shape: pl.BlockSpec(shape, lambda b: (0,) * len(shape))
    rows_of = lambda cols: pl.BlockSpec((block, cols), lambda b: (b, 0))
    return pl.pallas_call(
        local_kernel,
        grid=(blocks,),
        out_shape=(
            jax.ShapeDtypeStruct((steps, rank), jnp.bfloat16),
            jax.ShapeDtypeStruct((steps, size), jnp.float32),
            jax.ShapeDtypeStruct((steps, size), jnp.bfloat16),
            jax.ShapeDtypeStruct((steps, size), jnp.bfloat16),
        ),
        in_specs=[
            whole(padded.shape),
            whole(table.shape),
            whole(kinds.shape),
            whole(row_bases.shape),
            whole(near_blocks.shape[1:]),
            whole(flags.shape),
        ],
        out_specs=(rows_of(rank), rows_of(size), rows_of(size), rows_of(size)),
        scratch_shapes=[
            pltpu.VMEM((class_total, block, width), jnp.bfloat16),
            pltpu.VMEM((class_total, block, width), jnp.bfloat16),
        ],
        compiler_params=pltpu.CompilerParams(dimension_semantics=("arbitrary",)),
    )(padded, table, kinds, row_bases, near_blocks[0], flags)


def ring_kernel(
    z_count, keep_ref, give_ref, upper_ref, lower_ref, out_ref, left_ref, right_ref,
    mate, recv, send, mate_send, mate_recv, send_sem, recv_sem, sides, side_send, side_recv,
):
    row = lax.axis_index("row")
    col = lax.axis_index("col")
    zpos = (row // 2) % z_count
    base = row - zpos * 2
    up_dev = base + ((zpos + 1) % z_count) * 2
    down_dev = base + ((zpos + z_count - 1) % z_count) * 2
    mate_dev = row + 1 - 2 * (row % 2)
    rows = lax.axis_size("row")
    cols = lax.axis_size("col")
    next_row = (row + (col + 1) // cols) % rows
    next_col = (col + 1) % cols
    prev_row = (row + rows - 1 + (col + cols - 1) // cols) % rows
    prev_col = (col + cols - 1) % cols
    half = keep_ref.shape[3] // 2
    mesh_kind = pl.DeviceIdType.MESH

    barrier = pltpu.get_barrier_semaphore()
    for neighbour in ((up_dev, col), (down_dev, col), (mate_dev, col), (next_row, next_col), (prev_row, prev_col)):
        pl.semaphore_signal(barrier, inc=1, device_id=neighbour, device_id_type=mesh_kind)
    pl.semaphore_wait(barrier, 5)

    side_copies = []
    for slot, (source, target) in enumerate(
        ((upper_ref, (next_row, next_col)), (lower_ref, (prev_row, prev_col)))
    ):
        copy = pltpu.make_async_remote_copy(
            src_ref=source,
            dst_ref=sides.at[slot],
            send_sem=side_send.at[slot],
            recv_sem=side_recv.at[slot],
            device_id=target,
            device_id_type=mesh_kind,
        )
        copy.start()
        side_copies.append(copy)

    order = []
    for distance in range(1, z_count // 2 + 1):
        for shift in (-distance, distance):
            if shift % z_count not in order:
                order.append(shift % z_count)
    order.append(0)
    mate_copies = {}
    for slot, shift in enumerate(order):
        index = (zpos + shift) % z_count
        copy = pltpu.make_async_remote_copy(
            src_ref=give_ref.at[index],
            dst_ref=mate.at[index],
            send_sem=mate_send.at[slot],
            recv_sem=mate_recv.at[slot],
            device_id=(mate_dev, col),
            device_id_type=mesh_kind,
        )
        copy.start()
        mate_copies[shift] = copy
    arrived = set()

    def own(shift, low):
        if shift not in arrived:
            mate_copies[shift].wait_recv()
            arrived.add(shift)
        index = (zpos + shift) % z_count
        mine = keep_ref[index, :, :, pl.ds(low, half)].astype(jnp.float32)
        return mine + mate[index, :, :, pl.ds(low, half)].astype(jnp.float32)

    rings = ((0, up_dev, -1, 0), (1, down_dev, 1, half))
    last = z_count - 1
    copies = {}
    for step in range(last):
        for way, target, sign, low in rings:
            shift = (sign * (step + 1)) % z_count
            total = own(shift, low)
            if step > 0:
                copies[(way, step - 1)].wait_recv()
                total = total + recv[way, step - 1].astype(jnp.float32)
            send[way, step] = total.astype(jnp.bfloat16)
            copy = pltpu.make_async_remote_copy(
                src_ref=send.at[way, step],
                dst_ref=recv.at[way, step],
                send_sem=send_sem.at[way, step],
                recv_sem=recv_sem.at[way, step],
                device_id=(target, col),
                device_id_type=mesh_kind,
            )
            copy.start()
            copies[(way, step)] = copy
    for way, target, sign, low in rings:
        copies[(way, last - 1)].wait_recv()
        out_ref[:, :, pl.ds(low, half)] = recv[way, last - 1].astype(jnp.float32) + own(0, low)
    for copy, target in zip(side_copies, (left_ref, right_ref)):
        copy.wait_recv()
    left_ref[...] = sides[0]
    right_ref[...] = sides[1]
    for copy in copies.values():
        copy.wait_send()
    for copy in mate_copies.values():
        copy.wait_send()
    for copy in side_copies:
        copy.wait_send()


def z_ring(keep, give, upper, lower, z_count):
    _, pairs, width, steps = keep.shape
    half = steps // 2
    return pl.pallas_call(
        functools.partial(ring_kernel, z_count),
        out_shape=(
            jax.ShapeDtypeStruct((pairs, width, steps), jnp.float32),
            jax.ShapeDtypeStruct(upper.shape, upper.dtype),
            jax.ShapeDtypeStruct(lower.shape, lower.dtype),
        ),
        in_specs=[pl.BlockSpec(memory_space=pltpu.VMEM)] * 4,
        out_specs=(pl.BlockSpec(memory_space=pltpu.VMEM),) * 3,
        scratch_shapes=[
            pltpu.VMEM(keep.shape, jnp.bfloat16),
            pltpu.VMEM((2, z_count - 1, pairs, width, half), jnp.bfloat16),
            pltpu.VMEM((2, z_count - 1, pairs, width, half), jnp.bfloat16),
            pltpu.SemaphoreType.DMA((z_count,)),
            pltpu.SemaphoreType.DMA((z_count,)),
            pltpu.SemaphoreType.DMA((2, z_count - 1)),
            pltpu.SemaphoreType.DMA((2, z_count - 1)),
            pltpu.VMEM((2,) + upper.shape, upper.dtype),
            pltpu.SemaphoreType.DMA((2,)),
            pltpu.SemaphoreType.DMA((2,)),
        ],
        compiler_params=pltpu.CompilerParams(collective_id=0, has_side_effects=True),
    )(keep, give, upper, lower)


def row_reduce(keep, give, upper, lower, row_count):
    r = lax.axis_index("row")
    z_count = row_count // 4
    yh = r // (2 * z_count)
    mine, from_left, from_right = z_ring(keep, give, upper, lower, z_count)
    keep_y = lax.dynamic_index_in_dim(mine, yh, axis=0, keepdims=False)
    give_y = lax.dynamic_index_in_dim(mine, 1 - yh, axis=0, keepdims=False)
    y_pairs = [(s, s ^ (2 * z_count)) for s in range(row_count)]
    got_y = lax.ppermute(give_y.astype(jnp.bfloat16), "row", y_pairs)
    return keep_y + got_y.astype(jnp.float32), from_left, from_right


def local(
    history,
    lag_class,
    lag_table,
    row_bases,
    coupling,
    block_ranks,
    col_bases,
    near_blocks,
    near_flags,
):
    row_count = lax.axis_size("row")
    col_count = lax.axis_size("col")
    cluster_total = row_count * col_count
    row_index = lax.axis_index("row")
    col_index = lax.axis_index("col")
    rank_cap = row_bases.shape[1]
    steps = history.shape[0] - lag_table.shape[1] + 1
    projected, centre, lower_terms, upper_terms = local_terms(
        history, lag_class, lag_table, row_bases, near_blocks, near_flags, steps
    )
    flag_block = jnp.zeros((16, rank_cap), jnp.bfloat16).at[0, 0:2].set(
        near_flags[0].astype(jnp.bfloat16)
    )
    extended = jnp.concatenate([projected, flag_block], axis=0)
    gathered = lax.all_gather(extended, "col", axis=0, tiled=False)
    source_proj = gathered[:, :steps]
    flag_rows = gathered[:, steps, 0:2]


    source_local = jnp.arange(col_count, dtype=jnp.int32)[:, None]
    target_row = jnp.arange(row_count, dtype=jnp.int32)[None, :]
    offset = jnp.remainder(
        (target_row - row_index) * col_count + col_index - source_local, cluster_total
    )
    levels = jnp.arange(rank_cap, dtype=jnp.int32)
    live_rank = levels[None, None, :] < block_ranks[:, :, 0][:, :, None]
    live_pairs = (
        (offset != 0)[:, :, None, None] & live_rank[:, :, :, None] & live_rank[:, :, None, :]
    )
    masked = jnp.where(live_pairs, coupling[:, :, 0], jnp.zeros((), jnp.bfloat16))
    for way, lane in ((1, 1), (-1, 0)):
        source = jnp.remainder(col_index - way, col_count)
        target = jnp.remainder(row_index + (way - col_index + source) // col_count, row_count)
        corner = (source, target, 0, 0)
        piece = lax.dynamic_slice(masked, corner, (1, 1, rank_cap, rank_cap))
        far = lax.dynamic_index_in_dim(flag_rows, source, axis=0, keepdims=False)[lane] < 0.5
        piece = jnp.where(far, piece, jnp.zeros((), jnp.bfloat16))
        masked = lax.dynamic_update_slice(masked, piece, corner)
    z_count = row_count // 4
    masked = masked.reshape(col_count, 2, z_count, 2, rank_cap, rank_cap)
    core = row_index % 2
    halves = []
    for pick in (core, 1 - core):
        chosen = lax.dynamic_index_in_dim(masked, pick, axis=3, keepdims=False)
        halves.append(
            jnp.einsum(
                "sta,syzab->zybt", source_proj, chosen, preferred_element_type=jnp.float32
            ).astype(jnp.bfloat16)
        )
    coeffs, from_left, from_right = row_reduce(
        halves[0], halves[1], upper_terms, lower_terms, row_count
    )
    coeffs = coeffs.astype(jnp.bfloat16)
    far_part = jnp.einsum("bt,eb->te", coeffs, col_bases, preferred_element_type=jnp.float32)
    return far_part + centre + from_left.astype(jnp.float32) + from_right.astype(jnp.float32)


def solution(mesh):
    return jax.shard_map(
        local,
        mesh=mesh,
        in_specs=(
            P(None, ("row", "col")),
            P(("row", "col")),
            P(),
            P(("row", "col"), None),
            P("row", None, "col", None, None),
            P("row", None, "col"),
            P(("row", "col"), None),
            P(("row", "col"), None, None, None),
            P(("row", "col"), None),
        ),
        out_specs=P(None, ("row", "col")),
        check_vma=False,
    )
```

```python
import functools

import jax
import jax.numpy as jnp
from jax import lax
from jax.experimental import pallas as pl
from jax.experimental.pallas import tpu as pltpu
from jax.sharding import PartitionSpec as P


def local_kernel(
    hist_ref, table_ref, class_ref, rows_ref, near_ref, flag_ref,
    proj_ref, centre_ref, lower_ref, upper_ref, high_ref, low_ref,
):
    block, width = high_ref.shape[1], high_ref.shape[2]
    step = pl.program_id(0)

    @pl.when(step == 0)
    def _():
        table = table_ref[...]
        for kind in range(high_ref.shape[0]):
            row = jnp.broadcast_to(table[kind : kind + 1, :], (block, width))
            full = pltpu.roll(row, 0, 1, stride=1, stride_axis=0)
            high = full.astype(jnp.bfloat16)
            high_ref[kind] = high
            low_ref[kind] = (full - high.astype(jnp.float32)).astype(jnp.bfloat16)

    start = pl.multiple_of(step * block, block)
    window = hist_ref[pl.ds(start, width), :]
    kinds = class_ref[...]
    total = jnp.zeros((block, window.shape[1]), jnp.float32)
    for kind in range(high_ref.shape[0]):
        part = jnp.dot(high_ref[kind], window, preferred_element_type=jnp.float32)
        part = part + jnp.dot(low_ref[kind], window, preferred_element_type=jnp.float32)
        total = jnp.where(kinds == kind, part, total)
    contracted = total.astype(jnp.bfloat16)
    proj_ref[...] = jnp.dot(contracted, rows_ref[...], preferred_element_type=jnp.float32).astype(
        jnp.bfloat16
    )
    flags = flag_ref[...]
    centre_ref[...] = jnp.dot(contracted, near_ref[1], preferred_element_type=jnp.float32)
    lower = jnp.dot(contracted, near_ref[0], preferred_element_type=jnp.float32)
    lower_ref[...] = (lower * flags[0:1, :]).astype(jnp.bfloat16)
    upper = jnp.dot(contracted, near_ref[2], preferred_element_type=jnp.float32)
    upper_ref[...] = (upper * flags[1:2, :]).astype(jnp.bfloat16)


def local_terms(history, lag_class, lag_table, row_bases, near_blocks, near_flags, steps):
    class_total, lags = lag_table.shape
    size = history.shape[1]
    rank = row_bases.shape[1]
    block = 256
    width = block + 128
    blocks = steps // block
    padded = jnp.pad(history, ((0, (blocks - 1) * block + width - history.shape[0]), (0, 0)))
    table = jnp.pad(lag_table, ((0, 0), (0, width - lags)))
    kinds = lag_class.reshape(1, size)
    flags = jnp.broadcast_to(near_flags[0].astype(jnp.float32)[:, None], (2, size))
    whole = lambda shape: pl.BlockSpec(shape, lambda b: (0,) * len(shape))
    rows_of = lambda cols: pl.BlockSpec((block, cols), lambda b: (b, 0))
    return pl.pallas_call(
        local_kernel,
        grid=(blocks,),
        out_shape=(
            jax.ShapeDtypeStruct((steps, rank), jnp.bfloat16),
            jax.ShapeDtypeStruct((steps, size), jnp.float32),
            jax.ShapeDtypeStruct((steps, size), jnp.bfloat16),
            jax.ShapeDtypeStruct((steps, size), jnp.bfloat16),
        ),
        in_specs=[
            whole(padded.shape),
            whole(table.shape),
            whole(kinds.shape),
            whole(row_bases.shape),
            whole(near_blocks.shape[1:]),
            whole(flags.shape),
        ],
        out_specs=(rows_of(rank), rows_of(size), rows_of(size), rows_of(size)),
        scratch_shapes=[
            pltpu.VMEM((class_total, block, width), jnp.bfloat16),
            pltpu.VMEM((class_total, block, width), jnp.bfloat16),
        ],
        compiler_params=pltpu.CompilerParams(dimension_semantics=("arbitrary",)),
    )(padded, table, kinds, row_bases, near_blocks[0], flags)


def ring_kernel(z_count, data_ref, out_ref, recv, send, send_sem, recv_sem, pair, far, far_send, far_recv):
    row = lax.axis_index("row")
    col = lax.axis_index("col")
    core = row % 2
    zpos = (row // 2) % z_count
    base = row - zpos * 2
    up_dev = base + ((zpos + 1) % z_count) * 2
    down_dev = base + ((zpos + z_count - 1) % z_count) * 2
    half = data_ref.shape[3] // 2
    mesh_kind = pl.DeviceIdType.MESH

    barrier = pltpu.get_barrier_semaphore()
    for neighbour in (up_dev, down_dev):
        pl.semaphore_signal(barrier, inc=1, device_id=(neighbour, col), device_id_type=mesh_kind)
    rows = lax.axis_size("row")
    far_dev = (row + rows // 2) % rows
    pl.semaphore_signal(barrier, inc=1, device_id=(far_dev, col), device_id_type=mesh_kind)
    pl.semaphore_wait(barrier, 3)

    rings = (
        (0, up_dev, lambda s: (zpos + (z_count - 1) * (s + 1)) % z_count, 0),
        (1, down_dev, lambda s: (zpos + s + 1) % z_count, half),
    )
    last = z_count - 1
    copies = {}
    for step in range(last):
        for way, target, index, low in rings:
            if step == 0:
                source = data_ref.at[index(step), :, :, pl.ds(low, half)]
            else:
                copies[(way, step - 1)].wait_recv()
                own = data_ref[index(step), :, :, pl.ds(low, half)].astype(jnp.float32)
                send[way, step] = (recv[way, step - 1].astype(jnp.float32) + own).astype(jnp.bfloat16)
                source = send.at[way, step]
            copy = pltpu.make_async_remote_copy(
                src_ref=source,
                dst_ref=recv.at[way, step],
                send_sem=send_sem.at[way, step],
                recv_sem=recv_sem.at[way, step],
                device_id=(target, col),
                device_id_type=mesh_kind,
            )
            copy.start()
            copies[(way, step)] = copy
    for way, target, index, low in rings:
        copies[(way, last - 1)].wait_recv()
        own = data_ref[zpos, :, :, pl.ds(low, half)].astype(jnp.float32)
        pair[:, :, pl.ds(low, half)] = recv[way, last - 1].astype(jnp.float32) + own
    high = row // (rows // 2)
    far[0] = pair[1 - high].astype(jnp.bfloat16)
    far_copy = pltpu.make_async_remote_copy(
        src_ref=far.at[0],
        dst_ref=far.at[1],
        send_sem=far_send,
        recv_sem=far_recv,
        device_id=(far_dev, col),
        device_id_type=mesh_kind,
    )
    far_copy.start()
    far_copy.wait_recv()
    out_ref[...] = pair[high] + far[1].astype(jnp.float32)
    for copy in copies.values():
        copy.wait_send()
    far_copy.wait_send()


def z_ring(data, z_count):
    _, pairs, width, steps = data.shape
    half = steps // 2
    return pl.pallas_call(
        functools.partial(ring_kernel, z_count),
        out_shape=jax.ShapeDtypeStruct((width, steps), jnp.float32),
        in_specs=[pl.BlockSpec(memory_space=pltpu.VMEM)],
        out_specs=pl.BlockSpec(memory_space=pltpu.VMEM),
        scratch_shapes=[
            pltpu.VMEM((2, z_count - 1, pairs, width, half), jnp.bfloat16),
            pltpu.VMEM((2, z_count - 1, pairs, width, half), jnp.bfloat16),
            pltpu.SemaphoreType.DMA((2, z_count - 1)),
            pltpu.SemaphoreType.DMA((2, z_count - 1)),
            pltpu.VMEM((pairs, width, steps), jnp.float32),
            pltpu.VMEM((2, width, steps), jnp.bfloat16),
            pltpu.SemaphoreType.DMA,
            pltpu.SemaphoreType.DMA,
        ],
        compiler_params=pltpu.CompilerParams(collective_id=0, has_side_effects=True),
    )(data)


def row_reduce(keep, give, row_count):
    z_count = row_count // 4
    core_pairs = [(s, s ^ 1) for s in range(row_count)]
    got = lax.ppermute(give, "row", core_pairs)
    summed = (keep.astype(jnp.float32) + got.astype(jnp.float32)).astype(jnp.bfloat16)
    return z_ring(summed, z_count)


def local(
    history,
    lag_class,
    lag_table,
    row_bases,
    coupling,
    block_ranks,
    col_bases,
    near_blocks,
    near_flags,
):
    row_count = lax.axis_size("row")
    col_count = lax.axis_size("col")
    cluster_total = row_count * col_count
    row_index = lax.axis_index("row")
    col_index = lax.axis_index("col")
    rank_cap = row_bases.shape[1]
    steps = history.shape[0] - lag_table.shape[1] + 1
    projected, centre, lower_terms, upper_terms = local_terms(
        history, lag_class, lag_table, row_bases, near_blocks, near_flags, steps
    )
    flag_block = jnp.zeros((16, rank_cap), jnp.bfloat16).at[0, 0:2].set(
        near_flags[0].astype(jnp.bfloat16)
    )
    extended = jnp.concatenate([projected, flag_block], axis=0)
    gathered = lax.all_gather(extended, "col", axis=0, tiled=False)
    source_proj = gathered[:, :steps]
    flag_rows = gathered[:, steps, 0:2]

    flat_next = [(s, (s + 1) % cluster_total) for s in range(cluster_total)]
    flat_prev = [(s, (s - 1) % cluster_total) for s in range(cluster_total)]
    from_left = lax.ppermute(upper_terms, ("row", "col"), flat_next)
    from_right = lax.ppermute(lower_terms, ("row", "col"), flat_prev)

    source_local = jnp.arange(col_count, dtype=jnp.int32)[:, None]
    target_row = jnp.arange(row_count, dtype=jnp.int32)[None, :]
    offset = jnp.remainder(
        (target_row - row_index) * col_count + col_index - source_local, cluster_total
    )
    levels = jnp.arange(rank_cap, dtype=jnp.int32)
    live_rank = levels[None, None, :] < block_ranks[:, :, 0][:, :, None]
    live_pairs = (
        (offset != 0)[:, :, None, None] & live_rank[:, :, :, None] & live_rank[:, :, None, :]
    )
    masked = jnp.where(live_pairs, coupling[:, :, 0], jnp.zeros((), jnp.bfloat16))
    for way, lane in ((1, 1), (-1, 0)):
        source = jnp.remainder(col_index - way, col_count)
        target = jnp.remainder(row_index + (way - col_index + source) // col_count, row_count)
        corner = (source, target, 0, 0)
        piece = lax.dynamic_slice(masked, corner, (1, 1, rank_cap, rank_cap))
        far = lax.dynamic_index_in_dim(flag_rows, source, axis=0, keepdims=False)[lane] < 0.5
        piece = jnp.where(far, piece, jnp.zeros((), jnp.bfloat16))
        masked = lax.dynamic_update_slice(masked, piece, corner)
    z_count = row_count // 4
    masked = masked.reshape(col_count, 2, z_count, 2, rank_cap, rank_cap)
    core = row_index % 2
    halves = []
    for pick in (core, 1 - core):
        chosen = lax.dynamic_index_in_dim(masked, pick, axis=3, keepdims=False)
        halves.append(
            jnp.einsum(
                "sta,syzab->zybt", source_proj, chosen, preferred_element_type=jnp.float32
            ).astype(jnp.bfloat16)
        )
    coeffs = row_reduce(halves[0], halves[1], row_count).astype(jnp.bfloat16)
    far_part = jnp.einsum("bt,eb->te", coeffs, col_bases, preferred_element_type=jnp.float32)
    return far_part + centre + from_left.astype(jnp.float32) + from_right.astype(jnp.float32)


def solution(mesh):
    return jax.shard_map(
        local,
        mesh=mesh,
        in_specs=(
            P(None, ("row", "col")),
            P(("row", "col")),
            P(),
            P(("row", "col"), None),
            P("row", None, "col", None, None),
            P("row", None, "col"),
            P(("row", "col"), None),
            P(("row", "col"), None, None, None),
            P(("row", "col"), None),
        ),
        out_specs=P(None, ("row", "col")),
        check_vma=False,
    )
```

```python
import functools

import jax
import jax.numpy as jnp
from jax import lax
from jax.experimental import pallas as pl
from jax.experimental.pallas import tpu as pltpu
from jax.sharding import PartitionSpec as P


def local_kernel(
    hist_ref, tail_ref, table_ref, class_ref, rows_ref, near_ref, flag_ref,
    proj_ref, centre_ref, lower_ref, upper_ref, high_ref, low_ref,
):
    block, width = high_ref.shape[1], high_ref.shape[2]
    step = pl.program_id(0)

    @pl.when(step == 0)
    def _():
        table = table_ref[...]
        for kind in range(high_ref.shape[0]):
            row = jnp.broadcast_to(table[kind : kind + 1, :], (block, width))
            full = pltpu.roll(row, 0, 1, stride=1, stride_axis=0)
            high = full.astype(jnp.bfloat16)
            high_ref[kind] = high
            low_ref[kind] = (full - high.astype(jnp.float32)).astype(jnp.bfloat16)

    start = pl.multiple_of(step * block, block)
    head = hist_ref[pl.ds(start, block), :]
    extra = width - block
    limit = ((hist_ref.shape[0] - extra) // 16) * 16
    later = pl.multiple_of(jnp.minimum(start + block, limit), 16)
    rest = jnp.where(step == pl.num_programs(0) - 1, tail_ref[...], hist_ref[pl.ds(later, extra), :])
    kinds = class_ref[...]
    total = jnp.zeros((block, head.shape[1]), jnp.float32)
    for kind in range(high_ref.shape[0]):
        part = jnp.dot(high_ref[kind, :, :block], head, preferred_element_type=jnp.float32)
        part = part + jnp.dot(high_ref[kind, :, block:], rest, preferred_element_type=jnp.float32)
        part = part + jnp.dot(low_ref[kind, :, :block], head, preferred_element_type=jnp.float32)
        part = part + jnp.dot(low_ref[kind, :, block:], rest, preferred_element_type=jnp.float32)
        total = jnp.where(kinds == kind, part, total)
    contracted = total.astype(jnp.bfloat16)
    proj_ref[...] = jnp.dot(contracted, rows_ref[...], preferred_element_type=jnp.float32).astype(
        jnp.bfloat16
    )
    flags = flag_ref[...]
    centre_ref[...] = jnp.dot(contracted, near_ref[1], preferred_element_type=jnp.float32)
    lower = jnp.dot(contracted, near_ref[0], preferred_element_type=jnp.float32)
    lower_ref[...] = (lower * flags[0:1, :]).astype(jnp.bfloat16)
    upper = jnp.dot(contracted, near_ref[2], preferred_element_type=jnp.float32)
    upper_ref[...] = (upper * flags[1:2, :]).astype(jnp.bfloat16)


def local_terms(history, lag_class, lag_table, row_bases, near_blocks, near_flags, steps):
    class_total, lags = lag_table.shape
    size = history.shape[1]
    rank = row_bases.shape[1]
    block = 256
    width = block + 128
    blocks = steps // block
    tail = history[blocks * block :]
    tail = jnp.pad(tail, ((0, width - block - tail.shape[0]), (0, 0)))
    table = jnp.pad(lag_table, ((0, 0), (0, width - lags)))
    kinds = lag_class.reshape(1, size)
    flags = jnp.broadcast_to(near_flags[0].astype(jnp.float32)[:, None], (2, size))
    whole = lambda shape: pl.BlockSpec(shape, lambda b: (0,) * len(shape))
    rows_of = lambda cols: pl.BlockSpec((block, cols), lambda b: (b, 0))
    return pl.pallas_call(
        local_kernel,
        grid=(blocks,),
        out_shape=(
            jax.ShapeDtypeStruct((steps, rank), jnp.bfloat16),
            jax.ShapeDtypeStruct((steps, size), jnp.float32),
            jax.ShapeDtypeStruct((steps, size), jnp.bfloat16),
            jax.ShapeDtypeStruct((steps, size), jnp.bfloat16),
        ),
        in_specs=[
            whole(history.shape),
            whole(tail.shape),
            whole(table.shape),
            whole(kinds.shape),
            whole(row_bases.shape),
            whole(near_blocks.shape[1:]),
            whole(flags.shape),
        ],
        out_specs=(rows_of(rank), rows_of(size), rows_of(size), rows_of(size)),
        scratch_shapes=[
            pltpu.VMEM((class_total, block, width), jnp.bfloat16),
            pltpu.VMEM((class_total, block, width), jnp.bfloat16),
        ],
        compiler_params=pltpu.CompilerParams(dimension_semantics=("arbitrary",)),
    )(history, tail, table, kinds, row_bases, near_blocks[0], flags)


def ring_kernel(z_count, data_ref, out_ref, recv, send, send_sem, recv_sem, pair, far, far_send, far_recv):
    row = lax.axis_index("row")
    col = lax.axis_index("col")
    core = row % 2
    zpos = (row // 2) % z_count
    base = row - zpos * 2
    up_dev = base + ((zpos + 1) % z_count) * 2
    down_dev = base + ((zpos + z_count - 1) % z_count) * 2
    half = data_ref.shape[3] // 2
    mesh_kind = pl.DeviceIdType.MESH

    barrier = pltpu.get_barrier_semaphore()
    for neighbour in (up_dev, down_dev):
        pl.semaphore_signal(barrier, inc=1, device_id=(neighbour, col), device_id_type=mesh_kind)
    rows = lax.axis_size("row")
    far_dev = (row + rows // 2) % rows
    pl.semaphore_signal(barrier, inc=1, device_id=(far_dev, col), device_id_type=mesh_kind)
    pl.semaphore_wait(barrier, 3)

    rings = (
        (0, up_dev, lambda s: (zpos + (z_count - 1) * (s + 1)) % z_count, 0),
        (1, down_dev, lambda s: (zpos + s + 1) % z_count, half),
    )
    last = z_count - 1
    copies = {}
    for step in range(last):
        for way, target, index, low in rings:
            if step == 0:
                source = data_ref.at[index(step), :, :, pl.ds(low, half)]
            else:
                copies[(way, step - 1)].wait_recv()
                own = data_ref[index(step), :, :, pl.ds(low, half)].astype(jnp.float32)
                send[way, step] = (recv[way, step - 1].astype(jnp.float32) + own).astype(jnp.bfloat16)
                source = send.at[way, step]
            copy = pltpu.make_async_remote_copy(
                src_ref=source,
                dst_ref=recv.at[way, step],
                send_sem=send_sem.at[way, step],
                recv_sem=recv_sem.at[way, step],
                device_id=(target, col),
                device_id_type=mesh_kind,
            )
            copy.start()
            copies[(way, step)] = copy
    for way, target, index, low in rings:
        copies[(way, last - 1)].wait_recv()
        own = data_ref[zpos, :, :, pl.ds(low, half)].astype(jnp.float32)
        pair[:, :, pl.ds(low, half)] = recv[way, last - 1].astype(jnp.float32) + own
    high = row // (rows // 2)
    far[0] = pair[1 - high].astype(jnp.bfloat16)
    far_copy = pltpu.make_async_remote_copy(
        src_ref=far.at[0],
        dst_ref=far.at[1],
        send_sem=far_send,
        recv_sem=far_recv,
        device_id=(far_dev, col),
        device_id_type=mesh_kind,
    )
    far_copy.start()
    far_copy.wait_recv()
    out_ref[...] = pair[high] + far[1].astype(jnp.float32)
    for copy in copies.values():
        copy.wait_send()
    far_copy.wait_send()


def z_ring(data, z_count):
    _, pairs, width, steps = data.shape
    half = steps // 2
    return pl.pallas_call(
        functools.partial(ring_kernel, z_count),
        out_shape=jax.ShapeDtypeStruct((width, steps), jnp.float32),
        in_specs=[pl.BlockSpec(memory_space=pltpu.VMEM)],
        out_specs=pl.BlockSpec(memory_space=pltpu.VMEM),
        scratch_shapes=[
            pltpu.VMEM((2, z_count - 1, pairs, width, half), jnp.bfloat16),
            pltpu.VMEM((2, z_count - 1, pairs, width, half), jnp.bfloat16),
            pltpu.SemaphoreType.DMA((2, z_count - 1)),
            pltpu.SemaphoreType.DMA((2, z_count - 1)),
            pltpu.VMEM((pairs, width, steps), jnp.float32),
            pltpu.VMEM((2, width, steps), jnp.bfloat16),
            pltpu.SemaphoreType.DMA,
            pltpu.SemaphoreType.DMA,
        ],
        compiler_params=pltpu.CompilerParams(collective_id=0, has_side_effects=True),
    )(data)


def row_reduce(keep, give, row_count):
    z_count = row_count // 4
    core_pairs = [(s, s ^ 1) for s in range(row_count)]
    got = lax.ppermute(give, "row", core_pairs)
    summed = (keep.astype(jnp.float32) + got.astype(jnp.float32)).astype(jnp.bfloat16)
    return z_ring(summed, z_count)


def local(
    history,
    lag_class,
    lag_table,
    row_bases,
    coupling,
    block_ranks,
    col_bases,
    near_blocks,
    near_flags,
):
    row_count = lax.axis_size("row")
    col_count = lax.axis_size("col")
    cluster_total = row_count * col_count
    row_index = lax.axis_index("row")
    col_index = lax.axis_index("col")
    rank_cap = row_bases.shape[1]
    steps = history.shape[0] - lag_table.shape[1] + 1
    projected, centre, lower_terms, upper_terms = local_terms(
        history, lag_class, lag_table, row_bases, near_blocks, near_flags, steps
    )
    flag_block = jnp.zeros((16, rank_cap), jnp.bfloat16).at[0, 0:2].set(
        near_flags[0].astype(jnp.bfloat16)
    )
    extended = jnp.concatenate([projected, flag_block], axis=0)
    gathered = lax.all_gather(extended, "col", axis=0, tiled=False)
    source_proj = gathered[:, :steps]
    flag_rows = gathered[:, steps, 0:2]

    flat_next = [(s, (s + 1) % cluster_total) for s in range(cluster_total)]
    flat_prev = [(s, (s - 1) % cluster_total) for s in range(cluster_total)]
    from_left = lax.ppermute(upper_terms, ("row", "col"), flat_next)
    from_right = lax.ppermute(lower_terms, ("row", "col"), flat_prev)

    source_local = jnp.arange(col_count, dtype=jnp.int32)[:, None]
    target_row = jnp.arange(row_count, dtype=jnp.int32)[None, :]
    offset = jnp.remainder(
        (target_row - row_index) * col_count + col_index - source_local, cluster_total
    )
    levels = jnp.arange(rank_cap, dtype=jnp.int32)
    live_rank = levels[None, None, :] < block_ranks[:, :, 0][:, :, None]
    live_pairs = (
        (offset != 0)[:, :, None, None] & live_rank[:, :, :, None] & live_rank[:, :, None, :]
    )
    masked = jnp.where(live_pairs, coupling[:, :, 0], jnp.zeros((), jnp.bfloat16))
    for way, lane in ((1, 1), (-1, 0)):
        source = jnp.remainder(col_index - way, col_count)
        target = jnp.remainder(row_index + (way - col_index + source) // col_count, row_count)
        corner = (source, target, 0, 0)
        piece = lax.dynamic_slice(masked, corner, (1, 1, rank_cap, rank_cap))
        far = lax.dynamic_index_in_dim(flag_rows, source, axis=0, keepdims=False)[lane] < 0.5
        piece = jnp.where(far, piece, jnp.zeros((), jnp.bfloat16))
        masked = lax.dynamic_update_slice(masked, piece, corner)
    z_count = row_count // 4
    masked = masked.reshape(col_count, 2, z_count, 2, rank_cap, rank_cap)
    core = row_index % 2
    halves = []
    for pick in (core, 1 - core):
        chosen = lax.dynamic_index_in_dim(masked, pick, axis=3, keepdims=False)
        halves.append(
            jnp.einsum(
                "sta,syzab->zybt", source_proj, chosen, preferred_element_type=jnp.float32
            ).astype(jnp.bfloat16)
        )
    coeffs = row_reduce(halves[0], halves[1], row_count).astype(jnp.bfloat16)
    far_part = jnp.einsum("bt,eb->te", coeffs, col_bases, preferred_element_type=jnp.float32)
    return far_part + centre + from_left.astype(jnp.float32) + from_right.astype(jnp.float32)


def solution(mesh):
    return jax.shard_map(
        local,
        mesh=mesh,
        in_specs=(
            P(None, ("row", "col")),
            P(("row", "col")),
            P(),
            P(("row", "col"), None),
            P("row", None, "col", None, None),
            P("row", None, "col"),
            P(("row", "col"), None),
            P(("row", "col"), None, None, None),
            P(("row", "col"), None),
        ),
        out_specs=P(None, ("row", "col")),
        check_vma=False,
    )
```

```python
import functools

import jax
import jax.numpy as jnp
from jax import lax
from jax.experimental import pallas as pl
from jax.experimental.pallas import tpu as pltpu
from jax.sharding import PartitionSpec as P


def local_kernel(
    hist_ref, tail_ref, table_ref, class_ref, rows_ref, near_ref, flag_ref,
    proj_ref, centre_ref, lower_ref, upper_ref, high_ref, low_ref,
):
    block, width = high_ref.shape[1], high_ref.shape[2]
    step = pl.program_id(0)

    @pl.when(step == 0)
    def _():
        table = table_ref[...]
        for kind in range(high_ref.shape[0]):
            row = jnp.broadcast_to(table[kind : kind + 1, :], (block, width))
            full = pltpu.roll(row, 0, 1, stride=1, stride_axis=0)
            high = full.astype(jnp.bfloat16)
            high_ref[kind] = high
            low_ref[kind] = (full - high.astype(jnp.float32)).astype(jnp.bfloat16)

    start = pl.multiple_of(step * block, block)
    head = hist_ref[pl.ds(start, block), :]
    extra = width - block
    limit = ((hist_ref.shape[0] - extra) // 16) * 16
    later = pl.multiple_of(jnp.minimum(start + block, limit), 16)
    rest = jnp.where(step == pl.num_programs(0) - 1, tail_ref[...], hist_ref[pl.ds(later, extra), :])
    kinds = class_ref[...]
    total = jnp.zeros((block, head.shape[1]), jnp.float32)
    for kind in range(high_ref.shape[0]):
        part = jnp.dot(high_ref[kind, :, :block], head, preferred_element_type=jnp.float32)
        part = part + jnp.dot(high_ref[kind, :, block:], rest, preferred_element_type=jnp.float32)
        part = part + jnp.dot(low_ref[kind, :, :block], head, preferred_element_type=jnp.float32)
        part = part + jnp.dot(low_ref[kind, :, block:], rest, preferred_element_type=jnp.float32)
        total = jnp.where(kinds == kind, part, total)
    contracted = total.astype(jnp.bfloat16)
    proj_ref[...] = jnp.dot(contracted, rows_ref[...], preferred_element_type=jnp.float32).astype(
        jnp.bfloat16
    )
    flags = flag_ref[...]
    centre_ref[...] = jnp.dot(contracted, near_ref[1], preferred_element_type=jnp.float32)
    lower = jnp.dot(contracted, near_ref[0], preferred_element_type=jnp.float32)
    lower_ref[...] = (lower * flags[0:1, :]).astype(jnp.bfloat16)
    upper = jnp.dot(contracted, near_ref[2], preferred_element_type=jnp.float32)
    upper_ref[...] = (upper * flags[1:2, :]).astype(jnp.bfloat16)


def local_terms(history, lag_class, lag_table, row_bases, near_blocks, near_flags, steps):
    class_total, lags = lag_table.shape
    size = history.shape[1]
    rank = row_bases.shape[1]
    block = 256
    width = block + 128
    blocks = steps // block
    tail = history[blocks * block :]
    tail = jnp.pad(tail, ((0, width - block - tail.shape[0]), (0, 0)))
    table = jnp.pad(lag_table, ((0, 0), (0, width - lags)))
    kinds = lag_class.reshape(1, size)
    flags = jnp.broadcast_to(near_flags[0].astype(jnp.float32)[:, None], (2, size))
    whole = lambda shape: pl.BlockSpec(shape, lambda b: (0,) * len(shape))
    rows_of = lambda cols: pl.BlockSpec((block, cols), lambda b: (b, 0))
    return pl.pallas_call(
        local_kernel,
        grid=(blocks,),
        out_shape=(
            jax.ShapeDtypeStruct((steps, rank), jnp.bfloat16),
            jax.ShapeDtypeStruct((steps, size), jnp.float32),
            jax.ShapeDtypeStruct((steps, size), jnp.bfloat16),
            jax.ShapeDtypeStruct((steps, size), jnp.bfloat16),
        ),
        in_specs=[
            whole(history.shape),
            whole(tail.shape),
            whole(table.shape),
            whole(kinds.shape),
            whole(row_bases.shape),
            whole(near_blocks.shape[1:]),
            whole(flags.shape),
        ],
        out_specs=(rows_of(rank), rows_of(size), rows_of(size), rows_of(size)),
        scratch_shapes=[
            pltpu.VMEM((class_total, block, width), jnp.bfloat16),
            pltpu.VMEM((class_total, block, width), jnp.bfloat16),
        ],
        compiler_params=pltpu.CompilerParams(dimension_semantics=("arbitrary",)),
    )(history, tail, table, kinds, row_bases, near_blocks[0], flags)


def ring_kernel(z_count, keep_ref, got_ref, out_ref, recv, send, send_sem, recv_sem, pair, far, far_send, far_recv):
    row = lax.axis_index("row")
    col = lax.axis_index("col")
    core = row % 2
    zpos = (row // 2) % z_count
    base = row - zpos * 2
    up_dev = base + ((zpos + 1) % z_count) * 2
    down_dev = base + ((zpos + z_count - 1) % z_count) * 2
    half = keep_ref.shape[3] // 2
    mesh_kind = pl.DeviceIdType.MESH

    barrier = pltpu.get_barrier_semaphore()
    for neighbour in (up_dev, down_dev):
        pl.semaphore_signal(barrier, inc=1, device_id=(neighbour, col), device_id_type=mesh_kind)
    rows = lax.axis_size("row")
    far_dev = (row + rows // 2) % rows
    pl.semaphore_signal(barrier, inc=1, device_id=(far_dev, col), device_id_type=mesh_kind)
    pl.semaphore_wait(barrier, 3)

    rings = (
        (0, up_dev, lambda s: (zpos + (z_count - 1) * (s + 1)) % z_count, 0),
        (1, down_dev, lambda s: (zpos + s + 1) % z_count, half),
    )
    last = z_count - 1
    copies = {}

    def both(index, low):
        mine = keep_ref[index, :, :, pl.ds(low, half)].astype(jnp.float32)
        return mine + got_ref[index, :, :, pl.ds(low, half)].astype(jnp.float32)

    for step in range(last):
        for way, target, index, low in rings:
            total = both(index(step), low)
            if step > 0:
                copies[(way, step - 1)].wait_recv()
                total = total + recv[way, step - 1].astype(jnp.float32)
            send[way, step] = total.astype(jnp.bfloat16)
            source = send.at[way, step]
            copy = pltpu.make_async_remote_copy(
                src_ref=source,
                dst_ref=recv.at[way, step],
                send_sem=send_sem.at[way, step],
                recv_sem=recv_sem.at[way, step],
                device_id=(target, col),
                device_id_type=mesh_kind,
            )
            copy.start()
            copies[(way, step)] = copy
    for way, target, index, low in rings:
        copies[(way, last - 1)].wait_recv()
        pair[:, :, pl.ds(low, half)] = recv[way, last - 1].astype(jnp.float32) + both(zpos, low)
    high = row // (rows // 2)
    far[0] = pair[1 - high].astype(jnp.bfloat16)
    far_copy = pltpu.make_async_remote_copy(
        src_ref=far.at[0],
        dst_ref=far.at[1],
        send_sem=far_send,
        recv_sem=far_recv,
        device_id=(far_dev, col),
        device_id_type=mesh_kind,
    )
    far_copy.start()
    far_copy.wait_recv()
    out_ref[...] = pair[high] + far[1].astype(jnp.float32)
    for copy in copies.values():
        copy.wait_send()
    far_copy.wait_send()


def z_ring(keep, got, z_count):
    _, pairs, width, steps = keep.shape
    half = steps // 2
    return pl.pallas_call(
        functools.partial(ring_kernel, z_count),
        out_shape=jax.ShapeDtypeStruct((width, steps), jnp.float32),
        in_specs=[pl.BlockSpec(memory_space=pltpu.VMEM)] * 2,
        out_specs=pl.BlockSpec(memory_space=pltpu.VMEM),
        scratch_shapes=[
            pltpu.VMEM((2, z_count - 1, pairs, width, half), jnp.bfloat16),
            pltpu.VMEM((2, z_count - 1, pairs, width, half), jnp.bfloat16),
            pltpu.SemaphoreType.DMA((2, z_count - 1)),
            pltpu.SemaphoreType.DMA((2, z_count - 1)),
            pltpu.VMEM((pairs, width, steps), jnp.float32),
            pltpu.VMEM((2, width, steps), jnp.bfloat16),
            pltpu.SemaphoreType.DMA,
            pltpu.SemaphoreType.DMA,
        ],
        compiler_params=pltpu.CompilerParams(collective_id=0, has_side_effects=True),
    )(keep, got)


def row_reduce(keep, give, row_count):
    z_count = row_count // 4
    core_pairs = [(s, s ^ 1) for s in range(row_count)]
    got = lax.ppermute(give, "row", core_pairs)
    return z_ring(keep, got, z_count)


def local(
    history,
    lag_class,
    lag_table,
    row_bases,
    coupling,
    block_ranks,
    col_bases,
    near_blocks,
    near_flags,
):
    row_count = lax.axis_size("row")
    col_count = lax.axis_size("col")
    cluster_total = row_count * col_count
    row_index = lax.axis_index("row")
    col_index = lax.axis_index("col")
    rank_cap = row_bases.shape[1]
    steps = history.shape[0] - lag_table.shape[1] + 1
    projected, centre, lower_terms, upper_terms = local_terms(
        history, lag_class, lag_table, row_bases, near_blocks, near_flags, steps
    )
    flag_block = jnp.zeros((16, rank_cap), jnp.bfloat16).at[0, 0:2].set(
        near_flags[0].astype(jnp.bfloat16)
    )
    extended = jnp.concatenate([projected, flag_block], axis=0)
    gathered = lax.all_gather(extended, "col", axis=0, tiled=False)
    source_proj = gathered[:, :steps]
    flag_rows = gathered[:, steps, 0:2]

    flat_next = [(s, (s + 1) % cluster_total) for s in range(cluster_total)]
    flat_prev = [(s, (s - 1) % cluster_total) for s in range(cluster_total)]
    from_left = lax.ppermute(upper_terms, ("row", "col"), flat_next)
    from_right = lax.ppermute(lower_terms, ("row", "col"), flat_prev)

    source_local = jnp.arange(col_count, dtype=jnp.int32)[:, None]
    target_row = jnp.arange(row_count, dtype=jnp.int32)[None, :]
    offset = jnp.remainder(
        (target_row - row_index) * col_count + col_index - source_local, cluster_total
    )
    levels = jnp.arange(rank_cap, dtype=jnp.int32)
    live_rank = levels[None, None, :] < block_ranks[:, :, 0][:, :, None]
    live_pairs = (
        (offset != 0)[:, :, None, None] & live_rank[:, :, :, None] & live_rank[:, :, None, :]
    )
    masked = jnp.where(live_pairs, coupling[:, :, 0], jnp.zeros((), jnp.bfloat16))
    for way, lane in ((1, 1), (-1, 0)):
        source = jnp.remainder(col_index - way, col_count)
        target = jnp.remainder(row_index + (way - col_index + source) // col_count, row_count)
        corner = (source, target, 0, 0)
        piece = lax.dynamic_slice(masked, corner, (1, 1, rank_cap, rank_cap))
        far = lax.dynamic_index_in_dim(flag_rows, source, axis=0, keepdims=False)[lane] < 0.5
        piece = jnp.where(far, piece, jnp.zeros((), jnp.bfloat16))
        masked = lax.dynamic_update_slice(masked, piece, corner)
    z_count = row_count // 4
    masked = masked.reshape(col_count, 2, z_count, 2, rank_cap, rank_cap)
    core = row_index % 2
    halves = []
    for pick in (core, 1 - core):
        chosen = lax.dynamic_index_in_dim(masked, pick, axis=3, keepdims=False)
        halves.append(
            jnp.einsum(
                "sta,syzab->zybt", source_proj, chosen, preferred_element_type=jnp.float32
            ).astype(jnp.bfloat16)
        )
    coeffs = row_reduce(halves[0], halves[1], row_count).astype(jnp.bfloat16)
    far_part = jnp.einsum("bt,eb->te", coeffs, col_bases, preferred_element_type=jnp.float32)
    return far_part + centre + from_left.astype(jnp.float32) + from_right.astype(jnp.float32)


def solution(mesh):
    return jax.shard_map(
        local,
        mesh=mesh,
        in_specs=(
            P(None, ("row", "col")),
            P(("row", "col")),
            P(),
            P(("row", "col"), None),
            P("row", None, "col", None, None),
            P("row", None, "col"),
            P(("row", "col"), None),
            P(("row", "col"), None, None, None),
            P(("row", "col"), None),
        ),
        out_specs=P(None, ("row", "col")),
        check_vma=False,
    )
```

```python
import functools

import jax
import jax.numpy as jnp
from jax import lax
from jax.experimental import pallas as pl
from jax.experimental.pallas import tpu as pltpu
from jax.sharding import PartitionSpec as P


def local_kernel(
    hist_ref, tail_ref, table_ref, class_ref, rows_ref, near_ref, flag_ref,
    proj_ref, centre_ref, lower_ref, upper_ref, high_ref, low_ref,
):
    block, width = high_ref.shape[1], high_ref.shape[2]
    step = pl.program_id(0)

    @pl.when(step == 0)
    def _():
        table = table_ref[...]
        for kind in range(high_ref.shape[0]):
            row = jnp.broadcast_to(table[kind : kind + 1, :], (block, width))
            full = pltpu.roll(row, 0, 1, stride=1, stride_axis=0)
            high = full.astype(jnp.bfloat16)
            high_ref[kind] = high
            low_ref[kind] = (full - high.astype(jnp.float32)).astype(jnp.bfloat16)

    start = pl.multiple_of(step * block, block)
    head = hist_ref[pl.ds(start, block), :]
    extra = width - block
    limit = ((hist_ref.shape[0] - extra) // 16) * 16
    later = pl.multiple_of(jnp.minimum(start + block, limit), 16)
    rest = jnp.where(step == pl.num_programs(0) - 1, tail_ref[...], hist_ref[pl.ds(later, extra), :])
    kinds = class_ref[...]
    total = jnp.zeros((block, head.shape[1]), jnp.float32)
    for kind in range(high_ref.shape[0]):
        part = jnp.dot(high_ref[kind, :, :block], head, preferred_element_type=jnp.float32)
        part = part + jnp.dot(high_ref[kind, :, block:], rest, preferred_element_type=jnp.float32)
        part = part + jnp.dot(low_ref[kind, :, :block], head, preferred_element_type=jnp.float32)
        part = part + jnp.dot(low_ref[kind, :, block:], rest, preferred_element_type=jnp.float32)
        total = jnp.where(kinds == kind, part, total)
    contracted = total.astype(jnp.bfloat16)
    projected = lax.dot_general(
        contracted, rows_ref[...], (((1,), (1,)), ((), ())), preferred_element_type=jnp.float32
    )
    proj_ref[...] = projected.astype(jnp.bfloat16)
    flags = flag_ref[...]
    centre_ref[...] = jnp.dot(contracted, near_ref[1], preferred_element_type=jnp.float32)
    lower = jnp.dot(contracted, near_ref[0], preferred_element_type=jnp.float32)
    lower_ref[...] = (lower * flags[0:1, :]).astype(jnp.bfloat16)
    upper = jnp.dot(contracted, near_ref[2], preferred_element_type=jnp.float32)
    upper_ref[...] = (upper * flags[1:2, :]).astype(jnp.bfloat16)


def local_terms(history, lag_class, lag_table, row_bases, near_blocks, near_flags, steps):
    class_total, lags = lag_table.shape
    size = history.shape[1]
    rank = row_bases.shape[1]
    columns = jnp.transpose(row_bases)
    block = 256
    width = block + 128
    blocks = steps // block
    tail = history[blocks * block :]
    tail = jnp.pad(tail, ((0, width - block - tail.shape[0]), (0, 0)))
    table = jnp.pad(lag_table, ((0, 0), (0, width - lags)))
    kinds = lag_class.reshape(1, size)
    flags = jnp.broadcast_to(near_flags[0].astype(jnp.float32)[:, None], (2, size))
    whole = lambda shape: pl.BlockSpec(shape, lambda b: (0,) * len(shape))
    rows_of = lambda cols: pl.BlockSpec((block, cols), lambda b: (b, 0))
    return pl.pallas_call(
        local_kernel,
        grid=(blocks,),
        out_shape=(
            jax.ShapeDtypeStruct((steps, rank), jnp.bfloat16),
            jax.ShapeDtypeStruct((steps, size), jnp.float32),
            jax.ShapeDtypeStruct((steps, size), jnp.bfloat16),
            jax.ShapeDtypeStruct((steps, size), jnp.bfloat16),
        ),
        in_specs=[
            whole(history.shape),
            whole(tail.shape),
            whole(table.shape),
            whole(kinds.shape),
            whole(columns.shape),
            whole(near_blocks.shape[1:]),
            whole(flags.shape),
        ],
        out_specs=(rows_of(rank), rows_of(size), rows_of(size), rows_of(size)),
        scratch_shapes=[
            pltpu.VMEM((class_total, block, width), jnp.bfloat16),
            pltpu.VMEM((class_total, block, width), jnp.bfloat16),
        ],
        compiler_params=pltpu.CompilerParams(dimension_semantics=("arbitrary",)),
    )(history, tail, table, kinds, columns, near_blocks[0], flags)


def ring_kernel(z_count, data_ref, out_ref, recv, send, send_sem, recv_sem, pair, far, far_send, far_recv):
    row = lax.axis_index("row")
    col = lax.axis_index("col")
    core = row % 2
    zpos = (row // 2) % z_count
    base = row - zpos * 2
    up_dev = base + ((zpos + 1) % z_count) * 2
    down_dev = base + ((zpos + z_count - 1) % z_count) * 2
    half = data_ref.shape[3] // 2
    mesh_kind = pl.DeviceIdType.MESH

    barrier = pltpu.get_barrier_semaphore()
    for neighbour in (up_dev, down_dev):
        pl.semaphore_signal(barrier, inc=1, device_id=(neighbour, col), device_id_type=mesh_kind)
    rows = lax.axis_size("row")
    far_dev = (row + rows // 2) % rows
    pl.semaphore_signal(barrier, inc=1, device_id=(far_dev, col), device_id_type=mesh_kind)
    pl.semaphore_wait(barrier, 3)

    rings = (
        (0, up_dev, lambda s: (zpos + (z_count - 1) * (s + 1)) % z_count, 0),
        (1, down_dev, lambda s: (zpos + s + 1) % z_count, half),
    )
    last = z_count - 1
    copies = {}
    for step in range(last):
        for way, target, index, low in rings:
            if step == 0:
                source = data_ref.at[index(step), :, :, pl.ds(low, half)]
            else:
                copies[(way, step - 1)].wait_recv()
                own = data_ref[index(step), :, :, pl.ds(low, half)].astype(jnp.float32)
                send[way, step] = (recv[way, step - 1].astype(jnp.float32) + own).astype(jnp.bfloat16)
                source = send.at[way, step]
            copy = pltpu.make_async_remote_copy(
                src_ref=source,
                dst_ref=recv.at[way, step],
                send_sem=send_sem.at[way, step],
                recv_sem=recv_sem.at[way, step],
                device_id=(target, col),
                device_id_type=mesh_kind,
            )
            copy.start()
            copies[(way, step)] = copy
    for way, target, index, low in rings:
        copies[(way, last - 1)].wait_recv()
        own = data_ref[zpos, :, :, pl.ds(low, half)].astype(jnp.float32)
        pair[:, :, pl.ds(low, half)] = recv[way, last - 1].astype(jnp.float32) + own
    high = row // (rows // 2)
    far[0] = pair[1 - high].astype(jnp.bfloat16)
    far_copy = pltpu.make_async_remote_copy(
        src_ref=far.at[0],
        dst_ref=far.at[1],
        send_sem=far_send,
        recv_sem=far_recv,
        device_id=(far_dev, col),
        device_id_type=mesh_kind,
    )
    far_copy.start()
    far_copy.wait_recv()
    out_ref[...] = pair[high] + far[1].astype(jnp.float32)
    for copy in copies.values():
        copy.wait_send()
    far_copy.wait_send()


def z_ring(data, z_count):
    _, pairs, width, steps = data.shape
    half = steps // 2
    return pl.pallas_call(
        functools.partial(ring_kernel, z_count),
        out_shape=jax.ShapeDtypeStruct((width, steps), jnp.float32),
        in_specs=[pl.BlockSpec(memory_space=pltpu.VMEM)],
        out_specs=pl.BlockSpec(memory_space=pltpu.VMEM),
        scratch_shapes=[
            pltpu.VMEM((2, z_count - 1, pairs, width, half), jnp.bfloat16),
            pltpu.VMEM((2, z_count - 1, pairs, width, half), jnp.bfloat16),
            pltpu.SemaphoreType.DMA((2, z_count - 1)),
            pltpu.SemaphoreType.DMA((2, z_count - 1)),
            pltpu.VMEM((pairs, width, steps), jnp.float32),
            pltpu.VMEM((2, width, steps), jnp.bfloat16),
            pltpu.SemaphoreType.DMA,
            pltpu.SemaphoreType.DMA,
        ],
        compiler_params=pltpu.CompilerParams(collective_id=0, has_side_effects=True),
    )(data)


def row_reduce(keep, give, row_count):
    z_count = row_count // 4
    core_pairs = [(s, s ^ 1) for s in range(row_count)]
    got = lax.ppermute(give, "row", core_pairs)
    summed = (keep.astype(jnp.float32) + got.astype(jnp.float32)).astype(jnp.bfloat16)
    return z_ring(summed, z_count)


def local(
    history,
    lag_class,
    lag_table,
    row_bases,
    coupling,
    block_ranks,
    col_bases,
    near_blocks,
    near_flags,
):
    row_count = lax.axis_size("row")
    col_count = lax.axis_size("col")
    cluster_total = row_count * col_count
    row_index = lax.axis_index("row")
    col_index = lax.axis_index("col")
    rank_cap = row_bases.shape[1]
    steps = history.shape[0] - lag_table.shape[1] + 1
    projected, centre, lower_terms, upper_terms = local_terms(
        history, lag_class, lag_table, row_bases, near_blocks, near_flags, steps
    )
    flag_block = jnp.zeros((16, rank_cap), jnp.bfloat16).at[0, 0:2].set(
        near_flags[0].astype(jnp.bfloat16)
    )
    extended = jnp.concatenate([projected, flag_block], axis=0)
    gathered = lax.all_gather(extended, "col", axis=0, tiled=False)
    source_proj = gathered[:, :steps]
    flag_rows = gathered[:, steps, 0:2]

    flat_next = [(s, (s + 1) % cluster_total) for s in range(cluster_total)]
    flat_prev = [(s, (s - 1) % cluster_total) for s in range(cluster_total)]
    from_left = lax.ppermute(upper_terms, ("row", "col"), flat_next)
    from_right = lax.ppermute(lower_terms, ("row", "col"), flat_prev)

    source_local = jnp.arange(col_count, dtype=jnp.int32)[:, None]
    target_row = jnp.arange(row_count, dtype=jnp.int32)[None, :]
    offset = jnp.remainder(
        (target_row - row_index) * col_count + col_index - source_local, cluster_total
    )
    levels = jnp.arange(rank_cap, dtype=jnp.int32)
    live_rank = levels[None, None, :] < block_ranks[:, :, 0][:, :, None]
    live_pairs = (
        (offset != 0)[:, :, None, None] & live_rank[:, :, :, None] & live_rank[:, :, None, :]
    )
    masked = jnp.where(live_pairs, coupling[:, :, 0], jnp.zeros((), jnp.bfloat16))
    for way, lane in ((1, 1), (-1, 0)):
        source = jnp.remainder(col_index - way, col_count)
        target = jnp.remainder(row_index + (way - col_index + source) // col_count, row_count)
        corner = (source, target, 0, 0)
        piece = lax.dynamic_slice(masked, corner, (1, 1, rank_cap, rank_cap))
        far = lax.dynamic_index_in_dim(flag_rows, source, axis=0, keepdims=False)[lane] < 0.5
        piece = jnp.where(far, piece, jnp.zeros((), jnp.bfloat16))
        masked = lax.dynamic_update_slice(masked, piece, corner)
    z_count = row_count // 4
    masked = masked.reshape(col_count, 2, z_count, 2, rank_cap, rank_cap)
    core = row_index % 2
    halves = []
    for pick in (core, 1 - core):
        chosen = lax.dynamic_index_in_dim(masked, pick, axis=3, keepdims=False)
        halves.append(
            jnp.einsum(
                "sta,syzab->zybt", source_proj, chosen, preferred_element_type=jnp.float32
            ).astype(jnp.bfloat16)
        )
    coeffs = row_reduce(halves[0], halves[1], row_count).astype(jnp.bfloat16)
    far_part = jnp.einsum("bt,eb->te", coeffs, col_bases, preferred_element_type=jnp.float32)
    return far_part + centre + from_left.astype(jnp.float32) + from_right.astype(jnp.float32)


def solution(mesh):
    return jax.shard_map(
        local,
        mesh=mesh,
        in_specs=(
            P(None, ("row", "col")),
            P(("row", "col")),
            P(),
            P(("row", "col"), None),
            P("row", None, "col", None, None),
            P("row", None, "col"),
            P(("row", "col"), None),
            P(("row", "col"), None, None, None),
            P(("row", "col"), None),
        ),
        out_specs=P(None, ("row", "col")),
        check_vma=False,
    )
```

```python
import functools

import jax
import jax.numpy as jnp
from jax import lax
from jax.experimental import pallas as pl
from jax.experimental.pallas import tpu as pltpu
from jax.sharding import PartitionSpec as P


def local_kernel(
    hist_ref, tail_ref, table_ref, class_ref, rows_ref, near_ref, flag_ref,
    proj_ref, centre_ref, lower_ref, upper_ref, high_ref, low_ref,
):
    block, width = high_ref.shape[1], high_ref.shape[2]
    step = pl.program_id(0)

    @pl.when(step == 0)
    def _():
        table = table_ref[...]
        for kind in range(high_ref.shape[0]):
            row = jnp.broadcast_to(table[kind : kind + 1, :], (block, width))
            full = pltpu.roll(row, 0, 1, stride=1, stride_axis=0)
            high = full.astype(jnp.bfloat16)
            high_ref[kind] = high
            low_ref[kind] = (full - high.astype(jnp.float32)).astype(jnp.bfloat16)

    start = pl.multiple_of(step * block, block)
    head = hist_ref[pl.ds(start, block), :]
    extra = width - block
    limit = ((hist_ref.shape[0] - extra) // 16) * 16
    later = pl.multiple_of(jnp.minimum(start + block, limit), 16)
    rest = jnp.where(step == pl.num_programs(0) - 1, tail_ref[...], hist_ref[pl.ds(later, extra), :])
    kinds = class_ref[...]
    total = jnp.zeros((block, head.shape[1]), jnp.float32)
    for kind in range(high_ref.shape[0]):
        part = jnp.dot(high_ref[kind, :, :block], head, preferred_element_type=jnp.float32)
        part = part + jnp.dot(high_ref[kind, :, block:], rest, preferred_element_type=jnp.float32)
        part = part + jnp.dot(low_ref[kind, :, :block], head, preferred_element_type=jnp.float32)
        part = part + jnp.dot(low_ref[kind, :, block:], rest, preferred_element_type=jnp.float32)
        total = jnp.where(kinds == kind, part, total)
    contracted = total.astype(jnp.bfloat16)
    projected = lax.dot_general(
        contracted, rows_ref[...], (((1,), (1,)), ((), ())), preferred_element_type=jnp.float32
    )
    proj_ref[...] = projected.astype(jnp.bfloat16)
    flags = flag_ref[...]
    centre_ref[...] = jnp.dot(contracted, near_ref[1], preferred_element_type=jnp.float32)
    lower = jnp.dot(contracted, near_ref[0], preferred_element_type=jnp.float32)
    lower_ref[...] = (lower * flags[:, 0:1]).astype(jnp.bfloat16)
    upper = jnp.dot(contracted, near_ref[2], preferred_element_type=jnp.float32)
    upper_ref[...] = (upper * flags[:, 1:2]).astype(jnp.bfloat16)


def local_terms(history, lag_class, lag_table, row_bases, near_blocks, near_flags, steps):
    class_total, lags = lag_table.shape
    size = history.shape[1]
    rank = row_bases.shape[1]
    columns = jnp.transpose(row_bases)
    block = 256
    width = block + 128
    blocks = steps // block
    cut = blocks * block
    tail = lax.pad(
        history,
        jnp.zeros((), history.dtype),
        ((-cut, width - block - (history.shape[0] - cut), 0), (0, 0, 0)),
    )
    table = jnp.pad(lag_table, ((0, 0), (0, width - lags)))
    kinds = lag_class.reshape(1, size)
    flags = near_flags.astype(jnp.float32)
    whole = lambda shape: pl.BlockSpec(shape, lambda b: (0,) * len(shape))
    rows_of = lambda cols: pl.BlockSpec((block, cols), lambda b: (b, 0))
    return pl.pallas_call(
        local_kernel,
        grid=(blocks,),
        out_shape=(
            jax.ShapeDtypeStruct((steps, rank), jnp.bfloat16),
            jax.ShapeDtypeStruct((steps, size), jnp.float32),
            jax.ShapeDtypeStruct((steps, size), jnp.bfloat16),
            jax.ShapeDtypeStruct((steps, size), jnp.bfloat16),
        ),
        in_specs=[
            whole(history.shape),
            whole(tail.shape),
            whole(table.shape),
            whole(kinds.shape),
            whole(columns.shape),
            whole(near_blocks.shape[1:]),
            whole(flags.shape),
        ],
        out_specs=(rows_of(rank), rows_of(size), rows_of(size), rows_of(size)),
        scratch_shapes=[
            pltpu.VMEM((class_total, block, width), jnp.bfloat16),
            pltpu.VMEM((class_total, block, width), jnp.bfloat16),
        ],
        compiler_params=pltpu.CompilerParams(dimension_semantics=("arbitrary",)),
    )(history, tail, table, kinds, columns, near_blocks[0], flags)


def ring_kernel(z_count, data_ref, out_ref, recv, send, send_sem, recv_sem, pair, far, far_send, far_recv):
    row = lax.axis_index("row")
    col = lax.axis_index("col")
    core = row % 2
    zpos = (row // 2) % z_count
    base = row - zpos * 2
    up_dev = base + ((zpos + 1) % z_count) * 2
    down_dev = base + ((zpos + z_count - 1) % z_count) * 2
    half = data_ref.shape[3] // 2
    mesh_kind = pl.DeviceIdType.MESH

    barrier = pltpu.get_barrier_semaphore()
    for neighbour in (up_dev, down_dev):
        pl.semaphore_signal(barrier, inc=1, device_id=(neighbour, col), device_id_type=mesh_kind)
    rows = lax.axis_size("row")
    far_dev = (row + rows // 2) % rows
    pl.semaphore_signal(barrier, inc=1, device_id=(far_dev, col), device_id_type=mesh_kind)
    pl.semaphore_wait(barrier, 3)

    rings = (
        (0, up_dev, lambda s: (zpos + (z_count - 1) * (s + 1)) % z_count, 0),
        (1, down_dev, lambda s: (zpos + s + 1) % z_count, half),
    )
    last = z_count - 1
    copies = {}
    for step in range(last):
        for way, target, index, low in rings:
            if step == 0:
                source = data_ref.at[index(step), :, :, pl.ds(low, half)]
            else:
                copies[(way, step - 1)].wait_recv()
                own = data_ref[index(step), :, :, pl.ds(low, half)].astype(jnp.float32)
                send[way, step] = (recv[way, step - 1].astype(jnp.float32) + own).astype(jnp.bfloat16)
                source = send.at[way, step]
            copy = pltpu.make_async_remote_copy(
                src_ref=source,
                dst_ref=recv.at[way, step],
                send_sem=send_sem.at[way, step],
                recv_sem=recv_sem.at[way, step],
                device_id=(target, col),
                device_id_type=mesh_kind,
            )
            copy.start()
            copies[(way, step)] = copy
    for way, target, index, low in rings:
        copies[(way, last - 1)].wait_recv()
        own = data_ref[zpos, :, :, pl.ds(low, half)].astype(jnp.float32)
        pair[:, :, pl.ds(low, half)] = recv[way, last - 1].astype(jnp.float32) + own
    high = row // (rows // 2)
    far[0] = pair[1 - high].astype(jnp.bfloat16)
    far_copy = pltpu.make_async_remote_copy(
        src_ref=far.at[0],
        dst_ref=far.at[1],
        send_sem=far_send,
        recv_sem=far_recv,
        device_id=(far_dev, col),
        device_id_type=mesh_kind,
    )
    far_copy.start()
    far_copy.wait_recv()
    out_ref[...] = pair[high] + far[1].astype(jnp.float32)
    for copy in copies.values():
        copy.wait_send()
    far_copy.wait_send()


def z_ring(data, z_count):
    _, pairs, width, steps = data.shape
    half = steps // 2
    return pl.pallas_call(
        functools.partial(ring_kernel, z_count),
        out_shape=jax.ShapeDtypeStruct((width, steps), jnp.float32),
        in_specs=[pl.BlockSpec(memory_space=pltpu.VMEM)],
        out_specs=pl.BlockSpec(memory_space=pltpu.VMEM),
        scratch_shapes=[
            pltpu.VMEM((2, z_count - 1, pairs, width, half), jnp.bfloat16),
            pltpu.VMEM((2, z_count - 1, pairs, width, half), jnp.bfloat16),
            pltpu.SemaphoreType.DMA((2, z_count - 1)),
            pltpu.SemaphoreType.DMA((2, z_count - 1)),
            pltpu.VMEM((pairs, width, steps), jnp.float32),
            pltpu.VMEM((2, width, steps), jnp.bfloat16),
            pltpu.SemaphoreType.DMA,
            pltpu.SemaphoreType.DMA,
        ],
        compiler_params=pltpu.CompilerParams(collective_id=0, has_side_effects=True),
    )(data)


def row_reduce(keep, give, row_count):
    z_count = row_count // 4
    core_pairs = [(s, s ^ 1) for s in range(row_count)]
    got = lax.ppermute(give, "row", core_pairs)
    summed = (keep.astype(jnp.float32) + got.astype(jnp.float32)).astype(jnp.bfloat16)
    return z_ring(summed, z_count)


def local(
    history,
    lag_class,
    lag_table,
    row_bases,
    coupling,
    block_ranks,
    col_bases,
    near_blocks,
    near_flags,
):
    row_count = lax.axis_size("row")
    col_count = lax.axis_size("col")
    cluster_total = row_count * col_count
    row_index = lax.axis_index("row")
    col_index = lax.axis_index("col")
    rank_cap = row_bases.shape[1]
    steps = history.shape[0] - lag_table.shape[1] + 1
    projected, centre, lower_terms, upper_terms = local_terms(
        history, lag_class, lag_table, row_bases, near_blocks, near_flags, steps
    )
    flag_block = jnp.zeros((16, rank_cap), jnp.bfloat16).at[0, 0:2].set(
        near_flags[0].astype(jnp.bfloat16)
    )
    extended = jnp.concatenate([projected, flag_block], axis=0)
    gathered = lax.all_gather(extended, "col", axis=0, tiled=False)
    source_proj = gathered[:, :steps]
    flag_rows = gathered[:, steps, 0:2]

    flat_next = [(s, (s + 1) % cluster_total) for s in range(cluster_total)]
    flat_prev = [(s, (s - 1) % cluster_total) for s in range(cluster_total)]
    from_left = lax.ppermute(upper_terms, ("row", "col"), flat_next)
    from_right = lax.ppermute(lower_terms, ("row", "col"), flat_prev)

    source_local = jnp.arange(col_count, dtype=jnp.int32)[:, None]
    target_row = jnp.arange(row_count, dtype=jnp.int32)[None, :]
    offset = jnp.remainder(
        (target_row - row_index) * col_count + col_index - source_local, cluster_total
    )
    levels = jnp.arange(rank_cap, dtype=jnp.int32)
    live_rank = levels[None, None, :] < block_ranks[:, :, 0][:, :, None]
    live_pairs = (
        (offset != 0)[:, :, None, None] & live_rank[:, :, :, None] & live_rank[:, :, None, :]
    )
    masked = jnp.where(live_pairs, coupling[:, :, 0], jnp.zeros((), jnp.bfloat16))
    for way, lane in ((1, 1), (-1, 0)):
        source = jnp.remainder(col_index - way, col_count)
        target = jnp.remainder(row_index + (way - col_index + source) // col_count, row_count)
        corner = (source, target, 0, 0)
        piece = lax.dynamic_slice(masked, corner, (1, 1, rank_cap, rank_cap))
        far = lax.dynamic_index_in_dim(flag_rows, source, axis=0, keepdims=False)[lane] < 0.5
        piece = jnp.where(far, piece, jnp.zeros((), jnp.bfloat16))
        masked = lax.dynamic_update_slice(masked, piece, corner)
    z_count = row_count // 4
    masked = masked.reshape(col_count, 2, z_count, 2, rank_cap, rank_cap)
    core = row_index % 2
    halves = []
    for pick in (core, 1 - core):
        chosen = lax.dynamic_index_in_dim(masked, pick, axis=3, keepdims=False)
        halves.append(
            jnp.einsum(
                "sta,syzab->zybt", source_proj, chosen, preferred_element_type=jnp.float32
            ).astype(jnp.bfloat16)
        )
    coeffs = row_reduce(halves[0], halves[1], row_count).astype(jnp.bfloat16)
    far_part = jnp.einsum("bt,eb->te", coeffs, col_bases, preferred_element_type=jnp.float32)
    return far_part + centre + from_left.astype(jnp.float32) + from_right.astype(jnp.float32)


def solution(mesh):
    return jax.shard_map(
        local,
        mesh=mesh,
        in_specs=(
            P(None, ("row", "col")),
            P(("row", "col")),
            P(),
            P(("row", "col"), None),
            P("row", None, "col", None, None),
            P("row", None, "col"),
            P(("row", "col"), None),
            P(("row", "col"), None, None, None),
            P(("row", "col"), None),
        ),
        out_specs=P(None, ("row", "col")),
        check_vma=False,
    )
```

```python
import functools

import jax
import jax.numpy as jnp
from jax import lax
from jax.experimental import pallas as pl
from jax.experimental.pallas import tpu as pltpu
from jax.sharding import PartitionSpec as P


def local_kernel(
    hist_ref, tail_ref, table_ref, class_ref, rows_ref, near_ref, flag_ref,
    proj_ref, centre_ref, lower_ref, upper_ref, high_ref, low_ref,
):
    block, width = high_ref.shape[1], high_ref.shape[2]
    step = pl.program_id(0)

    @pl.when(step == 0)
    def _():
        table = table_ref[...]
        for kind in range(high_ref.shape[0]):
            row = jnp.broadcast_to(table[kind : kind + 1, :], (block, width))
            full = pltpu.roll(row, 0, 1, stride=1, stride_axis=0)
            high = full.astype(jnp.bfloat16)
            high_ref[kind] = high
            low_ref[kind] = (full - high.astype(jnp.float32)).astype(jnp.bfloat16)

    start = pl.multiple_of(step * block, block)
    head = hist_ref[pl.ds(start, block), :]
    extra = width - block
    limit = ((hist_ref.shape[0] - extra) // 16) * 16
    later = pl.multiple_of(jnp.minimum(start + block, limit), 16)
    rest = jnp.where(step == pl.num_programs(0) - 1, tail_ref[...], hist_ref[pl.ds(later, extra), :])
    kinds = class_ref[...]
    total = jnp.zeros((block, head.shape[1]), jnp.float32)
    for kind in range(high_ref.shape[0]):
        part = jnp.dot(high_ref[kind, :, :block], head, preferred_element_type=jnp.float32)
        part = part + jnp.dot(high_ref[kind, :, block:], rest, preferred_element_type=jnp.float32)
        part = part + jnp.dot(low_ref[kind, :, :block], head, preferred_element_type=jnp.float32)
        part = part + jnp.dot(low_ref[kind, :, block:], rest, preferred_element_type=jnp.float32)
        total = jnp.where(kinds == kind, part, total)
    contracted = total.astype(jnp.bfloat16)
    projected = lax.dot_general(
        contracted, rows_ref[...], (((1,), (1,)), ((), ())), preferred_element_type=jnp.float32
    )
    proj_ref[...] = projected.astype(jnp.bfloat16)
    flags = flag_ref[...]
    centre_ref[...] = jnp.dot(contracted, near_ref[1], preferred_element_type=jnp.float32)
    lower = jnp.dot(contracted, near_ref[0], preferred_element_type=jnp.float32)
    lower_ref[...] = (lower * flags[0:1, :]).astype(jnp.bfloat16)
    upper = jnp.dot(contracted, near_ref[2], preferred_element_type=jnp.float32)
    upper_ref[...] = (upper * flags[1:2, :]).astype(jnp.bfloat16)


def local_terms(history, lag_class, lag_table, row_bases, near_blocks, near_flags, steps):
    class_total, lags = lag_table.shape
    size = history.shape[1]
    rank = row_bases.shape[1]
    columns = jnp.transpose(row_bases)
    block = 256
    width = block + 128
    blocks = steps // block
    tail = history[blocks * block :]
    tail = jnp.pad(tail, ((0, width - block - tail.shape[0]), (0, 0)))
    table = jnp.pad(lag_table, ((0, 0), (0, width - lags)))
    kinds = lag_class.reshape(1, size)
    flags = jnp.broadcast_to(near_flags[0].astype(jnp.float32)[:, None], (2, size))
    whole = lambda shape: pl.BlockSpec(shape, lambda b: (0,) * len(shape))
    rows_of = lambda cols: pl.BlockSpec((block, cols), lambda b: (b, 0))
    return pl.pallas_call(
        local_kernel,
        grid=(blocks,),
        out_shape=(
            jax.ShapeDtypeStruct((steps, rank), jnp.bfloat16),
            jax.ShapeDtypeStruct((steps, size), jnp.float32),
            jax.ShapeDtypeStruct((steps, size), jnp.bfloat16),
            jax.ShapeDtypeStruct((steps, size), jnp.bfloat16),
        ),
        in_specs=[
            whole(history.shape),
            whole(tail.shape),
            whole(table.shape),
            whole(kinds.shape),
            whole(columns.shape),
            whole(near_blocks.shape[1:]),
            whole(flags.shape),
        ],
        out_specs=(rows_of(rank), rows_of(size), rows_of(size), rows_of(size)),
        scratch_shapes=[
            pltpu.VMEM((class_total, block, width), jnp.bfloat16),
            pltpu.VMEM((class_total, block, width), jnp.bfloat16),
        ],
        compiler_params=pltpu.CompilerParams(dimension_semantics=("arbitrary",)),
    )(history, tail, table, kinds, columns, near_blocks[0], flags)


def ring_kernel(z_count, data_ref, out_ref, recv, send, send_sem, recv_sem, pair, far, far_send, far_recv):
    row = lax.axis_index("row")
    col = lax.axis_index("col")
    core = row % 2
    zpos = (row // 2) % z_count
    base = row - zpos * 2
    up_dev = base + ((zpos + 1) % z_count) * 2
    down_dev = base + ((zpos + z_count - 1) % z_count) * 2
    half = data_ref.shape[3] // 2
    mesh_kind = pl.DeviceIdType.MESH

    barrier = pltpu.get_barrier_semaphore()
    for neighbour in (up_dev, down_dev):
        pl.semaphore_signal(barrier, inc=1, device_id=(neighbour, col), device_id_type=mesh_kind)
    rows = lax.axis_size("row")
    far_dev = (row + rows // 2) % rows
    pl.semaphore_signal(barrier, inc=1, device_id=(far_dev, col), device_id_type=mesh_kind)
    pl.semaphore_wait(barrier, 3)

    rings = (
        (0, up_dev, lambda s: (zpos + (z_count - 1) * (s + 1)) % z_count, 0),
        (1, down_dev, lambda s: (zpos + s + 1) % z_count, half),
    )
    last = z_count - 1
    copies = {}
    for step in range(last):
        for way, target, index, low in rings:
            if step == 0:
                source = data_ref.at[index(step), :, :, pl.ds(low, half)]
            else:
                copies[(way, step - 1)].wait_recv()
                own = data_ref[index(step), :, :, pl.ds(low, half)].astype(jnp.float32)
                send[way, step] = (recv[way, step - 1].astype(jnp.float32) + own).astype(jnp.bfloat16)
                source = send.at[way, step]
            copy = pltpu.make_async_remote_copy(
                src_ref=source,
                dst_ref=recv.at[way, step],
                send_sem=send_sem.at[way, step],
                recv_sem=recv_sem.at[way, step],
                device_id=(target, col),
                device_id_type=mesh_kind,
            )
            copy.start()
            copies[(way, step)] = copy
    for way, target, index, low in rings:
        copies[(way, last - 1)].wait_recv()
        own = data_ref[zpos, :, :, pl.ds(low, half)].astype(jnp.float32)
        pair[:, :, pl.ds(low, half)] = recv[way, last - 1].astype(jnp.float32) + own
    high = row // (rows // 2)
    far[0] = pair[1 - high].astype(jnp.bfloat16)
    far_copy = pltpu.make_async_remote_copy(
        src_ref=far.at[0],
        dst_ref=far.at[1],
        send_sem=far_send,
        recv_sem=far_recv,
        device_id=(far_dev, col),
        device_id_type=mesh_kind,
    )
    far_copy.start()
    far_copy.wait_recv()
    out_ref[...] = pair[high] + far[1].astype(jnp.float32)
    for copy in copies.values():
        copy.wait_send()
    far_copy.wait_send()


def z_ring(data, z_count):
    _, pairs, width, steps = data.shape
    half = steps // 2
    return pl.pallas_call(
        functools.partial(ring_kernel, z_count),
        out_shape=jax.ShapeDtypeStruct((width, steps), jnp.float32),
        in_specs=[pl.BlockSpec(memory_space=pltpu.VMEM)],
        out_specs=pl.BlockSpec(memory_space=pltpu.VMEM),
        scratch_shapes=[
            pltpu.VMEM((2, z_count - 1, pairs, width, half), jnp.bfloat16),
            pltpu.VMEM((2, z_count - 1, pairs, width, half), jnp.bfloat16),
            pltpu.SemaphoreType.DMA((2, z_count - 1)),
            pltpu.SemaphoreType.DMA((2, z_count - 1)),
            pltpu.VMEM((pairs, width, steps), jnp.float32),
            pltpu.VMEM((2, width, steps), jnp.bfloat16),
            pltpu.SemaphoreType.DMA,
            pltpu.SemaphoreType.DMA,
        ],
        compiler_params=pltpu.CompilerParams(collective_id=0, has_side_effects=True),
    )(data)


def row_reduce(keep, give, row_count):
    z_count = row_count // 4
    core_pairs = [(s, s ^ 1) for s in range(row_count)]
    got = lax.ppermute(give, "row", core_pairs)
    summed = (keep.astype(jnp.float32) + got.astype(jnp.float32)).astype(jnp.bfloat16)
    return z_ring(summed, z_count)


def local(
    history,
    lag_class,
    lag_table,
    row_bases,
    coupling,
    block_ranks,
    col_bases,
    near_blocks,
    near_flags,
):
    row_count = lax.axis_size("row")
    col_count = lax.axis_size("col")
    cluster_total = row_count * col_count
    row_index = lax.axis_index("row")
    col_index = lax.axis_index("col")
    rank_cap = row_bases.shape[1]
    steps = history.shape[0] - lag_table.shape[1] + 1
    projected, centre, lower_terms, upper_terms = local_terms(
        history, lag_class, lag_table, row_bases, near_blocks, near_flags, steps
    )
    flag_block = jnp.zeros((16, rank_cap), jnp.bfloat16).at[0, 0:2].set(
        near_flags[0].astype(jnp.bfloat16)
    )
    extended = jnp.concatenate([projected, flag_block], axis=0)
    gathered = lax.all_gather(extended, "col", axis=0, tiled=False)
    source_proj = gathered[:, :steps]
    flag_rows = gathered[:, steps, 0:2]

    flat_next = [(s, (s + 1) % cluster_total) for s in range(cluster_total)]
    flat_prev = [(s, (s - 1) % cluster_total) for s in range(cluster_total)]
    from_left = lax.ppermute(upper_terms, ("row", "col"), flat_next)
    from_right = lax.ppermute(lower_terms, ("row", "col"), flat_prev)

    source_local = jnp.arange(col_count, dtype=jnp.int32)[:, None]
    target_row = jnp.arange(row_count, dtype=jnp.int32)[None, :]
    offset = jnp.remainder(
        (target_row - row_index) * col_count + col_index - source_local, cluster_total
    )
    levels = jnp.arange(rank_cap, dtype=jnp.int32)
    live_rank = levels[None, None, :] < block_ranks[:, :, 0][:, :, None]
    live_pairs = (
        (offset != 0)[:, :, None, None] & live_rank[:, :, :, None] & live_rank[:, :, None, :]
    )
    masked = jnp.where(live_pairs, coupling[:, :, 0], jnp.zeros((), jnp.bfloat16))
    flag_near = ((offset == cluster_total - 1) & (flag_rows[:, 0:1] > 0.5)) | (
        (offset == 1) & (flag_rows[:, 1:2] > 0.5)
    )
    masked = jnp.where(flag_near[:, :, None, None], jnp.zeros((), jnp.bfloat16), masked)
    z_count = row_count // 4
    masked = masked.reshape(col_count, 2, z_count, 2, rank_cap, rank_cap)
    core = row_index % 2
    halves = []
    for pick in (core, 1 - core):
        chosen = lax.dynamic_index_in_dim(masked, pick, axis=3, keepdims=False)
        halves.append(
            jnp.einsum(
                "sta,syzab->zybt", source_proj, chosen, preferred_element_type=jnp.float32
            ).astype(jnp.bfloat16)
        )
    coeffs = row_reduce(halves[0], halves[1], row_count).astype(jnp.bfloat16)
    far_part = jnp.einsum("bt,eb->te", coeffs, col_bases, preferred_element_type=jnp.float32)
    return far_part + centre + from_left.astype(jnp.float32) + from_right.astype(jnp.float32)


def solution(mesh):
    return jax.shard_map(
        local,
        mesh=mesh,
        in_specs=(
            P(None, ("row", "col")),
            P(("row", "col")),
            P(),
            P(("row", "col"), None),
            P("row", None, "col", None, None),
            P("row", None, "col"),
            P(("row", "col"), None),
            P(("row", "col"), None, None, None),
            P(("row", "col"), None),
        ),
        out_specs=P(None, ("row", "col")),
        check_vma=False,
    )
```

```python
import functools

import jax
import jax.numpy as jnp
from jax import lax
from jax.experimental import pallas as pl
from jax.experimental.pallas import tpu as pltpu
from jax.sharding import PartitionSpec as P


def local_kernel(
    hist_ref, tail_ref, table_ref, class_ref, rows_ref, near_ref, flag_ref,
    proj_ref, centre_ref, lower_ref, upper_ref, high_ref, low_ref,
):
    block, width = high_ref.shape[1], high_ref.shape[2]
    step = pl.program_id(0)

    @pl.when(step == 0)
    def _():
        table = table_ref[...]
        for kind in range(high_ref.shape[0]):
            row = jnp.broadcast_to(table[kind : kind + 1, :], (block, width))
            full = pltpu.roll(row, 0, 1, stride=1, stride_axis=0)
            high = full.astype(jnp.bfloat16)
            high_ref[kind] = high
            low_ref[kind] = (full - high.astype(jnp.float32)).astype(jnp.bfloat16)

    start = pl.multiple_of(step * block, block)
    head = hist_ref[pl.ds(start, block), :]
    extra = width - block
    limit = ((hist_ref.shape[0] - extra) // 16) * 16
    later = pl.multiple_of(jnp.minimum(start + block, limit), 16)
    rest = jnp.where(step == pl.num_programs(0) - 1, tail_ref[...], hist_ref[pl.ds(later, extra), :])
    kinds = class_ref[...]
    total = jnp.zeros((block, head.shape[1]), jnp.float32)
    for kind in range(high_ref.shape[0]):
        part = jnp.dot(high_ref[kind, :, :block], head, preferred_element_type=jnp.float32)
        part = part + jnp.dot(high_ref[kind, :, block:], rest, preferred_element_type=jnp.float32)
        part = part + jnp.dot(low_ref[kind, :, :block], head, preferred_element_type=jnp.float32)
        part = part + jnp.dot(low_ref[kind, :, block:], rest, preferred_element_type=jnp.float32)
        total = jnp.where(kinds == kind, part, total)
    contracted = total.astype(jnp.bfloat16)
    projected = lax.dot_general(
        contracted, rows_ref[...], (((1,), (1,)), ((), ())), preferred_element_type=jnp.float32
    )
    proj_ref[...] = projected.astype(jnp.bfloat16)
    flags = flag_ref[...]
    centre_ref[...] = jnp.dot(contracted, near_ref[1], preferred_element_type=jnp.float32)
    lower = jnp.dot(contracted, near_ref[0], preferred_element_type=jnp.float32)
    lower_ref[...] = (lower * flags[0:1, :]).astype(jnp.bfloat16)
    upper = jnp.dot(contracted, near_ref[2], preferred_element_type=jnp.float32)
    upper_ref[...] = (upper * flags[1:2, :]).astype(jnp.bfloat16)


def local_terms(history, lag_class, lag_table, row_bases, near_blocks, near_flags, steps):
    class_total, lags = lag_table.shape
    size = history.shape[1]
    rank = row_bases.shape[1]
    columns = jnp.transpose(row_bases)
    block = 256
    width = block + 128
    blocks = steps // block
    tail = history[blocks * block :]
    tail = jnp.pad(tail, ((0, width - block - tail.shape[0]), (0, 0)))
    table = jnp.pad(lag_table, ((0, 0), (0, width - lags)))
    kinds = lag_class.reshape(1, size)
    flags = jnp.broadcast_to(near_flags[0].astype(jnp.float32)[:, None], (2, size))
    whole = lambda shape: pl.BlockSpec(shape, lambda b: (0,) * len(shape))
    rows_of = lambda cols: pl.BlockSpec((block, cols), lambda b: (b, 0))
    return pl.pallas_call(
        local_kernel,
        grid=(blocks,),
        out_shape=(
            jax.ShapeDtypeStruct((steps, rank), jnp.bfloat16),
            jax.ShapeDtypeStruct((steps, size), jnp.float32),
            jax.ShapeDtypeStruct((steps, size), jnp.bfloat16),
            jax.ShapeDtypeStruct((steps, size), jnp.bfloat16),
        ),
        in_specs=[
            whole(history.shape),
            whole(tail.shape),
            whole(table.shape),
            whole(kinds.shape),
            whole(columns.shape),
            whole(near_blocks.shape[1:]),
            whole(flags.shape),
        ],
        out_specs=(rows_of(rank), rows_of(size), rows_of(size), rows_of(size)),
        scratch_shapes=[
            pltpu.VMEM((class_total, block, width), jnp.bfloat16),
            pltpu.VMEM((class_total, block, width), jnp.bfloat16),
        ],
        compiler_params=pltpu.CompilerParams(dimension_semantics=("arbitrary",)),
    )(history, tail, table, kinds, columns, near_blocks[0], flags)


def ring_kernel(z_count, data_ref, out_ref, recv, send, send_sem, recv_sem, pair, far, far_send, far_recv):
    row = lax.axis_index("row")
    col = lax.axis_index("col")
    core = row % 2
    zpos = (row // 2) % z_count
    base = row - zpos * 2
    up_dev = base + ((zpos + 1) % z_count) * 2
    down_dev = base + ((zpos + z_count - 1) % z_count) * 2
    half = data_ref.shape[3] // 2
    mesh_kind = pl.DeviceIdType.MESH

    barrier = pltpu.get_barrier_semaphore()
    for neighbour in (up_dev, down_dev):
        pl.semaphore_signal(barrier, inc=1, device_id=(neighbour, col), device_id_type=mesh_kind)
    rows = lax.axis_size("row")
    far_dev = (row + rows // 2) % rows
    pl.semaphore_signal(barrier, inc=1, device_id=(far_dev, col), device_id_type=mesh_kind)
    pl.semaphore_wait(barrier, 3)

    rings = (
        (0, up_dev, lambda s: (zpos + (z_count - 1) * (s + 1)) % z_count, 0),
        (1, down_dev, lambda s: (zpos + s + 1) % z_count, half),
    )
    last = z_count - 1
    copies = {}
    for step in range(last):
        for way, target, index, low in rings:
            if step == 0:
                source = data_ref.at[index(step), :, :, pl.ds(low, half)]
            else:
                copies[(way, step - 1)].wait_recv()
                own = data_ref[index(step), :, :, pl.ds(low, half)].astype(jnp.float32)
                send[way, step] = (recv[way, step - 1].astype(jnp.float32) + own).astype(jnp.bfloat16)
                source = send.at[way, step]
            copy = pltpu.make_async_remote_copy(
                src_ref=source,
                dst_ref=recv.at[way, step],
                send_sem=send_sem.at[way, step],
                recv_sem=recv_sem.at[way, step],
                device_id=(target, col),
                device_id_type=mesh_kind,
            )
            copy.start()
            copies[(way, step)] = copy
    for way, target, index, low in rings:
        copies[(way, last - 1)].wait_recv()
        own = data_ref[zpos, :, :, pl.ds(low, half)].astype(jnp.float32)
        pair[:, :, pl.ds(low, half)] = recv[way, last - 1].astype(jnp.float32) + own
    high = row // (rows // 2)
    far[0] = pair[1 - high].astype(jnp.bfloat16)
    far_copy = pltpu.make_async_remote_copy(
        src_ref=far.at[0],
        dst_ref=far.at[1],
        send_sem=far_send,
        recv_sem=far_recv,
        device_id=(far_dev, col),
        device_id_type=mesh_kind,
    )
    far_copy.start()
    far_copy.wait_recv()
    out_ref[...] = (pair[high] + far[1].astype(jnp.float32)).astype(out_ref.dtype)
    for copy in copies.values():
        copy.wait_send()
    far_copy.wait_send()


def z_ring(data, z_count):
    _, pairs, width, steps = data.shape
    half = steps // 2
    return pl.pallas_call(
        functools.partial(ring_kernel, z_count),
        out_shape=jax.ShapeDtypeStruct((width, steps), jnp.bfloat16),
        in_specs=[pl.BlockSpec(memory_space=pltpu.VMEM)],
        out_specs=pl.BlockSpec(memory_space=pltpu.VMEM),
        scratch_shapes=[
            pltpu.VMEM((2, z_count - 1, pairs, width, half), jnp.bfloat16),
            pltpu.VMEM((2, z_count - 1, pairs, width, half), jnp.bfloat16),
            pltpu.SemaphoreType.DMA((2, z_count - 1)),
            pltpu.SemaphoreType.DMA((2, z_count - 1)),
            pltpu.VMEM((pairs, width, steps), jnp.float32),
            pltpu.VMEM((2, width, steps), jnp.bfloat16),
            pltpu.SemaphoreType.DMA,
            pltpu.SemaphoreType.DMA,
        ],
        compiler_params=pltpu.CompilerParams(collective_id=0, has_side_effects=True),
    )(data)


def row_reduce(keep, give, row_count):
    z_count = row_count // 4
    core_pairs = [(s, s ^ 1) for s in range(row_count)]
    got = lax.ppermute(give, "row", core_pairs)
    summed = (keep.astype(jnp.float32) + got.astype(jnp.float32)).astype(jnp.bfloat16)
    return z_ring(summed, z_count)


def local(
    history,
    lag_class,
    lag_table,
    row_bases,
    coupling,
    block_ranks,
    col_bases,
    near_blocks,
    near_flags,
):
    row_count = lax.axis_size("row")
    col_count = lax.axis_size("col")
    cluster_total = row_count * col_count
    row_index = lax.axis_index("row")
    col_index = lax.axis_index("col")
    rank_cap = row_bases.shape[1]
    steps = history.shape[0] - lag_table.shape[1] + 1
    projected, centre, lower_terms, upper_terms = local_terms(
        history, lag_class, lag_table, row_bases, near_blocks, near_flags, steps
    )
    flag_block = jnp.zeros((16, rank_cap), jnp.bfloat16).at[0, 0:2].set(
        near_flags[0].astype(jnp.bfloat16)
    )
    extended = jnp.concatenate([projected, flag_block], axis=0)
    gathered = lax.all_gather(extended, "col", axis=0, tiled=False)
    source_proj = gathered[:, :steps]
    flag_rows = gathered[:, steps, 0:2]

    flat_next = [(s, (s + 1) % cluster_total) for s in range(cluster_total)]
    flat_prev = [(s, (s - 1) % cluster_total) for s in range(cluster_total)]
    from_left = lax.ppermute(upper_terms, ("row", "col"), flat_next)
    from_right = lax.ppermute(lower_terms, ("row", "col"), flat_prev)

    source_local = jnp.arange(col_count, dtype=jnp.int32)[:, None]
    target_row = jnp.arange(row_count, dtype=jnp.int32)[None, :]
    offset = jnp.remainder(
        (target_row - row_index) * col_count + col_index - source_local, cluster_total
    )
    levels = jnp.arange(rank_cap, dtype=jnp.int32)
    live_rank = levels[None, None, :] < block_ranks[:, :, 0][:, :, None]
    live_pairs = (
        (offset != 0)[:, :, None, None] & live_rank[:, :, :, None] & live_rank[:, :, None, :]
    )
    masked = jnp.where(live_pairs, coupling[:, :, 0], jnp.zeros((), jnp.bfloat16))
    for way, lane in ((1, 1), (-1, 0)):
        source = jnp.remainder(col_index - way, col_count)
        target = jnp.remainder(row_index + (way - col_index + source) // col_count, row_count)
        corner = (source, target, 0, 0)
        piece = lax.dynamic_slice(masked, corner, (1, 1, rank_cap, rank_cap))
        far = lax.dynamic_index_in_dim(flag_rows, source, axis=0, keepdims=False)[lane] < 0.5
        piece = jnp.where(far, piece, jnp.zeros((), jnp.bfloat16))
        masked = lax.dynamic_update_slice(masked, piece, corner)
    z_count = row_count // 4
    masked = masked.reshape(col_count, 2, z_count, 2, rank_cap, rank_cap)
    core = row_index % 2
    halves = []
    for pick in (core, 1 - core):
        chosen = lax.dynamic_index_in_dim(masked, pick, axis=3, keepdims=False)
        halves.append(
            jnp.einsum(
                "sta,syzab->zybt", source_proj, chosen, preferred_element_type=jnp.float32
            ).astype(jnp.bfloat16)
        )
    coeffs = row_reduce(halves[0], halves[1], row_count).astype(jnp.bfloat16)
    far_part = jnp.einsum("bt,eb->te", coeffs, col_bases, preferred_element_type=jnp.float32)
    return far_part + centre + from_left.astype(jnp.float32) + from_right.astype(jnp.float32)


def solution(mesh):
    return jax.shard_map(
        local,
        mesh=mesh,
        in_specs=(
            P(None, ("row", "col")),
            P(("row", "col")),
            P(),
            P(("row", "col"), None),
            P("row", None, "col", None, None),
            P("row", None, "col"),
            P(("row", "col"), None),
            P(("row", "col"), None, None, None),
            P(("row", "col"), None),
        ),
        out_specs=P(None, ("row", "col")),
        check_vma=False,
    )
```

```python
import functools

import jax
import jax.numpy as jnp
from jax import lax
from jax.experimental import pallas as pl
from jax.experimental.pallas import tpu as pltpu
from jax.sharding import PartitionSpec as P


def local_kernel(
    hist_ref, tail_ref, table_ref, class_ref, rows_ref, near_ref, flag_ref,
    proj_ref, centre_ref, lower_ref, upper_ref, high_ref, low_ref,
):
    block, width = high_ref.shape[1], high_ref.shape[2]
    step = pl.program_id(0)

    @pl.when(step == 0)
    def _():
        table = table_ref[...]
        for kind in range(high_ref.shape[0]):
            row = jnp.broadcast_to(table[kind : kind + 1, :], (block, width))
            full = pltpu.roll(row, 0, 1, stride=1, stride_axis=0)
            high = full.astype(jnp.bfloat16)
            high_ref[kind] = high
            low_ref[kind] = (full - high.astype(jnp.float32)).astype(jnp.bfloat16)

    start = pl.multiple_of(step * block, block)
    head = hist_ref[pl.ds(start, block), :]
    extra = width - block
    limit = ((hist_ref.shape[0] - extra) // 16) * 16
    later = pl.multiple_of(jnp.minimum(start + block, limit), 16)
    rest = jnp.where(step == pl.num_programs(0) - 1, tail_ref[...], hist_ref[pl.ds(later, extra), :])
    kinds = class_ref[...]
    total = jnp.zeros((block, head.shape[1]), jnp.float32)
    for kind in range(high_ref.shape[0]):
        part = jnp.dot(high_ref[kind, :, :block], head, preferred_element_type=jnp.float32)
        part = part + jnp.dot(high_ref[kind, :, block:], rest, preferred_element_type=jnp.float32)
        part = part + jnp.dot(low_ref[kind, :, :block], head, preferred_element_type=jnp.float32)
        part = part + jnp.dot(low_ref[kind, :, block:], rest, preferred_element_type=jnp.float32)
        total = jnp.where(kinds == kind, part, total)
    contracted = total.astype(jnp.bfloat16)
    projected = lax.dot_general(
        contracted, rows_ref[...], (((1,), (1,)), ((), ())), preferred_element_type=jnp.float32
    )
    proj_ref[...] = projected.astype(jnp.bfloat16)
    flags = flag_ref[...]
    centre_ref[...] = jnp.dot(contracted, near_ref[1], preferred_element_type=jnp.float32)
    lower = jnp.dot(contracted, near_ref[0], preferred_element_type=jnp.float32)
    lower_ref[...] = (lower * flags[:, 0:1]).astype(jnp.bfloat16)
    upper = jnp.dot(contracted, near_ref[2], preferred_element_type=jnp.float32)
    upper_ref[...] = (upper * flags[:, 1:2]).astype(jnp.bfloat16)


def local_terms(history, lag_class, lag_table, row_bases, near_blocks, near_flags, steps):
    class_total, lags = lag_table.shape
    size = history.shape[1]
    rank = row_bases.shape[1]
    columns = jnp.transpose(row_bases)
    block = 256
    width = block + 128
    blocks = steps // block
    cut = blocks * block
    tail = lax.pad(
        history,
        jnp.zeros((), history.dtype),
        ((-cut, width - block - (history.shape[0] - cut), 0), (0, 0, 0)),
    )
    table = jnp.pad(lag_table, ((0, 0), (0, width - lags)))
    kinds = lag_class.reshape(1, size)
    flags = near_flags.astype(jnp.float32)
    whole = lambda shape: pl.BlockSpec(shape, lambda b: (0,) * len(shape))
    rows_of = lambda cols: pl.BlockSpec((block, cols), lambda b: (b, 0))
    return pl.pallas_call(
        local_kernel,
        grid=(blocks,),
        out_shape=(
            jax.ShapeDtypeStruct((steps, rank), jnp.bfloat16),
            jax.ShapeDtypeStruct((steps, size), jnp.float32),
            jax.ShapeDtypeStruct((steps, size), jnp.bfloat16),
            jax.ShapeDtypeStruct((steps, size), jnp.bfloat16),
        ),
        in_specs=[
            whole(history.shape),
            whole(tail.shape),
            whole(table.shape),
            whole(kinds.shape),
            whole(columns.shape),
            whole(near_blocks.shape[1:]),
            whole(flags.shape),
        ],
        out_specs=(rows_of(rank), rows_of(size), rows_of(size), rows_of(size)),
        scratch_shapes=[
            pltpu.VMEM((class_total, block, width), jnp.bfloat16),
            pltpu.VMEM((class_total, block, width), jnp.bfloat16),
        ],
        compiler_params=pltpu.CompilerParams(dimension_semantics=("arbitrary",)),
    )(history, tail, table, kinds, columns, near_blocks[0], flags)


def ring_kernel(z_count, data_ref, out_ref, recv, send, send_sem, recv_sem, pair, far, far_send, far_recv):
    row = lax.axis_index("row")
    col = lax.axis_index("col")
    core = row % 2
    zpos = (row // 2) % z_count
    base = row - zpos * 2
    up_dev = base + ((zpos + 1) % z_count) * 2
    down_dev = base + ((zpos + z_count - 1) % z_count) * 2
    half = data_ref.shape[3] // 2
    mesh_kind = pl.DeviceIdType.MESH

    barrier = pltpu.get_barrier_semaphore()
    for neighbour in (up_dev, down_dev):
        pl.semaphore_signal(barrier, inc=1, device_id=(neighbour, col), device_id_type=mesh_kind)
    rows = lax.axis_size("row")
    far_dev = (row + rows // 2) % rows
    pl.semaphore_signal(barrier, inc=1, device_id=(far_dev, col), device_id_type=mesh_kind)
    pl.semaphore_wait(barrier, 3)

    rings = (
        (0, up_dev, lambda s: (zpos + (z_count - 1) * (s + 1)) % z_count, 0),
        (1, down_dev, lambda s: (zpos + s + 1) % z_count, half),
    )
    last = z_count - 1
    copies = {}
    for step in range(last):
        for way, target, index, low in rings:
            if step == 0:
                source = data_ref.at[index(step), :, :, pl.ds(low, half)]
            else:
                copies[(way, step - 1)].wait_recv()
                own = data_ref[index(step), :, :, pl.ds(low, half)].astype(jnp.float32)
                send[way, step] = (recv[way, step - 1].astype(jnp.float32) + own).astype(jnp.bfloat16)
                source = send.at[way, step]
            copy = pltpu.make_async_remote_copy(
                src_ref=source,
                dst_ref=recv.at[way, step],
                send_sem=send_sem.at[way, step],
                recv_sem=recv_sem.at[way, step],
                device_id=(target, col),
                device_id_type=mesh_kind,
            )
            copy.start()
            copies[(way, step)] = copy
    for way, target, index, low in rings:
        copies[(way, last - 1)].wait_recv()
        own = data_ref[zpos, :, :, pl.ds(low, half)].astype(jnp.float32)
        pair[:, :, pl.ds(low, half)] = recv[way, last - 1].astype(jnp.float32) + own
    high = row // (rows // 2)
    far[0] = pair[1 - high].astype(jnp.bfloat16)
    far_copy = pltpu.make_async_remote_copy(
        src_ref=far.at[0],
        dst_ref=far.at[1],
        send_sem=far_send,
        recv_sem=far_recv,
        device_id=(far_dev, col),
        device_id_type=mesh_kind,
    )
    far_copy.start()
    far_copy.wait_recv()
    out_ref[...] = (pair[high] + far[1].astype(jnp.float32)).astype(out_ref.dtype)
    for copy in copies.values():
        copy.wait_send()
    far_copy.wait_send()


def z_ring(data, z_count):
    _, pairs, width, steps = data.shape
    half = steps // 2
    return pl.pallas_call(
        functools.partial(ring_kernel, z_count),
        out_shape=jax.ShapeDtypeStruct((width, steps), jnp.bfloat16),
        in_specs=[pl.BlockSpec(memory_space=pltpu.VMEM)],
        out_specs=pl.BlockSpec(memory_space=pltpu.VMEM),
        scratch_shapes=[
            pltpu.VMEM((2, z_count - 1, pairs, width, half), jnp.bfloat16),
            pltpu.VMEM((2, z_count - 1, pairs, width, half), jnp.bfloat16),
            pltpu.SemaphoreType.DMA((2, z_count - 1)),
            pltpu.SemaphoreType.DMA((2, z_count - 1)),
            pltpu.VMEM((pairs, width, steps), jnp.float32),
            pltpu.VMEM((2, width, steps), jnp.bfloat16),
            pltpu.SemaphoreType.DMA,
            pltpu.SemaphoreType.DMA,
        ],
        compiler_params=pltpu.CompilerParams(collective_id=0, has_side_effects=True),
    )(data)


def row_reduce(keep, give, row_count):
    z_count = row_count // 4
    core_pairs = [(s, s ^ 1) for s in range(row_count)]
    got = lax.ppermute(give, "row", core_pairs)
    summed = (keep.astype(jnp.float32) + got.astype(jnp.float32)).astype(jnp.bfloat16)
    return z_ring(summed, z_count)


def local(
    history,
    lag_class,
    lag_table,
    row_bases,
    coupling,
    block_ranks,
    col_bases,
    near_blocks,
    near_flags,
):
    row_count = lax.axis_size("row")
    col_count = lax.axis_size("col")
    cluster_total = row_count * col_count
    row_index = lax.axis_index("row")
    col_index = lax.axis_index("col")
    rank_cap = row_bases.shape[1]
    steps = history.shape[0] - lag_table.shape[1] + 1
    projected, centre, lower_terms, upper_terms = local_terms(
        history, lag_class, lag_table, row_bases, near_blocks, near_flags, steps
    )
    flag_block = jnp.zeros((16, rank_cap), jnp.bfloat16).at[0, 0:2].set(
        near_flags[0].astype(jnp.bfloat16)
    )
    extended = jnp.concatenate([projected, flag_block], axis=0)
    gathered = lax.all_gather(extended, "col", axis=0, tiled=False)
    source_proj = gathered[:, :steps]
    flag_rows = gathered[:, steps, 0:2]

    flat_next = [(s, (s + 1) % cluster_total) for s in range(cluster_total)]
    flat_prev = [(s, (s - 1) % cluster_total) for s in range(cluster_total)]
    from_left = lax.ppermute(upper_terms, ("row", "col"), flat_next)
    from_right = lax.ppermute(lower_terms, ("row", "col"), flat_prev)

    source_local = jnp.arange(col_count, dtype=jnp.int32)[:, None]
    target_row = jnp.arange(row_count, dtype=jnp.int32)[None, :]
    offset = jnp.remainder(
        (target_row - row_index) * col_count + col_index - source_local, cluster_total
    )
    levels = jnp.arange(rank_cap, dtype=jnp.int32)
    live_rank = levels[None, None, :] < block_ranks[:, :, 0][:, :, None]
    live_pairs = (
        (offset != 0)[:, :, None, None] & live_rank[:, :, :, None] & live_rank[:, :, None, :]
    )
    masked = jnp.where(live_pairs, coupling[:, :, 0], jnp.zeros((), jnp.bfloat16))
    for way, lane in ((1, 1), (-1, 0)):
        source = jnp.remainder(col_index - way, col_count)
        target = jnp.remainder(row_index + (way - col_index + source) // col_count, row_count)
        corner = (source, target, 0, 0)
        piece = lax.dynamic_slice(masked, corner, (1, 1, rank_cap, rank_cap))
        far = lax.dynamic_index_in_dim(flag_rows, source, axis=0, keepdims=False)[lane] < 0.5
        piece = jnp.where(far, piece, jnp.zeros((), jnp.bfloat16))
        masked = lax.dynamic_update_slice(masked, piece, corner)
    z_count = row_count // 4
    masked = masked.reshape(col_count, 2, z_count, 2, rank_cap, rank_cap)
    core = row_index % 2
    halves = []
    for pick in (core, 1 - core):
        chosen = lax.dynamic_index_in_dim(masked, pick, axis=3, keepdims=False)
        halves.append(
            jnp.einsum(
                "sta,syzab->zybt", source_proj, chosen, preferred_element_type=jnp.float32
            ).astype(jnp.bfloat16)
        )
    coeffs = row_reduce(halves[0], halves[1], row_count).astype(jnp.bfloat16)
    far_part = jnp.einsum("bt,eb->te", coeffs, col_bases, preferred_element_type=jnp.float32)
    return far_part + centre + from_left.astype(jnp.float32) + from_right.astype(jnp.float32)


def solution(mesh):
    return jax.shard_map(
        local,
        mesh=mesh,
        in_specs=(
            P(None, ("row", "col")),
            P(("row", "col")),
            P(),
            P(("row", "col"), None),
            P("row", None, "col", None, None),
            P("row", None, "col"),
            P(("row", "col"), None),
            P(("row", "col"), None, None, None),
            P(("row", "col"), None),
        ),
        out_specs=P(None, ("row", "col")),
        check_vma=False,
    )
```
